32 devices in a mesh: dp: 16 (over z, x, core), tensor: 2 (over y).
Axes of the slice: x: 2, y: 2, z: 4, core: 2. Of those that a mesh axis runs over, the one named last changes fastest.
Arguments:
- tokens: bfloat16 [24576, 768], P('dp'), may hold values from -2.5 to 2.5
- teacher: bfloat16 [24576, 768], P('dp'), may hold values from -2.5 to 2.5
- lengths: int32 [16, 8], P('dp'), may hold values from 1 to 128, 576 in all within a row
- prev_prompt: bfloat16 [16, 12, 512, 512], P('dp', 'tensor'), may hold values from -2.5 to 2.5
- prev_cont: bfloat16 [16, 8, 12, 128, 640], P('dp', None, 'tensor'), may hold values from -2.5 to 2.5
- w_qkv: bfloat16 [768, 3, 768], P(None, None, 'tensor'), may hold values from -0.21875 to 0.21875
- bias_qv: float32 [2, 768], P(None, 'tensor'), may hold values from -0.6 to 0.6
- w_out: bfloat16 [768, 768], P('tensor'), may hold values from -1.25 to 1.25
- w_in: bfloat16 [768, 3072], P(None, 'tensor'), may hold values from -0.21875 to 0.21875
- b_in: float32 [3072], P('tensor'), may hold values from -0.6 to 0.6
- w_back: bfloat16 [3072, 768], P('tensor'), may hold values from -0.109375 to 0.109375
- bias_out: float32 [2, 768], replicated, may hold values from -0.6 to 0.6
- norm_gain: float32 [2, 768], replicated, may hold values from 0.5 to 1.5
- norm_bias: float32 [2, 768], replicated, may hold values from -0.6 to 0.6
Outputs:
- output: bfloat16 [24576, 768], P('dp', 'tensor')
- logits_prompt: bfloat16 [16, 12, 512, 512], P('dp', 'tensor')
- logits_cont: bfloat16 [16, 8, 12, 128, 640], P('dp', None, 'tensor')
- grad_tokens: float32 [24576, 768], P('dp', 'tensor')
- grad_w_qkv: float32 [768, 3, 768], P(None, None, 'tensor')
- grad_bias_qv: float32 [2, 768], P(None, 'tensor')
- grad_w_out: float32 [768, 768], P('tensor')
- grad_w_in: float32 [768, 3072], P(None, 'tensor')
- grad_b_in: float32 [3072], P('tensor')
- grad_w_back: float32 [3072, 768], P('tensor')
- grad_bias_out: float32 [2, 768], replicated
- grad_norm_gain: float32 [2, 768], replicated
- grad_norm_bias: float32 [2, 768], replicated
- loss: float32 [], replicated
The draws below stay inside these ranges and needn't reach their ends.
Inputs may be any that keep to these rules, and one draw needn't show every extreme that they name: The 8 lengths of each group sum to 576, and the largest of them is 128.
All inputs are finite; a program needn't handle non-finite values.
Results may differ from the reference program's by a relative error of at most 0.009.
Values sent between devices are 32-bit elements; how exact they have to be, the bound alone decides.
No kernel may reach another device: no remote copies, remote signals or barrier semaphores. Data moves between devices by JAX's collectives and lax.ppermute only.
A program may use at most 256 MiB of HBM per device.

```python
import math
import jax
import jax.numpy as jnp
import numpy as np
from jax import lax

D = 768
HEADS = 12
HEAD = 64
FF = 3072
PROMPT = 512
CONT = 8
CONT_LEN = 128
TOTAL = 576
KEYS = 640
SLOTS = 1536
GROUPS = 16
TOKENS = 24576


def block_scale(key, shape, pieces, least, largest):
    def one(axis_at, shards_of):
        steps = jax.random.uniform(jax.random.fold_in(jax.random.fold_in(key, 6), axis_at), (shards_of,), jnp.float32, least / len(pieces), largest / len(pieces))
        return jnp.repeat(jnp.exp(steps), shape[axis_at] // shards_of).reshape((-1,) + (1,) * (len(shape) - axis_at - 1))

    factor_of = one(*pieces[0])
    for cut in pieces[1:]:
        factor_of = factor_of * one(*cut)
    return factor_of


def profile(count, total, reach, skew):
    portions = [(1 << 20) // math.isqrt(grade ** skew) + 1 for grade in range(2, count + 1)]
    surplus, counts = total - reach - (count - 1), [1] * (count - 1)
    while surplus > 0:
        free = [i for i in range(count - 1) if counts[i] < reach]
        mass, remaining = sum([portions[i] for i in free]), surplus
        for i in free:
            extra = min(reach - counts[i], max(1, remaining * portions[i] // mass), surplus)
            counts[i] = counts[i] + extra
            surplus = surplus - extra
    return np.array([reach] + counts)


def ragged_sizes(rng, count, total, bound, skew):
    if count == 2:
        one = jax.random.randint(rng, (), max(1, total - bound), min(bound, total - 1) + 1)
        return jnp.stack([one, total - one])
    sizes = jnp.asarray(profile(count, total, bound, skew), jnp.int32)
    couples = (count - 1) // 2
    donor, taker = sizes[1:1 + 2 * couples:2], sizes[2:2 + 2 * couples:2]
    slack = jnp.minimum(donor - 1, bound - taker)
    passed = jax.random.randint(jax.random.fold_in(rng, 1), (couples,), 0, 1 << 20) % (slack + 1)
    sizes = sizes.at[1:1 + 2 * couples:2].set(donor - passed).at[2:2 + 2 * couples:2].set(taker + passed)
    return sizes[jax.random.permutation(jax.random.fold_in(rng, 2), count)]


def scatter_about(own_key, shape, width, limit, pieces=(), kind=jnp.bfloat16):
    level = block_scale(own_key, shape, pieces, -0.22, 0.18) if pieces else 1.0
    drawn = jax.random.normal(own_key, shape, jnp.float32) * width * level
    return jnp.minimum(jnp.maximum(drawn, -limit), limit).astype(kind)


def setup_inputs(seed: int = 0) -> dict:
    key_of = jax.random.split(jax.random.key(seed), 15)
    return {
        "tokens": scatter_about(key_of[0], (TOKENS, D), 1.0, 2.5, ((0, 16),)),
        "teacher": scatter_about(key_of[1], (TOKENS, D), 1.0, 2.5, ((0, 16),)),
        "lengths": jax.vmap(lambda own: ragged_sizes(own, CONT, TOTAL, CONT_LEN, 2))(jax.random.split(key_of[2], GROUPS)).reshape((GROUPS, CONT)).astype(jnp.int32),
        "prev_prompt": scatter_about(key_of[3], (GROUPS, HEADS, PROMPT, PROMPT), 1.0, 2.5, ((0, 16), (1, 2))),
        "prev_cont": scatter_about(key_of[4], (GROUPS, CONT, HEADS, CONT_LEN, KEYS), 1.0, 2.5, ((0, 16), (2, 2))),
        "w_qkv": scatter_about(key_of[5], (D, 3, D), D ** -0.5, 0.21875, ((2, 2),)),
        "bias_qv": scatter_about(key_of[6], (2, D), 0.1, 0.6, ((1, 2),), jnp.float32),
        "w_out": scatter_about(key_of[7], (D, D), (D // 32) ** -0.5, 1.25, ((0, 2),)),
        "w_in": scatter_about(key_of[8], (D, FF), D ** -0.5, 0.21875, ((1, 2),)),
        "b_in": scatter_about(key_of[9], (FF,), 0.1, 0.6, ((0, 2),), jnp.float32),
        "w_back": scatter_about(key_of[10], (FF, D), FF ** -0.5, 0.109375, ((0, 2),)),
        "bias_out": scatter_about(key_of[11], (2, D), 0.1, 0.6, (), jnp.float32),
        "norm_gain": jnp.clip(1.0 + 0.1 * jax.random.normal(key_of[12], (2, D), jnp.float32), 0.5, 1.5),
        "norm_bias": scatter_about(key_of[13], (2, D), 0.1, 0.6, (), jnp.float32),
    }


@jax.custom_vjp
def low(v):
    return lax.optimization_barrier(v.astype(jnp.bfloat16)).astype(jnp.float32)

@jax.custom_vjp
def low_back(v):
    return v

def low_keep(v):
    return (low(v), None)

def low_pass(kept, grad):
    return (grad,)

def back_keep(v):
    return (v, None)

def back_low(kept, grad):
    return (low(grad),)
low.defvjp(low_keep, low_pass)
low_back.defvjp(back_keep, back_low)
HIGH = lax.Precision.HIGHEST
NEG_FILL = -1e+30
EPS_NORM = 1e-12

def layer_norm(resid, gain, shift):
    center = resid - lax.optimization_barrier(jnp.mean(resid, axis=-1, keepdims=True))
    spread = lax.optimization_barrier(jnp.mean(center * center, axis=-1, keepdims=True))
    return center * lax.rsqrt(spread + EPS_NORM) * gain + shift

def group_layer(params, states, prompt_prev, cont_prev, group_lengths):
    w_qkv, bias_qv, w_out, w_in, b_in, w_back, bias_out, norm_gain, norm_bias = params
    projected = jnp.dot(states, w_qkv.reshape(D, 3 * D), precision=HIGH).reshape(SLOTS, 3, D)
    queries = low_back(low(projected[:, 0] + bias_qv[0])).reshape(SLOTS, HEADS, HEAD)
    keys_all = low_back(low(projected[:, 1])).reshape(SLOTS, HEADS, HEAD)
    values_all = low_back(low(projected[:, 2] + bias_qv[1])).reshape(SLOTS, HEADS, HEAD)
    q_prompt = queries[:PROMPT]
    k_prompt = keys_all[:PROMPT]
    v_prompt = values_all[:PROMPT]
    score_prompt = jnp.einsum('qhd,khd->hqk', q_prompt, k_prompt, precision=HIGH) * 0.125 + prompt_prev
    score_prompt = low_back(score_prompt)
    prob_prompt = jax.nn.softmax(score_prompt, axis=-1)
    ctx_prompt = jnp.einsum('hqk,khd->qhd', low(prob_prompt), v_prompt, precision=HIGH)
    q_cont = queries[PROMPT:].reshape(CONT, CONT_LEN, HEADS, HEAD)
    k_cont = jnp.concatenate([jnp.broadcast_to(k_prompt[None], (CONT, PROMPT, HEADS, HEAD)), keys_all[PROMPT:].reshape(CONT, CONT_LEN, HEADS, HEAD)], axis=1)
    v_cont = jnp.concatenate([jnp.broadcast_to(v_prompt[None], (CONT, PROMPT, HEADS, HEAD)), values_all[PROMPT:].reshape(CONT, CONT_LEN, HEADS, HEAD)], axis=1)
    score_cont = jnp.einsum('cqhd,ckhd->chqk', q_cont, k_cont, precision=HIGH) * 0.125 + cont_prev
    score_cont = low_back(score_cont)
    place = jnp.arange(KEYS, dtype=jnp.int32)
    live = (place[None, :] < PROMPT) | (place[None, :] - PROMPT < group_lengths[:, None])
    masked = jnp.where(live[:, None, None, :], score_cont, NEG_FILL)
    prob_cont = jax.nn.softmax(masked, axis=-1)
    ctx_cont = jnp.einsum('chqk,ckhd->cqhd', low(prob_cont), v_cont, precision=HIGH)
    context = jnp.concatenate([ctx_prompt.reshape(PROMPT, D), ctx_cont.reshape(CONT * CONT_LEN, D)], axis=0)
    context = low_back(low(context))
    attn_core = low_back(jnp.dot(context, w_out, precision=HIGH))
    first = layer_norm(states + attn_core + bias_out[0], norm_gain[0], norm_bias[0])
    hidden_pre = low_back(jnp.dot(low(first), w_in, precision=HIGH) + b_in)
    active = jax.nn.gelu(hidden_pre, approximate=False)
    ffn_core = low_back(jnp.dot(low(active), w_back, precision=HIGH))
    result = layer_norm(first + ffn_core + bias_out[1], norm_gain[1], norm_bias[1])
    return (result, score_prompt, score_cont)

def reference(tokens, teacher, lengths, prev_prompt, prev_cont, w_qkv, bias_qv, w_out, w_in, b_in, w_back, bias_out, norm_gain, norm_bias):
    weights = tuple((entry.astype(jnp.float32) for entry in (w_qkv, bias_qv, w_out, w_in, b_in, w_back, bias_out, norm_gain, norm_bias)))
    prompt_prev = prev_prompt.astype(jnp.float32)
    cont_prev = prev_cont.astype(jnp.float32)
    target = teacher.astype(jnp.float32).reshape(GROUPS, SLOTS, D)
    offsets = jnp.arange(CONT_LEN, dtype=jnp.int32)
    cont_valid = (offsets[None, None, :] < lengths[:, :, None]).reshape(GROUPS, CONT * CONT_LEN)
    row_valid = jnp.concatenate([jnp.ones((GROUPS, PROMPT), dtype=bool), cont_valid], axis=1).astype(jnp.float32)
    count = (jnp.sum(lengths) + GROUPS * PROMPT).astype(jnp.float32)

    def whole(params, states):

        def one_group(entries):
            return group_layer(params, entries[0], entries[1], entries[2], entries[3])
        result, logit_prompt, logit_cont = lax.map(jax.checkpoint(one_group), (states.reshape(GROUPS, SLOTS, D), prompt_prev, cont_prev, lengths))
        difference = (result - target) * row_valid[:, :, None]
        return (jnp.sum(difference * difference) / count, (result, logit_prompt, logit_cont))
    loss, pullback, outputs = jax.vjp(whole, weights, tokens.astype(jnp.float32), has_aux=True)
    grad_weights, grad_tokens = pullback(jnp.ones_like(loss))
    result, logit_prompt, logit_cont = outputs
    return (result.reshape(TOKENS, D).astype(jnp.bfloat16), logit_prompt.astype(jnp.bfloat16), logit_cont.astype(jnp.bfloat16), grad_tokens, grad_weights[0], grad_weights[1], grad_weights[2], grad_weights[3], grad_weights[4], grad_weights[5], grad_weights[6], grad_weights[7], grad_weights[8], loss)
```

```python
import functools

import jax
import jax.numpy as jnp
from jax import lax
from jax.experimental import pallas as pl
from jax.experimental.pallas import tpu as pltpu
from jax.sharding import PartitionSpec as P

D = 768
HEAD = 64
PROMPT = 512
CONT = 8
CONT_LEN = 128
TOTAL = 576
KEYS = 640
SLOTS = 1536

NEG_FILL = -1e30
EPS_NORM = 1e-12
F32 = jnp.float32
BF16 = jnp.bfloat16
VMEM_CAP = 60 * 1024 * 1024
ROWS = 256
UNITS = 512


def nn(a, b):
    return lax.dot_general(a, b, (((1,), (0,)), ((), ())), preferred_element_type=F32)


def nt(a, b):
    return lax.dot_general(a, b, (((1,), (1,)), ((), ())), preferred_element_type=F32)


def tn(a, b):
    return lax.dot_general(a, b, (((0,), (0,)), ((), ())), preferred_element_type=F32)


def whole(shape):
    return pl.BlockSpec(shape, lambda *_: (0,) * len(shape))


ANY = pl.BlockSpec(memory_space=pl.ANY)


def params(n):
    return pltpu.CompilerParams(
        dimension_semantics=("arbitrary",) * n, vmem_limit_bytes=VMEM_CAP
    )


def cost(flops, nbytes, trans=0):
    return pl.CostEstimate(flops=int(flops), bytes_accessed=int(nbytes), transcendentals=int(trans))


def run(kernel, operands, in_specs, out_specs, out_shape, grid, name, estimate, scalars=0, scratch=(),
        aliases=None, after=()):
    n, m = len(operands), len(after)

    def body(*refs):
        kernel(*refs[:n], *refs[n + m :])

    return pl.pallas_call(
        body,
        name=name,
        grid_spec=pltpu.PrefetchScalarGridSpec(
            num_scalar_prefetch=scalars,
            grid=grid,
            in_specs=list(in_specs) + [ANY] * m,
            out_specs=out_specs,
            scratch_shapes=scratch,
        ),
        out_shape=out_shape,
        input_output_aliases=aliases or {},
        compiler_params=params(len(grid)),
        cost_estimate=estimate,
    )(*operands, *after)


def qkv_kernel(tok, w, bias, q, k, v):
    x = tok[...]
    q[...] = (nn(x, w[0]) + bias[0:1]).astype(BF16) * jnp.asarray(0.125, BF16)
    k[...] = nn(x, w[1]).astype(BF16)
    v[...] = (nn(x, w[2]) + bias[1:2]).astype(BF16)


def project(tokens, w3, bias_qv):
    width = w3.shape[2]
    rows = 512
    spec = pl.BlockSpec((rows, width), lambda i: (i, 0))
    out = jax.ShapeDtypeStruct((SLOTS, width), BF16)
    return pl.pallas_call(
        qkv_kernel,
        name="qkv_proj",
        grid=(SLOTS // rows,),
        in_specs=[
            pl.BlockSpec((rows, D), lambda i: (i, 0)),
            whole((3, D, width)),
            whole((2, width)),
        ],
        out_specs=[spec] * 3,
        out_shape=[out] * 3,
        compiler_params=params(1),
        cost_estimate=cost(2 * SLOTS * D * 3 * width, 2 * (SLOTS * D + 3 * D * width + 3 * SLOTS * width)),
    )(tokens, w3, bias_qv)


def half(x, h):
    return x[:, h * HEAD : (h + 1) * HEAD]


def prompt_fwd_kernel(q, k, v, prev, logits, probs, ctx):
    q2, k2, v2 = q[...], k[...], v[...]
    parts = []
    for h in range(2):
        s = nt(half(q2, h), half(k2, h)) + prev[h].astype(F32)
        logits[h] = s.astype(BF16)
        e = jnp.exp(s - jnp.max(s, axis=-1, keepdims=True))
        p = (e * (1.0 / jnp.sum(e, axis=-1, keepdims=True))).astype(BF16)
        probs[h] = p
        parts.append(nn(p, half(v2, h)))
    ctx[...] = jnp.concatenate(parts, axis=1).astype(BF16).astype(F32)


def prompt_forward(q, k, v, prev):
    heads = prev.shape[0]
    pairs = heads // 2
    rows = 256
    big = pl.BlockSpec((2, rows, PROMPT), lambda p, r: (p, r, 0))
    return pl.pallas_call(
        prompt_fwd_kernel,
        name="attn_prompt_fwd",
        grid=(pairs, PROMPT // rows),
        in_specs=[
            pl.BlockSpec((rows, 128), lambda p, r: (r, p)),
            pl.BlockSpec((PROMPT, 128), lambda p, r: (0, p)),
            pl.BlockSpec((PROMPT, 128), lambda p, r: (0, p)),
            big,
        ],
        out_specs=[big, big, pl.BlockSpec((rows, 128), lambda p, r: (r, p))],
        out_shape=[
            jax.ShapeDtypeStruct((heads, PROMPT, PROMPT), BF16),
            jax.ShapeDtypeStruct((heads, PROMPT, PROMPT), BF16),
            jax.ShapeDtypeStruct((PROMPT, heads * HEAD), F32),
        ],
        compiler_params=params(2),
        cost_estimate=cost(
            4 * heads * PROMPT * PROMPT * HEAD, 6 * heads * PROMPT * PROMPT, heads * PROMPT * PROMPT
        ),
    )(q, k, v, prev)


def cont_fwd_kernel(c0, lens, q, kp, vp, ko, vo, prev, *refs):
    logits, probs, ctx = refs[-3:]
    c = pl.program_id(1) + c0
    live = lax.broadcasted_iota(jnp.int32, (CONT_LEN, CONT_LEN), 1) < lens[0, c]
    q2, kp2, vp2, ko2, vo2 = q[...], kp[...], vp[...], ko[...], vo[...]
    parts = []
    for h in range(2):
        qh = half(q2, h)
        s1 = nt(qh, half(kp2, h)) + prev[0, h, :, :PROMPT].astype(F32)
        s2 = nt(qh, half(ko2, h)) + prev[0, h, :, PROMPT:].astype(F32)
        logits[0, h, :, :PROMPT] = s1.astype(BF16)
        logits[0, h, :, PROMPT:] = s2.astype(BF16)
        s2 = jnp.where(live, s2, NEG_FILL)
        top = jnp.maximum(
            jnp.max(s1, axis=-1, keepdims=True), jnp.max(s2, axis=-1, keepdims=True)
        )
        e1 = jnp.exp(s1 - top)
        e2 = jnp.exp(s2 - top)
        inv = 1.0 / (jnp.sum(e1, axis=-1, keepdims=True) + jnp.sum(e2, axis=-1, keepdims=True))
        p1 = (e1 * inv).astype(BF16)
        p2 = (e2 * inv).astype(BF16)
        probs[0, h, :, :PROMPT] = p1
        probs[0, h, :, PROMPT:] = p2
        parts.append(nn(p1, half(vp2, h)) + nn(p2, half(vo2, h)))
    ctx[...] = jnp.concatenate(parts, axis=1).astype(BF16).astype(F32)


def cont_forward(c0, n, lens, q, k, v, prev, earlier=(), after=()):
    heads = prev.shape[1]
    pairs = heads // 2
    first = PROMPT // CONT_LEN + c0
    own = pl.BlockSpec((CONT_LEN, 128), lambda p, c, *_: (c + first, p))
    front = pl.BlockSpec((PROMPT, 128), lambda p, c, *_: (0, p))
    big = pl.BlockSpec((1, 2, CONT_LEN, KEYS), lambda p, c, *_: (c + c0, p, 0, 0))
    shape = jax.ShapeDtypeStruct((CONT, heads, CONT_LEN, KEYS), BF16)
    size = n * heads * CONT_LEN * KEYS
    return run(
        functools.partial(cont_fwd_kernel, c0),
        (lens, q, k, v, k, v, prev) + tuple(earlier),
        [own, front, front, own, own, big] + [ANY] * len(earlier),
        [big, big, pl.BlockSpec((CONT_LEN, 128), lambda p, c, *_: (c, p))],
        [shape, shape, jax.ShapeDtypeStruct((n * CONT_LEN, heads * HEAD), F32)],
        (pairs, n),
        "attn_cont_fwd",
        cost(4 * size * HEAD, 6 * size, size),
        scalars=1,
        aliases={7: 0, 8: 1} if earlier else None,
        after=after,
    )


def unpack_in_kernel(place, near, far, wi, wo, b):
    me = place[1]
    for j in range(8):
        src = near if j < 4 else far
        at = (j % 4) * 128
        c = jnp.bitwise_xor(me, j)
        wi[pl.ds(pl.multiple_of(c * 96, 16), 96), :] = src[at : at + 96, :].astype(BF16)
        tail = src[at + 96 : at + 120, :]
        wo[pl.ds(pl.multiple_of(c * 48, 16), 48), :] = jnp.concatenate(
            [tail[:, :D], tail[:, D:]], axis=0
        ).astype(BF16)
    b[...] = near[120:128, :]


def unpack_back_kernel(place, near, far, wb):
    me = place[1]
    for j in range(8):
        src = near if j < 4 else far
        at = (j % 4) * 192
        c = jnp.bitwise_xor(me, j)
        wb[pl.ds(pl.multiple_of(c * 192, 16), 192), :] = src[at : at + 192, :].astype(BF16)


def unpack(kernel, name, place, near, far, shapes, after=()):
    return run(
        kernel,
        (place, near, far),
        [whole(near.shape), whole(far.shape)],
        [whole(x.shape) for x in shapes],
        shapes,
        (1,),
        name,
        cost(0, 2 * 4 * near.size + 2 * 2 * near.size),
        scalars=1,
        after=after,
    )


def hop(x, bit):
    n = lax.axis_size("dp")
    return lax.ppermute(x, "dp", [(i, i ^ (1 << bit)) for i in range(n)])


def grad_back_kernel(flip, place, act, gffn, out):
    z = place[1] % 2
    acc = tn(act[...], gffn[...])
    out[pl.ds(z, 1)] = acc[None, :192]
    out[pl.ds(1 - z, 1)] = acc[None, 192:]


def grad_back(flip, place, act, gffn, after=()):
    return run(
        functools.partial(grad_back_kernel, flip),
        (place, act, gffn),
        [
            pl.BlockSpec(
                (SLOTS, 384),
                lambda i, place: (0, 2 * ((place[1] // 4 + flip) % 2) + (i + (place[1] // 2) % 2) % 2),
            ),
            whole((SLOTS, D)),
        ],
        pl.BlockSpec((2, 192, D), lambda i, place: (i, 0, 0)),
        jax.ShapeDtypeStruct((4, 192, D), F32),
        (2,),
        "grad_w_back",
        cost(2 * SLOTS * 768 * D, 2 * SLOTS * 768 * 2 + 4 * 768 * D),
        scalars=1,
        after=after,
    )


def grad_in_kernel(place, x, ghid, out, xt):
    @pl.when(pl.program_id(0) == 0)
    def _():
        xt[...] = x[...].T

    acc = nn(xt[...], ghid[...])
    for m in range(4):
        out[pl.ds(jnp.bitwise_xor(place[1] % 4, m), 1)] = acc[None, 96 * m : 96 * m + 96]


def grad_in(flip, place, xlow, ghid, after=()):
    units = ghid.shape[1]
    return run(
        grad_in_kernel,
        (place, xlow, ghid),
        [token_half(flip), pl.BlockSpec((SLOTS, UNITS), lambda i, place: (0, i))],
        pl.BlockSpec((4, 96, UNITS), lambda i, place: (0, 0, i)),
        jax.ShapeDtypeStruct((4, 96, units), F32),
        (units // UNITS,),
        "grad_w_in",
        cost(2 * SLOTS * 384 * units, 2 * SLOTS * (384 + units) + 4 * 384 * units),
        scalars=1,
        scratch=[pltpu.VMEM((384, SLOTS), BF16)],
        after=after,
    )


def grad_qk_kernel(place, tok, gq, gk, out):
    me = place[1] % 4
    tok_t = tok[...].T
    aq = nn(tok_t, gq[...])
    ak = nn(tok_t, gk[...])
    for m in range(4):
        j = jnp.bitwise_xor(me, m)
        r = slice(96 * m, 96 * m + 96)
        out[pl.ds(j, 1), :, 0:384] = aq[None, r]
        out[pl.ds(j, 1), :, 384:768] = ak[None, r]


def grad_vo_kernel(flip, place, tok, gv, ctx, gattn, small, out):
    me = place[1] % 4
    left = (place[1] // 4 + flip) % 2 == 0
    av = nn(tok[...].T, gv[...])
    ao = nn(ctx[...].astype(BF16).T, gattn[...])
    ao = jnp.where(left, ao[:192], ao[192:])
    for m in range(4):
        j = jnp.bitwise_xor(me, m)
        out[pl.ds(j, 1), 0:48, 0:384] = av[None, 96 * m : 96 * m + 48]
        out[pl.ds(j, 1), 0:48, 384:768] = av[None, 96 * m + 48 : 96 * m + 96]
        out[pl.ds(j, 1), 48:96, :] = ao[None, 48 * m : 48 * m + 48]
        out[pl.ds(j, 1), 96:104, :] = jnp.where(left, small[m : m + 1], small[m + 4 : m + 5])


def token_half(flip):
    return pl.BlockSpec((SLOTS, 384), lambda i, place: (0, (place[1] // 4 + flip) % 2))


def grad_qk(flip, place, tokens, gq, gk, after=()):
    width = gq.shape[1]
    return run(
        grad_qk_kernel,
        (place, tokens, gq, gk),
        [token_half(flip), whole((SLOTS, width)), whole((SLOTS, width))],
        whole((4, 96, D)),
        jax.ShapeDtypeStruct((4, 96, D), F32),
        (1,),
        "grad_w_qk",
        cost(2 * SLOTS * 384 * 2 * width, 2 * SLOTS * 3 * width),
        scalars=1,
        after=after,
    )


def grad_vo(flip, place, tokens, gv, ctx, gattn, small, after=()):
    width = gv.shape[1]
    return run(
        functools.partial(grad_vo_kernel, flip),
        (place, tokens, gv, ctx, gattn, small),
        [
            token_half(flip),
            whole((SLOTS, width)),
            whole((SLOTS, width)),
            whole((SLOTS, D)),
            whole((8, 8, D)),
        ],
        whole((4, 104, D)),
        jax.ShapeDtypeStruct((4, 104, D), F32),
        (1,),
        "grad_w_vo",
        cost(2 * SLOTS * (384 * width + width * D), 2 * SLOTS * (3 * width + 2 * D)),
        scalars=1,
        after=after,
    )


def order_kernel(place, near, far, out):
    j = pl.program_id(0)

    @pl.when(j < 4)
    def _():
        out[...] = near[0]

    @pl.when(j >= 4)
    def _():
        out[...] = far[0]


def in_order(place, near, far, after=()):
    _, rows, cols = near.shape
    return run(
        order_kernel,
        (place, near, far),
        [
            pl.BlockSpec((1, rows, cols), lambda j, place: (jnp.minimum(j, 3), 0, 0)),
            pl.BlockSpec((1, rows, cols), lambda j, place: (jnp.maximum(j - 4, 0), 0, 0)),
        ],
        pl.BlockSpec((rows, cols), lambda j, place: (jnp.bitwise_xor(place[1], j), 0)),
        jax.ShapeDtypeStruct((8 * rows, cols), F32),
        (8,),
        "in_order",
        cost(0, 8 * 8 * rows * cols),
        scalars=1,
        after=after,
    )


def order_rest_kernel(place, near, far, gw, gv, go, small):
    j = pl.program_id(0)

    def put(src):
        gv[0, 0:48] = src[0, 0:48, :384]
        gv[0, 48:96] = src[0, 0:48, 384:]
        go[...] = src[0, 48:96]
        small[...] = src[0, 96:104]

    pl.when(j < 4)(lambda: put(near))
    pl.when(j >= 4)(lambda: put(far))


def order_tail(place_x, place_z, pair, rest, width):
    ins = lambda rows: [
        pl.BlockSpec((1, rows, D), lambda j, place: (jnp.minimum(j, 3), 0, 0)),
        pl.BlockSpec((1, rows, D), lambda j, place: (jnp.maximum(j - 4, 0), 0, 0)),
    ]
    at = lambda j, place: jnp.bitwise_xor(place[1], j)
    w3 = jax.ShapeDtypeStruct((3, D, width), F32)

    def qk_kernel(place, near, far, gw):
        j = pl.program_id(0)

        def put(src):
            gw[0] = src[0, :, :384]
            gw[1] = src[0, :, 384:]

        pl.when(j < 4)(lambda: put(near))
        pl.when(j >= 4)(lambda: put(far))

    gw = run(
        qk_kernel,
        (place_x,) + tuple(pair),
        ins(96),
        pl.BlockSpec((2, 96, width), lambda j, place: (0, at(j, place), 0)),
        w3,
        (8,),
        "order_qk",
        cost(0, 8 * 8 * 96 * D),
        scalars=1,
    )
    return run(
        order_rest_kernel,
        (place_z,) + tuple(rest) + (gw,),
        ins(104) + [ANY],
        [
            pl.BlockSpec((1, 96, width), lambda j, place: (2, at(j, place), 0)),
            pl.BlockSpec((48, D), lambda j, place: (at(j, place), 0)),
            pl.BlockSpec((8, D), lambda j, place: (at(j, place), 0)),
        ],
        [w3, jax.ShapeDtypeStruct((width, D), F32), jax.ShapeDtypeStruct((64, D), F32)],
        (8,),
        "order_rest",
        cost(0, 8 * 8 * 104 * D),
        scalars=1,
        aliases={3: 0},
    )


def forward_kernel(first_block, count, has_prev, *refs):
    (lens, place, ctx_own, ctx_oth, tok, teach, wo_own, wo_oth, wi_own, wi_oth, wb_own, wb_oth) = refs[:12]
    b_own, b_oth, bias_out, gain, shift = refs[12:17]
    outs = refs[17 + (7 if has_prev else 0) :]
    out, act, gate, gffn, gsec, xlow, rstd, stats = outs
    i = pl.program_id(0)
    blk = i + first_block
    n_own = wi_own.shape[1] // UNITS

    @pl.when(i == 0)
    def _():
        stats[...] = jnp.zeros_like(stats)

    attn = nn(ctx_own[...].astype(BF16), wo_own[...]) + nn(ctx_oth[...].astype(BF16), wo_oth[...])
    fin = tok[...].astype(F32) + attn + bias_out[0:1]
    c1 = fin - jnp.mean(fin, axis=-1, keepdims=True)
    r1 = lax.rsqrt(jnp.mean(c1 * c1, axis=-1, keepdims=True) + EPS_NORM)
    rstd[...] = jnp.broadcast_to(r1, rstd.shape)
    first = c1 * r1 * gain[0:1] + shift[0:1]
    x = first.astype(BF16)
    xlow[...] = x
    ffn = None
    for side in range(2):
        wi, wb, bb = ((wi_own, wb_own, b_own), (wi_oth, wb_oth, b_oth))[side]
        for u in range(n_own):
            cols = slice(u * UNITS, (u + 1) * UNITS)
            h = nn(x, wi[:, cols]) + bb[0:1, cols]
            cdf = 0.5 + 0.5 * lax.erf(h * 0.7071067811865476)
            pdf = jnp.exp(-0.5 * h * h) * 0.3989422804014327
            a = (h * cdf).astype(BF16)
            at = (side * n_own + u) * UNITS
            gate[:, at : at + UNITS] = (cdf + h * pdf).astype(BF16)
            if side == 0:
                act[:, cols] = a
            part = nn(a, wb[cols, :])
            ffn = part if ffn is None else ffn + part
    sec = first + ffn + bias_out[1:2]
    c2 = sec - jnp.mean(sec, axis=-1, keepdims=True)
    r2 = lax.rsqrt(jnp.mean(c2 * c2, axis=-1, keepdims=True) + EPS_NORM)
    xh2 = c2 * r2
    result = xh2 * gain[1:2] + shift[1:2]
    left = place[0] == 0
    hd = D // 2
    out[...] = jnp.where(left, result[:, :hd], result[:, hd:]).astype(BF16)
    row = lax.broadcasted_iota(jnp.int32, (ROWS, 1), 0)
    per = ROWS // CONT_LEN
    cont0 = (blk - PROMPT // ROWS) * per
    valid = jnp.zeros((ROWS, 1), jnp.bool_)
    for m in range(per):
        length = jnp.where(cont0 < 0, CONT_LEN, lens[0, jnp.maximum(cont0 + m, 0)])
        valid = valid | ((row >= m * CONT_LEN) & (row < m * CONT_LEN + length))
    diff = jnp.where(valid, result - teach[...].astype(F32), 0.0)
    g = diff * (2.0 / count)
    gy = g * gain[1:2]
    g2 = r2 * (
        gy
        - jnp.mean(gy, axis=-1, keepdims=True)
        - xh2 * jnp.mean(gy * xh2, axis=-1, keepdims=True)
    )
    stats[0:1] += jnp.sum(diff * diff, axis=0, keepdims=True)
    stats[1:2] += jnp.sum(g2, axis=0, keepdims=True)
    stats[2:3] += jnp.sum(g * xh2, axis=0, keepdims=True)
    stats[3:4] += jnp.sum(g, axis=0, keepdims=True)
    gsec[...] = g2
    gffn[...] = g2.astype(BF16)


def const(a):
    return pl.BlockSpec(a.shape, lambda *_: (0,) * a.ndim, pipeline_mode=pl.Buffered(1))


def rows_forward(first_block, blocks, count, lens, place, ctx_own, ctx_oth, tok, teach, fixed, prev, after=()):
    width = ctx_own.shape[1]
    units = fixed[2].shape[1]
    near = lambda w: pl.BlockSpec((ROWS, w), lambda i, *_: (i, 0))
    far = lambda w: pl.BlockSpec((ROWS, w), lambda i, *_: (i + first_block, 0))
    shapes = [(D // 2, BF16), (units, BF16), (2 * units, BF16), (D, BF16), (D, F32), (D, BF16), (128, F32)]
    operands = [lens, place, ctx_own, ctx_oth, tok, teach] + list(fixed)
    in_specs = [near(width), near(width), far(D), far(D)] + [const(a) for a in fixed]
    aliases = {}
    if prev is not None:
        aliases = {len(operands) + n: n for n in range(7)}
        operands = operands + list(prev)
        in_specs = in_specs + [ANY] * 7
    return run(
        functools.partial(forward_kernel, first_block, count, prev is not None),
        operands,
        in_specs,
        [far(w) for w, _ in shapes] + [whole((8, D))],
        [jax.ShapeDtypeStruct((SLOTS, w), t) for w, t in shapes] + [jax.ShapeDtypeStruct((8, D), F32)],
        (blocks,),
        "rows_forward",
        cost(
            2 * blocks * ROWS * D * (4 * units + 2 * width),
            8 * D * units + blocks * ROWS * 24000,
            blocks * ROWS * 4 * units,
        ),
        scalars=2,
        aliases=aliases,
        after=after,
    )


def backward_kernel(place, gate, gffn, gsec, xlow, rstd, wo, wi_own, wi_oth, wb_own, wb_oth, gain, shift,
                    ghid, gattn, gctx, gfin, stats, gbin):
    i = pl.program_id(0)
    n_own = wi_own.shape[1] // UNITS

    @pl.when(i == 0)
    def _():
        stats[...] = jnp.zeros_like(stats)
        gbin[...] = jnp.zeros_like(gbin)

    gf = gffn[...]
    gfirst = gsec[...]
    for side in range(2):
        wi, wb = ((wi_own, wb_own), (wi_oth, wb_oth))[side]
        for u in range(n_own):
            cols = slice(u * UNITS, (u + 1) * UNITS)
            at = (side * n_own + u) * UNITS
            gh = (nt(gf, wb[cols, :]) * gate[:, at : at + UNITS].astype(F32)).astype(BF16)
            if side == 0:
                ghid[:, cols] = gh
                gbin[0:1, cols] += jnp.sum(gh.astype(F32), axis=0, keepdims=True)
            gfirst = gfirst + nt(gh, wi[:, cols])
    xh1 = (xlow[...].astype(F32) - shift[0:1]) * (1.0 / gain[0:1])
    gy1 = gfirst * gain[0:1]
    g1 = rstd[:, 0:1] * (
        gy1
        - jnp.mean(gy1, axis=-1, keepdims=True)
        - xh1 * jnp.mean(gy1 * xh1, axis=-1, keepdims=True)
    )
    stats[0:1] += jnp.sum(g1, axis=0, keepdims=True)
    stats[1:2] += jnp.sum(gfirst * xh1, axis=0, keepdims=True)
    stats[2:3] += jnp.sum(gfirst, axis=0, keepdims=True)
    hd = D // 2
    gfin[...] = jnp.where(place[0] == 0, g1[:, :hd], g1[:, hd:])
    ga1 = g1.astype(BF16)
    gattn[...] = ga1
    gctx[...] = nt(ga1, wo[...]).astype(BF16)


def rows_backward(place, gate, gffn, gsec, xlow, rstd, fixed, after=()):
    wo, wi_own = fixed[:2]
    width, units = wo.shape[0], wi_own.shape[1]
    row = lambda w: pl.BlockSpec((ROWS, w), lambda i, *_: (i, 0))
    shapes = [(units, BF16), (D, BF16), (width, BF16), (D // 2, F32)]
    return run(
        backward_kernel,
        (place, gate, gffn, gsec, xlow, rstd) + tuple(fixed),
        [row(2 * units), row(D), row(D), row(D), row(128)] + [const(a) for a in fixed],
        [row(w) for w, _ in shapes] + [whole((8, D)), whole((8, units))],
        [jax.ShapeDtypeStruct((SLOTS, w), t) for w, t in shapes]
        + [jax.ShapeDtypeStruct((8, D), F32), jax.ShapeDtypeStruct((8, units), F32)],
        (SLOTS // ROWS,),
        "rows_backward",
        cost(2 * SLOTS * D * (4 * units + width), 8 * D * units + SLOTS * 20000),
        scalars=1,
        after=after,
    )


def cont_bwd_kernel(q, kp, vp, ko, vo, probs, gctx, ctx, gq, gk, gv, gkp, gvp):
    c = pl.program_id(1)

    @pl.when(c == 0)
    def _():
        gkp[...] = jnp.zeros_like(gkp)
        gvp[...] = jnp.zeros_like(gvp)

    q2, kp2, vp2, ko2, vo2, gc2 = q[...], kp[...], vp[...], ko[...], vo[...], gctx[...]
    prod = gc2.astype(F32) * ctx[...]
    dq, dk, dv = [], [], []
    for h in range(2):
        qh, gh = half(q2, h), half(gc2, h)
        inner = jnp.sum(half(prod, h), axis=-1, keepdims=True)
        p1 = probs[0, h, :, :PROMPT]
        p2 = probs[0, h, :, PROMPT:]
        l1 = (p1.astype(F32) * (nt(gh, half(vp2, h)) - inner)).astype(BF16)
        l2 = (p2.astype(F32) * (nt(gh, half(vo2, h)) - inner)).astype(BF16)
        dq.append((nn(l1, half(kp2, h)) + nn(l2, half(ko2, h))) * 0.125)
        rows = slice(h * HEAD, (h + 1) * HEAD)
        gkp[0, rows] += tn(qh, l1)
        gvp[0, rows] += tn(gh, p1)
        dk.append(tn(qh, l2))
        dv.append(tn(gh, p2))
    gq[...] = jnp.concatenate(dq, axis=1).astype(BF16)
    gk[...] = jnp.concatenate(dk, axis=0).T.astype(BF16)
    gv[...] = jnp.concatenate(dv, axis=0).T.astype(BF16)


def cont_backward(q, k, v, probs, gctx, ctx, after=()):
    heads = probs.shape[1]
    pairs = heads // 2
    first = PROMPT // CONT_LEN
    own = pl.BlockSpec((CONT_LEN, 128), lambda p, c: (c + first, p))
    front = pl.BlockSpec((PROMPT, 128), lambda p, c: (0, p))
    big = pl.BlockSpec((1, 2, CONT_LEN, KEYS), lambda p, c: (c, p, 0, 0))
    acc = pl.BlockSpec((1, 128, PROMPT), lambda p, c: (p, 0, 0))
    rows = jax.ShapeDtypeStruct((SLOTS, heads * HEAD), BF16)
    sums = jax.ShapeDtypeStruct((pairs, 128, PROMPT), F32)
    n = CONT * heads * CONT_LEN * KEYS
    return run(
        cont_bwd_kernel,
        (q, k, v, k, v, probs, gctx, ctx),
        [own, front, front, own, own, big, own, own],
        [own, own, own, acc, acc],
        [rows, rows, rows, sums, sums],
        (pairs, CONT),
        "attn_cont_bwd",
        cost(8 * n * HEAD, 2 * n + 8 * SLOTS * heads * HEAD * 2),
        after=after,
    )


def prompt_bwd_kernel(q, k, v, probs, gctx, ctx, gkp, gvp, a, b, c, gq, gk, gv):
    q2, k2, v2, gc2 = q[...], k[...], v[...], gctx[...]
    prod = gc2.astype(F32) * ctx[...]
    dq, dk, dv = [], [], []
    for h in range(2):
        qh, gh = half(q2, h), half(gc2, h)
        inner = jnp.sum(half(prod, h), axis=-1, keepdims=True)
        p = probs[h]
        l = (p.astype(F32) * (nt(gh, half(v2, h)) - inner)).astype(BF16)
        dq.append(nn(l, half(k2, h)) * 0.125)
        rows = slice(h * HEAD, (h + 1) * HEAD)
        dk.append(gkp[0, rows] + tn(qh, l))
        dv.append(gvp[0, rows] + tn(gh, p))
    gq[...] = jnp.concatenate(dq, axis=1).astype(BF16)
    gk[...] = jnp.concatenate(dk, axis=0).T.astype(BF16)
    gv[...] = jnp.concatenate(dv, axis=0).T.astype(BF16)


def prompt_backward(q, k, v, probs, gctx, ctx, gkp, gvp, gq, gk, gv, after=()):
    heads = probs.shape[0]
    pairs = heads // 2
    blk = pl.BlockSpec((PROMPT, 128), lambda p: (0, p))
    acc = pl.BlockSpec((1, 128, PROMPT), lambda p: (p, 0, 0))
    rows = jax.ShapeDtypeStruct((SLOTS, heads * HEAD), BF16)
    n = heads * PROMPT * PROMPT
    return run(
        prompt_bwd_kernel,
        (q, k, v, probs, gctx, ctx, gkp, gvp, gq, gk, gv),
        [blk, blk, blk, pl.BlockSpec((2, PROMPT, PROMPT), lambda p: (p, 0, 0)), blk, blk, acc, acc] + [ANY] * 3,
        [blk] * 3,
        [rows] * 3,
        (pairs,),
        "attn_prompt_bwd",
        cost(8 * n * HEAD, 2 * n + 8 * PROMPT * heads * HEAD * 2),
        aliases={8: 0, 9: 1, 10: 2},
        after=after,
    )


def input_grad_kernel(place, gq, gk, gv, w, base, send, keep):
    a, b, c = gq[...], gk[...], gv[...]
    hd = D // 2
    mine = place[0] == 0
    part = nt(a, w[0]) + nt(b, w[1]) + nt(c, w[2])
    keep[...] = base[...] + jnp.where(mine, part[:, :hd], part[:, hd:])
    send[...] = jnp.where(mine, part[:, hd:], part[:, :hd])


def input_grad(place, gq, gk, gv, w3, base, after=()):
    width = w3.shape[2]
    rows = 256
    row = lambda w: pl.BlockSpec((rows, w), lambda i, *_: (i, 0))
    out = jax.ShapeDtypeStruct((SLOTS, D // 2), F32)
    return run(
        input_grad_kernel,
        (place, gq, gk, gv, w3, base),
        [row(width)] * 3 + [whole((3, D, width)), row(D // 2)],
        [row(D // 2)] * 2,
        [out, out],
        (SLOTS // rows,),
        "input_grad",
        cost(2 * SLOTS * D * 3 * width, 2 * (SLOTS * 3 * width) + 6 * SLOTS * D),
        scalars=1,
        after=after,
    )


def swap(x):
    n = lax.axis_size("tensor")
    return lax.ppermute(x, "tensor", [(i, n - 1 - i) for i in range(n)])


def tie(*values):
    return lax.optimization_barrier(values)


def exchange_rest(total):
    bit = 3
    while (1 << bit) < lax.axis_size("dp"):
        total = total + hop(total, bit)
        bit += 1
    return total


def gather_back(total, first, second):
    two = jnp.concatenate([total, hop(total, second)], axis=0)
    four = jnp.concatenate([two, hop(two, first)], axis=0)
    return four, hop(four, 0)


def local(
    tokens, teacher, lengths, prev_prompt, prev_cont, w_qkv, bias_qv, w_out, w_in, b_in, w_back,
    bias_out, norm_gain, norm_bias,
):
    width = w_qkv.shape[2]
    units = w_in.shape[1]
    w3 = jnp.transpose(w_qkv, (1, 0, 2))
    t = lax.axis_index("tensor").astype(jnp.int32)
    i = lax.axis_index("dp").astype(jnp.int32)
    core, x, z = i % 2, (i // 2) % 2, (i // 4) % 2
    chunk = core * 4 + x * 2 + z
    place = jnp.stack([t, chunk])
    place_z = jnp.stack([t, core * 4 + z * 2 + x])
    count = float(lax.axis_size("dp") * (PROMPT + TOTAL))

    part_o = lax.dynamic_slice_in_dim(w_out, chunk * 48, 48, 0)
    part_i = lax.dynamic_slice_in_dim(w_in, chunk * 96, 96, 0)
    piece_a = jnp.concatenate(
        [
            part_i.astype(F32),
            jnp.concatenate([part_o[:24], part_o[24:]], axis=1).astype(F32),
            jnp.broadcast_to(b_in[None], (8, units)),
        ],
        axis=0,
    )
    piece_b = lax.dynamic_slice_in_dim(w_back, chunk * 192, 192, 0).astype(F32)
    own_a = swap(piece_a)
    own_b = swap(piece_b)
    q, k, v = project(tokens, w3, bias_qv)
    logits_p, probs_p, ctx_p = prompt_forward(q, k, v, prev_prompt[0])
    own_a, ctx_p = tie(own_a, ctx_p)
    oth_p = swap(ctx_p)
    zs_a, xs_a = hop(own_a, 2), hop(own_a, 1)
    logits_c, probs_c, ctx_a = cont_forward(0, 4, lengths, q, k, v, prev_cont[0], after=(own_a,))
    own_b, zs_a, xs_a, ctx_a = tie(own_b, zs_a, xs_a, ctx_a)
    oth_a = swap(ctx_a)
    zs_b, xs_b = hop(own_b, 2), hop(own_b, 1)
    cross_a = hop(zs_a[:64], 1), hop(xs_a[64:], 2)
    logits_c, probs_c, ctx_b = cont_forward(
        4, 4, lengths, q, k, v, prev_cont[0], (logits_c, probs_c), after=(own_b, zs_a, xs_a)
    )
    *cross_a, zs_b, xs_b, oth_p, ctx_b = tie(*cross_a, zs_b, xs_b, oth_p, ctx_b)
    oth_b = swap(ctx_b)
    near_a = jnp.concatenate([own_a, zs_a, xs_a, *cross_a], axis=0)
    far_a = hop(near_a, 0)
    cross_b = hop(zs_b[:96], 1), hop(xs_b[96:], 2)
    wi_oth, wo_oth, b_oth = unpack(
        unpack_in_kernel,
        "unpack_w_in",
        place,
        near_a,
        far_a,
        [
            jax.ShapeDtypeStruct(w_in.shape, BF16),
            jax.ShapeDtypeStruct(w_out.shape, BF16),
            jax.ShapeDtypeStruct((8, units), F32),
        ],
    )
    *cross_b, oth_a = tie(*cross_b, oth_a)
    near_b = jnp.concatenate([own_b, zs_b, xs_b, *cross_b], axis=0)
    far_b = hop(near_b, 0)
    (wb_oth,) = unpack(
        unpack_back_kernel, "unpack_w_back", place, near_b, far_b, [jax.ShapeDtypeStruct(w_back.shape, BF16)]
    )

    fixed = (w_out, wo_oth, w_in, wi_oth, w_back, wb_oth, b_in[None], b_oth, bias_out, norm_gain, norm_bias)
    nb = 512 // ROWS
    kept, stats_f = None, None
    for n, (ctx_own, ctx_oth) in enumerate(((ctx_p, oth_p), (ctx_a, oth_a), (ctx_b, oth_b))):
        *kept, st = rows_forward(n * nb, nb, count, lengths, place, ctx_own, ctx_oth, tokens, teacher, fixed, kept)
        stats_f = st if n == 0 else stats_f + st
    output, act, gate, gffn, gsec, xlow, rstd = kept
    ctx = jnp.concatenate([ctx_p, ctx_a, ctx_b], axis=0)

    b_send = grad_back(1, place, act, gffn)
    b_got = hop(b_send, 0)
    b_keep = grad_back(0, place, act, gffn, after=(b_send,))
    b_got, b_keep = tie(b_got, b_keep)
    b_out, b_base = b_keep[2:] + b_got[2:], b_keep[:2] + b_got[:2]
    b_got = hop(b_out, 1)
    ghid, gattn, gctx, gfin_half, stats_b, gbin = rows_backward(
        place, gate, gffn, gsec, xlow, rstd, (w_out, w_in, wi_oth, w_back, wb_oth, norm_gain, norm_bias),
        after=(b_out, b_base),
    )
    b_got, ghid = tie(b_got, ghid)
    b_out, b_base = b_base[1:] + b_got[1:], b_base[:1] + b_got[:1]
    b_got = hop(b_out, 2)
    i_send = grad_in(1, place, xlow, ghid, after=(b_out, b_base))
    i_got = hop(i_send, 0)
    stats = jnp.concatenate([stats_f[:4], stats_b[:4]], axis=0)
    swapped_stats = swap(stats)
    i_keep = grad_in(0, place, xlow, ghid, after=(i_send,))
    i_got, b_got, i_keep = tie(i_got, b_got, i_keep)
    i_out, i_base = i_keep[2:] + i_got[2:], i_keep[:2] + i_got[:2]
    i_got = hop(i_out, 1)
    b_total = b_base + b_got
    b_got = hop(b_total, 3)
    gq, gk, gv, gkp, gvp = cont_backward(q, k, v, probs_c, gctx, ctx, after=(i_out, i_base, b_total))
    i_got, b_got, gq = tie(i_got, b_got, gq)
    i_out, i_base = i_base[1:] + i_got[1:], i_base[:1] + i_got[:1]
    i_got = hop(i_out, 2)
    b_total = b_total + b_got
    bit = 4
    while (1 << bit) < lax.axis_size("dp"):
        b_total = b_total + hop(b_total, bit)
        bit += 1
    b_z = hop(b_total, 2)
    gq, gk, gv = prompt_backward(
        q, k, v, probs_p, gctx, ctx, gkp, gvp, gq, gk, gv, after=(i_out, i_base, b_total)
    )
    column = lax.broadcasted_iota(jnp.int32, (1, D), 1) // (D // 2)
    stats = jnp.where(column == t, stats, swapped_stats)
    bias_sums = jnp.concatenate([jnp.sum(gq.astype(F32), axis=0), jnp.sum(gv.astype(F32), axis=0)], axis=0)
    rows = jnp.concatenate(
        [stats[:7], gbin[0].reshape(2, D), bias_sums.reshape(1, D), jnp.zeros((6, D), F32)], axis=0
    )
    small = jnp.concatenate([rows.reshape(8, 2, D), jnp.zeros((8, 6, D), F32)], axis=1)
    qk_send = grad_qk(1, place, tokens, gq, gk)
    qk_got = hop(qk_send, 0)
    vo_send = grad_vo(1, place_z, tokens, gv, ctx, gattn, small, after=(qk_send,))
    vo_got = hop(vo_send, 0)
    qk_keep = grad_qk(0, place, tokens, gq, gk, after=(vo_send,))
    i_got, b_z, qk_got, qk_keep = tie(i_got, b_z, qk_got, qk_keep)
    i_total = i_base + i_got
    i_got = hop(i_total, 3)
    b_two = jnp.concatenate([b_total, b_z], axis=0)
    b_x = hop(b_two, 1)
    qk_out, qk_base = qk_keep[2:] + qk_got[2:], qk_keep[:2] + qk_got[:2]
    qk_got = hop(qk_out, 1)
    vo_keep = grad_vo(0, place_z, tokens, gv, ctx, gattn, small, after=(qk_out,))
    vo_got, vo_keep = tie(vo_got, vo_keep)
    vo_out, vo_base = vo_keep[2:] + vo_got[2:], vo_keep[:2] + vo_got[:2]
    vo_got = hop(vo_out, 2)
    send, keep = input_grad(place, gq, gk, gv, w3, gfin_half, after=(vo_out,))
    i_got, b_x, qk_got, vo_got, send = tie(i_got, b_x, qk_got, vo_got, send)
    swapped = swap(send)
    qk_out, qk_base = qk_base[1:] + qk_got[1:], qk_base[:1] + qk_got[:1]
    qk_got = hop(qk_out, 2)
    vo_out, vo_base = vo_base[1:] + vo_got[1:], vo_base[:1] + vo_got[:1]
    vo_got = hop(vo_out, 1)
    i_total = i_total + i_got
    bit = 4
    while (1 << bit) < lax.axis_size("dp"):
        i_total = i_total + hop(i_total, bit)
        bit += 1
    i_z = hop(i_total, 2)
    b_four = jnp.concatenate([b_two, b_x], axis=0)
    b_sum = b_four, hop(b_four, 0)
    qk_total = exchange_rest(qk_base + qk_got)
    vo_total = exchange_rest(vo_base + vo_got)
    grad_w_back = in_order(place, *b_sum, after=(qk_total, vo_total))
    i_two = jnp.concatenate([i_total, i_z], axis=0)
    i_four = jnp.concatenate([i_two, hop(i_two, 1)], axis=0)
    i_sum = i_four, hop(i_four, 0)
    qk_sum = gather_back(qk_total, 1, 2)
    vo_sum = gather_back(vo_total, 2, 1)
    grad_tokens = keep + swapped
    grad_w_in = in_order(place, *i_sum)
    grad_w3, grad_w_out, tail = order_tail(place, place_z, qk_sum, vo_sum, width)
    rows = tail.reshape(8, 8, D)[:, :2].reshape(16, D)
    loss = jnp.sum(rows[0]) / count
    return (
        output,
        logits_p[None],
        logits_c[None],
        grad_tokens,
        jnp.transpose(grad_w3, (1, 0, 2)),
        rows[9].reshape(2, width),
        grad_w_out,
        grad_w_in,
        rows[7:9].reshape(units),
        grad_w_back,
        jnp.stack([rows[4], rows[1]], axis=0),
        jnp.stack([rows[5], rows[2]], axis=0),
        jnp.stack([rows[6], rows[3]], axis=0),
        loss,
    )


def solution(mesh):
    in_specs = (
        P("dp", None),
        P("dp", None),
        P("dp", None),
        P("dp", "tensor", None, None),
        P("dp", None, "tensor", None, None),
        P(None, None, "tensor"),
        P(None, "tensor"),
        P("tensor", None),
        P(None, "tensor"),
        P("tensor"),
        P("tensor", None),
        P(),
        P(),
        P(),
    )
    out_specs = (
        P("dp", "tensor"),
        P("dp", "tensor", None, None),
        P("dp", None, "tensor", None, None),
        P("dp", "tensor"),
        P(None, None, "tensor"),
        P(None, "tensor"),
        P("tensor", None),
        P(None, "tensor"),
        P("tensor"),
        P("tensor", None),
        P(),
        P(),
        P(),
        P(),
    )
    return jax.shard_map(local, mesh=mesh, in_specs=in_specs, out_specs=out_specs, check_vma=False)
```

```python
import functools

import jax
import jax.numpy as jnp
from jax import lax
from jax.experimental import pallas as pl
from jax.experimental.pallas import tpu as pltpu
from jax.sharding import PartitionSpec as P

D = 768
HEAD = 64
PROMPT = 512
CONT = 8
CONT_LEN = 128
TOTAL = 576
KEYS = 640
SLOTS = 1536

NEG_FILL = -1e30
EPS_NORM = 1e-12
F32 = jnp.float32
BF16 = jnp.bfloat16
VMEM_CAP = 36 * 1024 * 1024
VMEM_WIDE = 60 * 1024 * 1024
ROWS = 256
UNITS = 1536
GROUP = 2
COST_DIV = 1000


def nn(a, b):
    return lax.dot_general(a, b, (((1,), (0,)), ((), ())), preferred_element_type=F32)


def nt(a, b):
    return lax.dot_general(a, b, (((1,), (1,)), ((), ())), preferred_element_type=F32)


def tn(a, b):
    return lax.dot_general(a, b, (((0,), (0,)), ((), ())), preferred_element_type=F32)


def whole(shape):
    return pl.BlockSpec(shape, lambda *_: (0,) * len(shape))


def const(a):
    return pl.BlockSpec(a.shape, lambda *_: (0,) * len(a.shape), pipeline_mode=pl.Buffered(1))


ANY = pl.BlockSpec(memory_space=pl.ANY)


def params(n, cap):
    return pltpu.CompilerParams(dimension_semantics=("arbitrary",) * n, vmem_limit_bytes=cap)


def cost(flops, nbytes, trans=0):
    return pl.CostEstimate(flops=int(flops / COST_DIV), bytes_accessed=int(nbytes / COST_DIV), transcendentals=0)


def run(kernel, operands, in_specs, out_specs, out_shape, grid, name, estimate, scalars=0, scratch=(),
        aliases=None, after=(), cap=VMEM_CAP):
    n, m = len(operands), len(after)

    def body(*refs):
        kernel(*refs[:n], *refs[n + m :])

    return pl.pallas_call(
        body,
        name=name,
        grid_spec=pltpu.PrefetchScalarGridSpec(
            num_scalar_prefetch=scalars,
            grid=grid,
            in_specs=list(in_specs) + [ANY] * m,
            out_specs=out_specs,
            scratch_shapes=scratch,
        ),
        out_shape=out_shape,
        input_output_aliases=aliases or {},
        compiler_params=params(len(grid), cap),
        cost_estimate=estimate,
    )(*operands, *after)


def qkv_kernel(tok, w, bias, q, k, v):
    x = tok[...]
    q[...] = (nn(x, w[0]) + bias[0:1]).astype(BF16) * jnp.asarray(0.125, BF16)
    k[...] = nn(x, w[1]).astype(BF16)
    v[...] = (nn(x, w[2]) + bias[1:2]).astype(BF16)


def project(tokens, w3, bias_qv):
    width = w3.shape[2]
    rows = 512
    spec = pl.BlockSpec((rows, width), lambda i: (i, 0))
    out = jax.ShapeDtypeStruct((SLOTS, width), BF16)
    return pl.pallas_call(
        qkv_kernel,
        name="qkv_proj",
        grid=(SLOTS // rows,),
        in_specs=[
            pl.BlockSpec((rows, D), lambda i: (i, 0)),
            whole((3, D, width)),
            whole((2, width)),
        ],
        out_specs=[spec] * 3,
        out_shape=[out] * 3,
        compiler_params=params(1, VMEM_CAP),
        cost_estimate=cost(2 * SLOTS * D * 3 * width, 2 * (SLOTS * D + 3 * D * width + 3 * SLOTS * width)),
    )(tokens, w3, bias_qv)


def half_mask(rows, h):
    lane = lax.broadcasted_iota(jnp.int32, (rows, 128), 1)
    return lane < HEAD if h == 0 else lane >= HEAD


def only(x, h):
    return jnp.where(half_mask(x.shape[0], h), x, jnp.zeros_like(x))


def pair(h):
    return slice(h // 2 * 128, h // 2 * 128 + 128)


def parts(groups):
    return [slice(g * CONT_LEN, (g + 1) * CONT_LEN) for g in range(groups)]


def own_keys(groups):
    return [slice(PROMPT + g * CONT_LEN, PROMPT + (g + 1) * CONT_LEN) for g in range(groups)]


def fill(kp, vp, kt, vx):
    kt[:, :PROMPT] = kp[...].T
    for p in range(kp.shape[1] // 128):
        vx[p, :PROMPT, :128] = vp[:, p * 128 : (p + 1) * 128]
        vx[p, :, 128:] = jnp.ones_like(vx[p, :, 128:])


def attend(q, kt, vx, soft, ctx, inv, groups):
    heads = q.shape[1] // HEAD

    def score(h):
        qm = only(q[:, pair(h)], h % 2)
        return nn(qm, kt[pair(h), :PROMPT]), [
            nn(qm[r], kt[pair(h), c]) for r, c in zip(parts(groups), own_keys(groups))
        ]

    def mix(h, e):
        out = nn(e[0], vx[h // 2, :PROMPT])
        if groups:
            out = out + jnp.concatenate(
                [nn(x, vx[h // 2, c]) for x, c in zip(e[1], own_keys(groups))], axis=0
            )
        return out

    s, e, outs = [score(0)], [], []
    for h in range(heads):
        if h + 1 < heads:
            s.append(score(h + 1))
        e.append(soft(h, *s[h]))
        if h:
            outs.append(mix(h - 1, e[h - 1]))
    outs.append(mix(heads - 1, e[-1]))
    mine = half_mask(q.shape[0], 0)
    for h in range(0, heads, 2):
        scale = 1.0 / jnp.where(mine, outs[h][:, 128:], outs[h + 1][:, 128:])
        inv[:, pair(h)] = scale
        ctx[:, pair(h)] = (
            (jnp.where(mine, outs[h][:, :128], outs[h + 1][:, :128]) * scale).astype(BF16).astype(F32)
        )


def prompt_fwd_kernel(q, k, v, prev, logits, weights, ctx, inv, kt, vx):
    @pl.when(pl.program_id(0) == 0)
    def _():
        fill(k, v, kt, vx)

    def soft(h, s, _):
        x = s + prev[h].astype(F32)
        logits[h] = x.astype(BF16)
        e = jnp.exp(x - jnp.max(x, axis=-1, keepdims=True)).astype(BF16)
        weights[h] = e
        return e, []

    attend(q[...], kt, vx, soft, ctx, inv, 0)


def prompt_forward(q, k, v, prev, after=()):
    heads = prev.shape[0]
    width = heads * HEAD
    rows = 256
    big = pl.BlockSpec((heads, rows, PROMPT), lambda r: (0, r, 0))
    row = pl.BlockSpec((rows, width), lambda r: (r, 0))
    front = pl.BlockSpec((PROMPT, width), lambda r: (0, 0))
    shape = jax.ShapeDtypeStruct((heads, PROMPT, PROMPT), BF16)
    n = heads * PROMPT * PROMPT
    return run(
        prompt_fwd_kernel,
        (q, k, v, prev),
        [row, front, front, big],
        [big, big, row, row],
        [shape, shape] + [jax.ShapeDtypeStruct((PROMPT, width), F32)] * 2,
        (PROMPT // rows,),
        "attn_prompt_fwd",
        cost(4 * n * HEAD, 6 * n, n),
        scratch=[pltpu.VMEM((width, PROMPT), BF16), pltpu.VMEM((heads // 2, PROMPT, 256), BF16)],
        after=after,
    )


def cont_fwd_kernel(c0, lens, q, kp, vp, ko, vo, prev, *refs):
    logits, weights, ctx, inv, kt, vx = refs[-6:]

    @pl.when(pl.program_id(0) == 0)
    def _():
        fill(kp, vp, kt, vx)

    kt[:, PROMPT:] = ko[...].T
    for p in range(ko.shape[1] // 128):
        vx[p, PROMPT:, :128] = vo[:, p * 128 : (p + 1) * 128]
    column = lax.broadcasted_iota(jnp.int32, (CONT_LEN, CONT_LEN), 1)
    first = c0 + pl.program_id(0) * GROUP
    live = [column < lens[0, first + g] for g in range(GROUP)]

    def soft(h, s1, s2):
        front, own = [], []
        for g, r in enumerate(parts(GROUP)):
            a = s1[r] + prev[g, h, :, :PROMPT].astype(F32)
            b = s2[g] + prev[g, h, :, PROMPT:].astype(F32)
            logits[g, h, :, :PROMPT] = a.astype(BF16)
            logits[g, h, :, PROMPT:] = b.astype(BF16)
            b = jnp.where(live[g], b, NEG_FILL)
            top = jnp.maximum(
                jnp.max(a, axis=-1, keepdims=True), jnp.max(b, axis=-1, keepdims=True)
            )
            front.append(jnp.exp(a - top).astype(BF16))
            own.append(jnp.exp(b - top).astype(BF16))
            weights[g, h, :, :PROMPT] = front[g]
            weights[g, h, :, PROMPT:] = own[g]
        return jnp.concatenate(front, axis=0), own

    attend(q[...], kt, vx, soft, ctx, inv, GROUP)


def cont_forward(c0, n, lens, q, k, v, prev, earlier=(), after=()):
    heads = prev.shape[1]
    width = heads * HEAD
    rows = GROUP * CONT_LEN
    first, at = (PROMPT // CONT_LEN + c0) // GROUP, c0 // GROUP
    own = pl.BlockSpec((rows, width), lambda c, *_: (c + first, 0))
    front = pl.BlockSpec((PROMPT, width), lambda c, *_: (0, 0))
    big = pl.BlockSpec((GROUP, heads, CONT_LEN, KEYS), lambda c, *_: (c + at, 0, 0, 0))
    row = pl.BlockSpec((rows, width), lambda c, *_: (c, 0))
    shape = jax.ShapeDtypeStruct((CONT, heads, CONT_LEN, KEYS), BF16)
    size = n * heads * CONT_LEN * KEYS
    return run(
        functools.partial(cont_fwd_kernel, c0),
        (lens, q, k, v, k, v, prev, *earlier),
        [own, front, front, own, own, big] + [ANY] * len(earlier),
        [big, big, row, row],
        [shape, shape] + [jax.ShapeDtypeStruct((n * CONT_LEN, width), F32)] * 2,
        (n // GROUP,),
        "attn_cont_fwd",
        cost(4 * size * HEAD, 6 * size, size),
        scalars=1,
        scratch=[
            pltpu.VMEM((width, PROMPT + rows), BF16),
            pltpu.VMEM((heads // 2, PROMPT + rows, 256), BF16),
        ],
        aliases={7 + m: m for m in range(len(earlier))},
        after=after,
    )


def hop(x, bit):
    n = lax.axis_size("dp")
    return lax.ppermute(x, "dp", [(i, i ^ (1 << bit)) for i in range(n)])


def turn(x, step):
    n = lax.axis_size("dp")
    return lax.ppermute(x, "dp", [(i, i ^ (4 if (i & 1) ^ step else 2)) for i in range(n)])


def grad_back_kernel(place, act, gffn, send, keep):
    i = pl.program_id(0)
    acc = tn(act[...], gffn[...])

    def put(out, low):
        for m in range(2):
            out[pl.ds(jnp.bitwise_xor(low % 2, m), 1)] = acc[None, 192 * m : 192 * m + 192]

    pl.when(i < 2)(lambda: put(send, place[2]))
    pl.when(i >= 2)(lambda: put(keep, place[1] % 4))


def grad_back(place, act, gffn, after=()):
    units = act.shape[1]
    shape = jax.ShapeDtypeStruct((4, 192, D), F32)
    return run(
        grad_back_kernel,
        (place, act, gffn),
        [
            pl.BlockSpec((SLOTS, 384), lambda i, place: (0, 2 * ((place[1] // 4 + 1 - i // 2) % 2) + i % 2)),
            whole((SLOTS, D)),
        ],
        [
            pl.BlockSpec(
                (2, 192, D), lambda i, place: (jnp.bitwise_xor(jnp.minimum(i, 1), place[2] // 2), 0, 0)
            ),
            pl.BlockSpec(
                (2, 192, D),
                lambda i, place: (jnp.bitwise_xor(jnp.maximum(i - 2, 0), (place[1] // 2) % 2), 0, 0),
            ),
        ],
        [shape] * 2,
        (4,),
        "grad_w_back",
        cost(2 * SLOTS * units * D, 2 * SLOTS * units * 2 + 4 * units * D),
        cap=VMEM_WIDE,
        scalars=1,
        after=after,
    )


IN_BLOCK = 512


def grad_in_kernel(n, place, x, ghid, send, keep, xt):
    i = pl.program_id(0)

    @pl.when(i % n == 0)
    def _():
        xt[...] = x[...].T

    acc = nn(xt[...], ghid[...])

    def put(out, low):
        for m in range(4):
            out[pl.ds(jnp.bitwise_xor(low, m), 1)] = acc[None, 96 * m : 96 * m + 96]

    pl.when(i < n)(lambda: put(send, place[2]))
    pl.when(i >= n)(lambda: put(keep, place[1] % 4))


def grad_in(place, xlow, ghid, after=()):
    units = ghid.shape[1]
    n = units // IN_BLOCK
    shape = jax.ShapeDtypeStruct((4, 96, units), F32)
    return run(
        functools.partial(grad_in_kernel, n),
        (place, xlow, ghid),
        [
            pl.BlockSpec((SLOTS, 384), lambda i, place: (0, (place[1] // 4 + 1 - i // n) % 2)),
            pl.BlockSpec((SLOTS, IN_BLOCK), lambda i, *_: (0, i % n)),
        ],
        [
            pl.BlockSpec((4, 96, IN_BLOCK), lambda i, *_: (0, 0, jnp.minimum(i, n - 1))),
            pl.BlockSpec((4, 96, IN_BLOCK), lambda i, *_: (0, 0, jnp.maximum(i - n, 0))),
        ],
        [shape] * 2,
        (2 * n,),
        "grad_w_in",
        cost(4 * SLOTS * 384 * units, 2 * SLOTS * (768 + 2 * units) + 8 * 384 * units),
        scalars=1,
        scratch=[pltpu.VMEM((384, SLOTS), BF16)],
        after=after,
    )


def grad_rest_kernel(place, tok, gq, gk, gv, ctx_p, ctx_a, ctx_b, gattn, stats, other, *refs):
    send, keep, ao = refs
    i = pl.program_id(0)
    left = (place[1] // 4 + 1 - i) % 2 == 0

    @pl.when(i == 0)
    def _():
        ctx = jnp.concatenate([ctx_p[...], ctx_a[...], ctx_b[...]], axis=0).astype(BF16)
        ao[...] = nn(ctx.T, gattn[...])

    tok_t = tok[...].T
    aq = nn(tok_t, gq[...])
    ak = nn(tok_t, gk[...])
    av = nn(tok_t, gv[...])
    o = jnp.where(left, ao[:192], ao[192:])
    bias = jnp.concatenate(
        [jnp.sum(g[...].astype(F32), axis=0, keepdims=True) for g in (gq, gv)], axis=1
    )
    row = lax.broadcasted_iota(jnp.int32, (16, D), 0)
    half_of = lax.broadcasted_iota(jnp.int32, (16, D), 1) // (D // 2)
    small = jnp.where((half_of == place[0]) | (row >= 7), stats[...], other[...])
    small = jnp.where(row == 9, bias, small)

    def put(out, low):
        for m in range(4):
            j = jnp.bitwise_xor(low, m)
            out[pl.ds(j, 1), 0:96, 0:384] = aq[None, 96 * m : 96 * m + 96]
            out[pl.ds(j, 1), 0:96, 384:768] = ak[None, 96 * m : 96 * m + 96]
            out[pl.ds(j, 1), 96:144, 0:384] = av[None, 96 * m : 96 * m + 48]
            out[pl.ds(j, 1), 96:144, 384:768] = av[None, 96 * m + 48 : 96 * m + 96]
            out[pl.ds(j, 1), 144:192, :] = o[None, 48 * m : 48 * m + 48]
            out[pl.ds(j, 1), 192:200, :] = jnp.concatenate(
                [
                    jnp.where(left, small[2 * m : 2 * m + 2], small[8 + 2 * m : 10 + 2 * m]),
                    jnp.zeros((6, D), F32),
                ],
                axis=0,
            )[None]

    pl.when(i == 0)(lambda: put(send, place[2]))
    pl.when(i == 1)(lambda: put(keep, place[1] % 4))


def grad_rest(place, tokens, gq, gk, gv, ctx_p, ctx_a, ctx_b, gattn, stats, other, after=()):
    width = gq.shape[1]
    shape = jax.ShapeDtypeStruct((4, 200, D), F32)
    fixed = (gq, gk, gv, ctx_p, ctx_a, ctx_b, gattn, stats, other)
    return run(
        grad_rest_kernel,
        (place, tokens) + fixed,
        [pl.BlockSpec((SLOTS, 384), lambda i, place: (0, (place[1] // 4 + 1 - i) % 2))]
        + [const(x) for x in fixed],
        [const(shape)] * 2,
        [shape] * 2,
        (2,),
        "grad_w_rest",
        cost(2 * SLOTS * (D * 3 * width + width * D), 2 * SLOTS * (6 * width + 2 * D)),
        scalars=1,
        scratch=[pltpu.VMEM((width, D), F32)],
        after=after,
    )


def chunk_of(place, far, m):
    if far:
        return (1 - place[1] // 4) * 4 + jnp.bitwise_xor(place[2], m)
    return jnp.bitwise_xor(place[1], m)


def staged(moves):
    for first, _ in moves:
        first.start()
    for first, rest in moves:
        first.wait()
        for c in rest:
            c.start()
    for _, rest in moves:
        for c in rest:
            c.wait()


def order_kernel(rows, far, place, src, *refs):
    out, hold, sems_in, sems_out = refs[-4:]
    moves = []
    for m in range(4):
        at = pl.multiple_of(chunk_of(place, far, m) * rows, 8)
        moves.append(
            (
                pltpu.make_async_copy(src.at[m], hold.at[m], sems_in.at[m]),
                [pltpu.make_async_copy(hold.at[m], out.at[pl.ds(at, rows)], sems_out.at[m])],
            )
        )
    staged(moves)


def in_order(far, place, chunks, prev=None, after=()):
    _, rows, cols = chunks.shape
    return run(
        functools.partial(order_kernel, rows, far),
        (place, chunks) + (() if prev is None else (prev,)),
        [ANY] * (1 if prev is None else 2),
        ANY,
        jax.ShapeDtypeStruct((8 * rows, cols), F32),
        (1,),
        "in_order",
        cost(0, 8 * chunks.size),
        scalars=1,
        scratch=[pltpu.VMEM(chunks.shape, F32), pltpu.SemaphoreType.DMA((4,)), pltpu.SemaphoreType.DMA((4,))],
        aliases={} if prev is None else {2: 0},
        after=after,
    )


def order_rest_kernel(far, width, place, src, *refs):
    gw, go, small, hold, sems_in, sems_out = refs[-6:]
    moves, n = [], 0

    def copy(a, b):
        nonlocal n
        n += 1
        return pltpu.make_async_copy(a, b, sems_out.at[n - 1])

    left, right = pl.ds(0, width), pl.ds(width, width)
    for m in range(4):
        c = chunk_of(place, far, m)
        rows = hold.at[m]
        wide = pl.ds(pl.multiple_of(c * 96, 8), 96)
        out = [
            copy(rows.at[pl.ds(0, 96), left], gw.at[0, wide]),
            copy(rows.at[pl.ds(0, 96), right], gw.at[1, wide]),
            copy(rows.at[pl.ds(96, 48), left], gw.at[2, pl.ds(pl.multiple_of(c * 96, 8), 48)]),
            copy(rows.at[pl.ds(96, 48), right], gw.at[2, pl.ds(pl.multiple_of(c * 96 + 48, 8), 48)]),
            copy(rows.at[pl.ds(144, 48)], go.at[pl.ds(pl.multiple_of(c * 48, 8), 48)]),
            copy(rows.at[pl.ds(192, 8)], small.at[pl.ds(pl.multiple_of(c * 8, 8), 8)]),
        ]
        moves.append((pltpu.make_async_copy(src.at[m], rows, sems_in.at[m]), out))
    staged(moves)


def order_rest(far, place, chunks, width, prev=None, after=()):
    return run(
        functools.partial(order_rest_kernel, far, width),
        (place, chunks) + (() if prev is None else tuple(prev)),
        [ANY] * (1 if prev is None else 4),
        [ANY] * 3,
        [
            jax.ShapeDtypeStruct((3, D, width), F32),
            jax.ShapeDtypeStruct((width, D), F32),
            jax.ShapeDtypeStruct((64, D), F32),
        ],
        (1,),
        "order_rest",
        cost(0, 8 * chunks.size),
        scalars=1,
        scratch=[
            pltpu.VMEM(chunks.shape, F32),
            pltpu.SemaphoreType.DMA((4,)),
            pltpu.SemaphoreType.DMA((24,)),
        ],
        aliases={} if prev is None else {2: 0, 3: 1, 4: 2},
        after=after,
    )


def small_kernel(count, rows, bias, gain, shift, b_in, qv, loss):
    row = lambda n: rows[8 * (n // 2) + n % 2 : 8 * (n // 2) + n % 2 + 1]
    bias[0:1], bias[1:2] = row(4), row(1)
    gain[0:1], gain[1:2] = row(5), row(2)
    shift[0:1], shift[1:2] = row(6), row(3)
    b_in[0:1, :D], b_in[0:1, D:] = row(7), row(8)
    qv[0:1], qv[1:2] = row(9)[:, : D // 2], row(9)[:, D // 2 :]
    loss[...] = jnp.sum(row(0), axis=1, keepdims=True) / count


def small_outputs(count, rows):
    shapes = [(2, D)] * 3 + [(1, 2 * D), (2, D // 2), (1, 1)]
    return run(
        functools.partial(small_kernel, count),
        (rows,),
        [whole(rows.shape)],
        [whole(x) for x in shapes],
        [jax.ShapeDtypeStruct(x, F32) for x in shapes],
        (1,),
        "small_outputs",
        cost(0, 8 * rows.size),
    )


def lay_out(place, pieces, wi, wo, wb, b):
    for far in range(2):
        own_a, rest_a = pieces[2 * far : 2 * far + 2]
        most_b, cross_b = pieces[4 + 2 * far : 6 + 2 * far]
        for m in range(4):
            c = jnp.bitwise_xor(place[3], 4 * far + m)
            src_a = own_a if m == 0 else rest_a.at[pl.ds((m - 1) * 128, 128)]
            src_b = cross_b if m == 3 else most_b.at[pl.ds(m * 192, 192)]
            wi[pl.ds(pl.multiple_of(c * 96, 16), 96), :] = src_a[0:96, :].astype(BF16)
            tail = src_a[96:120, :]
            wo[pl.ds(pl.multiple_of(c * 48, 16), 48), :] = jnp.concatenate(
                [tail[:, :D], tail[:, D:]], axis=0
            ).astype(BF16)
            wb[pl.ds(pl.multiple_of(c * 192, 16), 192), :] = src_b[...].astype(BF16)
    b[...] = pieces[0][120:128, :]


def forward_kernel(first_block, count, has_prev, *refs):
    lens, place = refs[:2]
    if has_prev:
        ctx_own, ctx_oth, tok, teach, wo_own, wi_own, wb_own, b_own, bias_out, gain, shift = refs[2:13]
        wo_oth, wi_oth, wb_oth, b_oth = refs[13:17]
        out, act, gate, gffn, gsec, xlow, rstd, stats = refs[-8:]
        own, oth = ctx_own[...], ctx_oth[...]
    else:
        ctx_p, ctx_a, oth_p, oth_a, tok, teach, wo_own, wi_own, wb_own, b_own, bias_out, gain, shift = refs[2:15]
        pieces = refs[15:23]
        out, act, gate, gffn, gsec, xlow, rstd, stats, wo_oth, wi_oth, wb_oth, b_oth = refs[-12:]
        early = pl.program_id(0) < PROMPT // ROWS
        own = jnp.where(early, ctx_p[...], ctx_a[...])
        oth = jnp.where(early, oth_p[...], oth_a[...])

        @pl.when(pl.program_id(0) == 0)
        def _():
            lay_out(place, pieces, wi_oth, wo_oth, wb_oth, b_oth)

    i = pl.program_id(0)
    blk = i + first_block
    n_own = wi_own.shape[1] // UNITS

    @pl.when(i == 0)
    def _():
        stats[...] = jnp.zeros_like(stats)

    attn = nn(own.astype(BF16), wo_own[...]) + nn(oth.astype(BF16), wo_oth[...])
    fin = tok[...].astype(F32) + attn + bias_out[0:1]
    c1 = fin - jnp.mean(fin, axis=-1, keepdims=True)
    r1 = lax.rsqrt(jnp.mean(c1 * c1, axis=-1, keepdims=True) + EPS_NORM)
    rstd[...] = jnp.broadcast_to(r1, rstd.shape)
    first = c1 * r1 * gain[0:1] + shift[0:1]
    x = first.astype(BF16)
    xlow[...] = x
    ffn = None
    for side in range(2):
        wi, wb, bb = ((wi_own, wb_own, b_own), (wi_oth, wb_oth, b_oth))[side]
        for u in range(n_own):
            cols = slice(u * UNITS, (u + 1) * UNITS)
            h = nn(x, wi[:, cols]) + bb[0:1, cols]
            cdf = 0.5 + 0.5 * lax.erf(h * 0.7071067811865476)
            pdf = jnp.exp(-0.5 * h * h) * 0.3989422804014327
            a = (h * cdf).astype(BF16)
            at = (side * n_own + u) * UNITS
            gate[:, at : at + UNITS] = (cdf + h * pdf).astype(BF16)
            if side == 0:
                act[:, cols] = a
            part = nn(a, wb[cols, :])
            ffn = part if ffn is None else ffn + part
    sec = first + ffn + bias_out[1:2]
    c2 = sec - jnp.mean(sec, axis=-1, keepdims=True)
    r2 = lax.rsqrt(jnp.mean(c2 * c2, axis=-1, keepdims=True) + EPS_NORM)
    xh2 = c2 * r2
    result = xh2 * gain[1:2] + shift[1:2]
    left = place[0] == 0
    hd = D // 2
    out[...] = jnp.where(left, result[:, :hd], result[:, hd:]).astype(BF16)
    row = lax.broadcasted_iota(jnp.int32, (ROWS, 1), 0)
    per = ROWS // CONT_LEN
    cont0 = (blk - PROMPT // ROWS) * per
    valid = jnp.zeros((ROWS, 1), jnp.bool_)
    for m in range(per):
        length = jnp.where(cont0 < 0, CONT_LEN, lens[0, jnp.maximum(cont0 + m, 0)])
        valid = valid | ((row >= m * CONT_LEN) & (row < m * CONT_LEN + length))
    diff = jnp.where(valid, result - teach[...].astype(F32), 0.0)
    g = diff * (2.0 / count)
    gy = g * gain[1:2]
    g2 = r2 * (
        gy
        - jnp.mean(gy, axis=-1, keepdims=True)
        - xh2 * jnp.mean(gy * xh2, axis=-1, keepdims=True)
    )
    stats[0:1] += jnp.sum(diff * diff, axis=0, keepdims=True)
    stats[1:2] += jnp.sum(g2, axis=0, keepdims=True)
    stats[2:3] += jnp.sum(g * xh2, axis=0, keepdims=True)
    stats[3:4] += jnp.sum(g, axis=0, keepdims=True)
    gsec[...] = g2
    gffn[...] = g2.astype(BF16)


def rows_forward(first_block, blocks, count, lens, place, ctxs, tok, teach, fixed, more, prev=None, after=()):
    width = ctxs[0].shape[1]
    units = fixed[1].shape[1]
    row = lambda w: pl.BlockSpec((ROWS, w), lambda i, *_: (i + first_block, 0))
    split = PROMPT // ROWS
    if prev is None:
        low = pl.BlockSpec((ROWS, width), lambda i, *_: (jnp.minimum(i, split - 1), 0))
        high = pl.BlockSpec((ROWS, width), lambda i, *_: (jnp.maximum(i - split, 0), 0))
        ctx_specs = [low, high, low, high]
    else:
        ctx_specs = [pl.BlockSpec((ROWS, width), lambda i, *_: (i, 0))] * 2
    shapes = [(D // 2, BF16), (units, BF16), (2 * units, BF16), (D, BF16), (D, F32), (D, BF16), (128, F32)]
    operands = [lens, place, *ctxs, tok, teach, *fixed, *more]
    specs = ctx_specs + [row(D), row(D)] + [const(a) for a in fixed] + [const(a) for a in more]
    aliases = {}
    out_specs = [row(w) for w, _ in shapes] + [whole((16, D))]
    out_shape = [jax.ShapeDtypeStruct((SLOTS, w), t) for w, t in shapes] + [jax.ShapeDtypeStruct((16, D), F32)]
    if prev is None:
        weights = [
            jax.ShapeDtypeStruct((width, D), BF16),
            jax.ShapeDtypeStruct((D, units), BF16),
            jax.ShapeDtypeStruct((units, D), BF16),
            jax.ShapeDtypeStruct((8, units), F32),
        ]
        out_specs, out_shape = out_specs + [const(w) for w in weights], out_shape + weights
    else:
        aliases = {len(operands) + n: n for n in range(7)}
        operands, specs = operands + list(prev), specs + [ANY] * 7
    return run(
        functools.partial(forward_kernel, first_block, count, prev is not None),
        operands,
        specs,
        out_specs,
        out_shape,
        (blocks,),
        "rows_forward",
        cap=VMEM_WIDE,
        estimate=cost(2 * blocks * ROWS * D * (4 * units + 2 * width), 8 * D * units + blocks * ROWS * 24000),
        scalars=2,
        aliases=aliases,
        after=after,
    )


def backward_kernel(place, gate, gffn, gsec, xlow, rstd, wo, wi_own, wi_oth, wb_own, wb_oth, gain, shift,
                    stats_f, *refs):
    ghid, gattn, gctx, gfin, stats, gbin = refs[-6:]
    i = pl.program_id(0)
    n_own = wi_own.shape[1] // UNITS

    @pl.when(i == 0)
    def _():
        stats[...] = stats_f[...]
        gbin[0:1, :D] = stats_f[7:8]
        gbin[0:1, D:] = stats_f[8:9]

    gf = gffn[...]
    gfirst = gsec[...]
    for side in range(2):
        wi, wb = ((wi_own, wb_own), (wi_oth, wb_oth))[side]
        for u in range(n_own):
            cols = slice(u * UNITS, (u + 1) * UNITS)
            at = (side * n_own + u) * UNITS
            gh = (nt(gf, wb[cols, :]) * gate[:, at : at + UNITS].astype(F32)).astype(BF16)
            if side == 0:
                ghid[:, cols] = gh
                gbin[0:1, cols] += jnp.sum(gh.astype(F32), axis=0, keepdims=True)
            gfirst = gfirst + nt(gh, wi[:, cols])
    xh1 = (xlow[...].astype(F32) - shift[0:1]) * (1.0 / gain[0:1])
    gy1 = gfirst * gain[0:1]
    g1 = rstd[:, 0:1] * (
        gy1
        - jnp.mean(gy1, axis=-1, keepdims=True)
        - xh1 * jnp.mean(gy1 * xh1, axis=-1, keepdims=True)
    )
    stats[4:5] += jnp.sum(g1, axis=0, keepdims=True)
    stats[5:6] += jnp.sum(gfirst * xh1, axis=0, keepdims=True)
    stats[6:7] += jnp.sum(gfirst, axis=0, keepdims=True)

    @pl.when(i == pl.num_programs(0) - 1)
    def _():
        stats[7:8] = gbin[0:1, :D]
        stats[8:9] = gbin[0:1, D:]

    hd = D // 2
    gfin[...] = jnp.where(place[0] == 0, g1[:, :hd], g1[:, hd:])
    ga1 = g1.astype(BF16)
    gattn[...] = ga1
    gctx[...] = nt(ga1, wo[...]).astype(BF16)


def rows_backward(first, blocks, place, gate, gffn, gsec, xlow, rstd, fixed, prev=None, after=()):
    wo, wi_own = fixed[:2]
    width, units = wo.shape[0], wi_own.shape[1]
    row = lambda w: pl.BlockSpec((ROWS, w), lambda i, *_: (i + first, 0))
    shapes = [(units, BF16), (D, BF16), (width, BF16), (D // 2, F32)]
    operands = [place, gate, gffn, gsec, xlow, rstd] + list(fixed)
    specs = [row(2 * units), row(D), row(D), row(D), row(128)] + [const(a) for a in fixed]
    aliases = {}
    if prev is not None:
        aliases = {len(operands) + n: n for n in range(4)}
        operands, specs = operands + list(prev), specs + [ANY] * 4
    return run(
        backward_kernel,
        operands,
        specs,
        [row(w) for w, _ in shapes] + [whole((16, D))],
        [jax.ShapeDtypeStruct((SLOTS, w), t) for w, t in shapes] + [jax.ShapeDtypeStruct((16, D), F32)],
        (blocks,),
        "rows_backward",
        cost(2 * SLOTS * D * (4 * units + width), 8 * D * units + SLOTS * 20000),
        scalars=1,
        scratch=[pltpu.VMEM((8, units), F32)],
        aliases=aliases,
        after=after,
    )


def attend_back(q, gctx, ctx, inv, load, vt, kall, gq, take, groups):
    heads = q.shape[1] // HEAD
    g2, inner, qt, gt = [], [], [], []
    for p in range(heads // 2):
        cols = pair(2 * p)
        g = (gctx[:, cols].astype(F32) * inv[:, cols]).astype(BF16)
        prod = g.astype(F32) * ctx[:, cols]
        g2.append(g)
        qt.append(q[:, cols].T)
        gt.append(g.T)
        inner += [jnp.sum(only(prod, h), axis=-1, keepdims=True) for h in range(2)]

    def weigh(h):
        gm = only(g2[h // 2], h % 2)
        return nn(gm, vt[pair(h), :PROMPT]), [
            nn(gm[r], vt[pair(h), c]) for r, c in zip(parts(groups), own_keys(groups))
        ]

    def finish(h, e, l):
        part = slice(h % 2 * HEAD, (h % 2 + 1) * HEAD)
        q_h, g_h = qt[h // 2][part], gt[h // 2][part]
        dq = nn(l[0], kall[:PROMPT, pair(h)])
        own = []
        if groups:
            dq = dq + jnp.concatenate(
                [nn(x, kall[c, pair(h)]) for x, c in zip(l[1], own_keys(groups))], axis=0
            )
            own = [
                (nn(q_h[:, r], x), nn(g_h[:, r], y))
                for r, x, y in zip(parts(groups), l[1], e[1])
            ]
        return dq, (nn(q_h, l[0]), nn(g_h, e[0])), own

    mine = half_mask(q.shape[0], 0)
    done = []

    def flush(h):
        done.append(finish(h, *held[h]))
        if h % 2:
            a, b = done[h - 1], done[h]
            gq[:, pair(h)] = (jnp.where(mine, a[0], b[0]) * 0.125).astype(BF16)
            both = lambda x, y: tuple(jnp.concatenate(z, axis=0) for z in zip(x, y))
            take(pair(h), both(a[1], b[1]), [both(x, y) for x, y in zip(a[2], b[2])])

    raw, held = [weigh(0)], []
    for h in range(heads):
        if h + 1 < heads:
            raw.append(weigh(h + 1))
        e = load(h)
        l = [(e[0].astype(F32) * (raw[h][0] - inner[h])).astype(BF16)]
        l.append(
            [
                (y.astype(F32) * (x - inner[h][r])).astype(BF16)
                for y, x, r in zip(e[1], raw[h][1], parts(groups))
            ]
        )
        held.append((e, l))
        if h:
            flush(h - 1)
    flush(heads - 1)


def cont_bwd_kernel(split, q, kp, vp, ko, vo, weights, gctx, ctx_a, inv_a, ctx_b, inv_b,
                    gq, gk, gv, gkp, gvp, vt, kall):
    early = pl.program_id(0) < split
    ctx = jnp.where(early, ctx_a[...], ctx_b[...])
    inv = jnp.where(early, inv_a[...], inv_b[...])

    @pl.when(pl.program_id(0) == 0)
    def _():
        gkp[...] = jnp.zeros_like(gkp)
        gvp[...] = jnp.zeros_like(gvp)
        vt[:, :PROMPT] = vp[...].T
        kall[:PROMPT] = kp[...]

    vt[:, PROMPT:] = vo[...].T
    kall[PROMPT:] = ko[...]

    def load(h):
        return (
            jnp.concatenate([weights[g, h, :, :PROMPT] for g in range(GROUP)], axis=0),
            [weights[g, h, :, PROMPT:] for g in range(GROUP)],
        )

    def take(cols, front, own):
        gkp[cols, :] += front[0]
        gvp[cols, :] += front[1]
        for r, (dk, dv) in zip(parts(GROUP), own):
            gk[r, cols] = dk.T.astype(BF16)
            gv[r, cols] = dv.T.astype(BF16)

    attend_back(q[...], gctx[...], ctx, inv, load, vt, kall, gq, take, GROUP)


def cont_backward(q, k, v, weights, gctx, ctx_a, inv_a, ctx_b, inv_b, after=()):
    heads = weights.shape[1]
    width = heads * HEAD
    rows = GROUP * CONT_LEN
    first = PROMPT // rows
    own = pl.BlockSpec((rows, width), lambda c: (c + first, 0))
    front = pl.BlockSpec((PROMPT, width), lambda c: (0, 0))
    big = pl.BlockSpec((GROUP, heads, CONT_LEN, KEYS), lambda c: (c, 0, 0, 0))
    shape = jax.ShapeDtypeStruct((SLOTS, width), BF16)
    sums = jax.ShapeDtypeStruct((width, PROMPT), F32)
    n = CONT * heads * CONT_LEN * KEYS
    split = ctx_a.shape[0] // rows
    head = pl.BlockSpec((rows, width), lambda c: (jnp.minimum(c, split - 1), 0))
    tail = pl.BlockSpec((rows, width), lambda c: (jnp.maximum(c - split, 0), 0))
    return run(
        functools.partial(cont_bwd_kernel, split),
        (q, k, v, k, v, weights, gctx, ctx_a, inv_a, ctx_b, inv_b),
        [own, front, front, own, own, big, own, head, head, tail, tail],
        [own, own, own, whole((width, PROMPT)), whole((width, PROMPT))],
        [shape, shape, shape, sums, sums],
        (CONT // GROUP,),
        "attn_cont_bwd",
        cost(8 * n * HEAD, 2 * n + 8 * SLOTS * heads * HEAD * 2),
        scratch=[pltpu.VMEM((width, PROMPT + rows), BF16), pltpu.VMEM((PROMPT + rows, width), BF16)],
        after=after,
    )


def prompt_bwd_kernel(q, k, v, weights, gctx, ctx, inv, gkp, gvp, a, b, c, gq, gk, gv, vt, ak, av):
    r = pl.program_id(0)

    @pl.when(r == 0)
    def _():
        vt[...] = v[...].T
        ak[...] = gkp[...]
        av[...] = gvp[...]

    def take(cols, front, own):
        ak[cols, :] += front[0]
        av[cols, :] += front[1]

    attend_back(q[...], gctx[...], ctx[...], inv[...], lambda h: (weights[h], []), vt, k, gq, take, 0)

    @pl.when(r == pl.num_programs(0) - 1)
    def _():
        gk[...] = ak[...].T.astype(BF16)
        gv[...] = av[...].T.astype(BF16)


def prompt_backward(q, k, v, weights, gctx, ctx, inv, gkp, gvp, gq, gk, gv, after=()):
    heads = weights.shape[0]
    width = heads * HEAD
    rows = 256
    row = pl.BlockSpec((rows, width), lambda r: (r, 0))
    front = pl.BlockSpec((PROMPT, width), lambda r: (0, 0))
    acc = whole((width, PROMPT))
    shape = jax.ShapeDtypeStruct((SLOTS, width), BF16)
    n = heads * PROMPT * PROMPT
    return run(
        prompt_bwd_kernel,
        (q, k, v, weights, gctx, ctx, inv, gkp, gvp, gq, gk, gv),
        [row, front, front, pl.BlockSpec((heads, rows, PROMPT), lambda r: (0, r, 0)), row, row, row, acc, acc]
        + [ANY] * 3,
        [row, front, front],
        [shape] * 3,
        (PROMPT // rows,),
        "attn_prompt_bwd",
        cost(8 * n * HEAD, 2 * n + 8 * PROMPT * heads * HEAD * 2),
        scratch=[
            pltpu.VMEM((width, PROMPT), BF16),
            pltpu.VMEM((width, PROMPT), F32),
            pltpu.VMEM((width, PROMPT), F32),
        ],
        aliases={9: 0, 10: 1, 11: 2},
        after=after,
    )


def input_grad_kernel(place, gq, gk, gv, w, base, *refs):
    sends, keep = refs[:-1], refs[-1]
    hd = D // 2
    mine = place[0] == 0
    part = nt(gq[...], w[0]) + nt(gk[...], w[1]) + nt(gv[...], w[2])
    keep[...] = base[...] + jnp.where(mine, part[:, :hd], part[:, hd:])
    away = jnp.where(mine, part[:, hd:], part[:, :hd])

    def put(send):
        send[...] = away

    per = SLOTS // part.shape[0] // len(sends)
    for n, send in enumerate(sends):
        pl.when(pl.program_id(0) // per == n)(functools.partial(put, send))


def input_grad(place, gq, gk, gv, w3, base, after=()):
    width = w3.shape[2]
    rows, cuts = 256, 3
    per = SLOTS // rows // cuts
    row = lambda w: pl.BlockSpec((rows, w), lambda i, *_: (i, 0))
    cut = lambda n: pl.BlockSpec((rows, D // 2), lambda i, *_: (jnp.clip(i - n * per, 0, per - 1), 0))
    return run(
        input_grad_kernel,
        (place, gq, gk, gv, w3, base),
        [row(width)] * 3 + [whole((3, D, width)), row(D // 2)],
        [cut(n) for n in range(cuts)] + [row(D // 2)],
        [jax.ShapeDtypeStruct((SLOTS // cuts, D // 2), F32)] * cuts + [jax.ShapeDtypeStruct((SLOTS, D // 2), F32)],
        (SLOTS // rows,),
        "input_grad",
        cost(2 * SLOTS * D * 3 * width, 2 * (SLOTS * 3 * width) + 6 * SLOTS * D),
        scalars=1,
        after=after,
    )


def swap(x):
    n = lax.axis_size("tensor")
    return lax.ppermute(x, "tensor", [(i, n - 1 - i) for i in range(n)])


def tie(*values):
    return lax.optimization_barrier(values)


def far_exchange(total):
    bit = 4
    while (1 << bit) < lax.axis_size("dp"):
        total = total + hop(total, bit)
        bit += 1
    return total


def local(
    tokens, teacher, lengths, prev_prompt, prev_cont, w_qkv, bias_qv, w_out, w_in, b_in, w_back,
    bias_out, norm_gain, norm_bias,
):
    width = w_qkv.shape[2]
    units = w_in.shape[1]
    w3 = jnp.transpose(w_qkv, (1, 0, 2))
    t = lax.axis_index("tensor").astype(jnp.int32)
    i = lax.axis_index("dp").astype(jnp.int32)
    core, x, z = i % 2, (i // 2) % 2, (i // 4) % 2
    x_first, z_first = 2 * x + z, 2 * z + x
    chunk = core * 4 + x_first
    place = jnp.stack(
        [
            t,
            core * 4 + jnp.where(core == 0, x_first, z_first),
            jnp.where(core == 0, z_first, x_first),
            chunk,
        ]
    )
    count = float(lax.axis_size("dp") * (PROMPT + TOTAL))

    part_o = lax.dynamic_slice_in_dim(w_out, chunk * 48, 48, 0)
    part_i = lax.dynamic_slice_in_dim(w_in, chunk * 96, 96, 0)
    piece_a = jnp.concatenate(
        [
            part_i.astype(F32),
            jnp.concatenate([part_o[:24], part_o[24:]], axis=1).astype(F32),
            jnp.broadcast_to(b_in[None], (8, units)),
        ],
        axis=0,
    )
    piece_b = lax.dynamic_slice_in_dim(w_back, chunk * 192, 192, 0).astype(F32)
    own_a = swap(piece_a)
    own_b = swap(piece_b)
    q, k, v = project(tokens, w3, bias_qv)
    logits_p, probs_p, ctx_p, inv_p = prompt_forward(q, k, v, prev_prompt[0])
    own_a, ctx_p = tie(own_a, ctx_p)
    oth_p = swap(ctx_p)
    zs_a, xs_a, far_own_a = hop(own_a, 2), hop(own_a, 1), hop(own_a, 0)
    logits_c, probs_c, ctx_a, inv_a = cont_forward(0, 4, lengths, q, k, v, prev_cont[0], after=(own_a,))
    oth_a = swap(ctx_a)
    logits_c, probs_c, ctx_b, inv_b = cont_forward(
        4, 4, lengths, q, k, v, prev_cont[0], (logits_c, probs_c)
    )
    zs_a, xs_a, far_own_a, own_b, ctx_b = tie(zs_a, xs_a, far_own_a, own_b, ctx_b)
    zs_b, xs_b = hop(own_b, 2), hop(own_b, 1)
    cross_a = turn(jnp.where(core == 0, zs_a, xs_a), 0)
    cross_a, oth_p, zs_b, xs_b = tie(cross_a, oth_p, zs_b, xs_b)
    cross_b = turn(jnp.where(core == 0, zs_b, xs_b), 0)
    rest_a = jnp.concatenate([zs_a, xs_a, cross_a], axis=0)
    most_b = jnp.concatenate([own_b, zs_b, xs_b], axis=0)
    far_rest_a, far_most_b = hop(rest_a, 0), hop(most_b, 0)
    oth_a, cross_b, far_rest_a, far_most_b = tie(oth_a, cross_b, far_rest_a, far_most_b)
    oth_b = swap(ctx_b)
    far_cross_b = hop(cross_b, 0)

    fixed = (w_out, w_in, w_back, b_in[None], bias_out, norm_gain, norm_bias)
    pieces = (
        own_a, rest_a, far_own_a, far_rest_a, most_b, cross_b, far_most_b, far_cross_b,
    )
    n_blocks = SLOTS // ROWS
    lead = (PROMPT + 4 * CONT_LEN) // ROWS
    first = rows_forward(
        0, lead, count, lengths, place, (ctx_p, ctx_a, oth_p, oth_a), tokens, teacher, fixed, pieces
    )
    kept, stats_a, (wo_oth, wi_oth, wb_oth, b_oth) = list(first[:7]), first[7], first[8:]
    oth_b, kept[0] = tie(oth_b, kept[0])
    *kept, stats_f = rows_forward(
        lead, n_blocks - lead, count, lengths, place, (ctx_b, oth_b), tokens, teacher, fixed,
        (wo_oth, wi_oth, wb_oth, b_oth), kept,
    )
    output, act, gate, gffn, gsec, xlow, rstd = kept
    stats_f = stats_f + stats_a

    def split(keep, got, n):
        return keep[n:] + got[n:], keep[:n] + got[:n]

    w_fixed = (w_out, w_in, wi_oth, w_back, wb_oth, norm_gain, norm_bias, stats_f)
    b_send, b_keep = grad_back(place, act, gffn)
    b_got = hop(b_send, 0)
    ghid, gattn, gctx, gfin_half, stats = rows_backward(
        0, n_blocks, place, gate, gffn, gsec, xlow, rstd, w_fixed, after=(b_send,)
    )
    b_got, ghid = tie(b_got, ghid)
    b_out, b_keep = split(b_keep, b_got, 2)
    b_got = turn(b_out, 0)
    other_stats = swap(stats)
    i_send, i_keep = grad_in(place, xlow, ghid, after=(b_out, b_keep))
    b_got, other_stats, i_send = tie(b_got, other_stats, i_send)
    b_out, b_keep = split(b_keep, b_got, 1)
    b_got = turn(b_out, 1)
    i_got = hop(i_send, 0)
    gq, gk, gv, gkp, gvp = cont_backward(
        q, k, v, probs_c, gctx, ctx_a, inv_a, ctx_b, inv_b, after=(b_out, b_keep)
    )
    i_got, b_got, gq = tie(i_got, b_got, gq)
    i_out, i_keep = split(i_keep, i_got, 2)
    i_got = turn(i_out, 0)
    b_total = b_keep + b_got
    b_got = hop(b_total, 3)
    gq, gk, gv = prompt_backward(
        q, k, v, probs_p, gctx, ctx_p, inv_p, gkp, gvp, gq, gk, gv, after=(i_out, i_keep, b_total)
    )
    r_send, r_keep = grad_rest(place, tokens, gq, gk, gv, ctx_p, ctx_a, ctx_b, gattn, stats, other_stats)
    i_got, b_got, r_send = tie(i_got, b_got, r_send)
    r_got = hop(r_send, 0)
    i_out, i_keep = split(i_keep, i_got, 1)
    i_got = turn(i_out, 1)
    r_got, i_got = tie(r_got, i_got)
    r_out, r_keep = split(r_keep, r_got, 2)
    r_got = turn(r_out, 0)
    i_total = i_keep + i_got
    i_got = hop(i_total, 3)
    b_total = far_exchange(b_total + b_got)
    b_got = turn(b_total, 1)
    *sends, keep = input_grad(place, gq, gk, gv, w3, gfin_half, after=(r_out, r_keep, i_total, b_total))
    r_got, i_got, b_got, keep = tie(r_got, i_got, b_got, keep)
    swapped = [swap(sends[0])]
    r_out, r_keep = split(r_keep, r_got, 1)
    r_got = turn(r_out, 1)
    b_two = jnp.concatenate([b_total, b_got], axis=0)
    b_got = turn(b_two, 0)
    r_got, swapped[0] = tie(r_got, swapped[0])
    swapped.append(swap(sends[1]))
    r_total = r_keep + r_got
    r_got = hop(r_total, 3)
    i_total = far_exchange(i_total + i_got)
    i_got = turn(i_total, 1)
    r_got, b_got, i_got, swapped[1] = tie(r_got, b_got, i_got, swapped[1])
    swapped.append(swap(sends[2]))
    r_total = far_exchange(r_total + r_got)
    r_got = turn(r_total, 1)
    i_two = jnp.concatenate([i_total, i_got], axis=0)
    i_got = turn(i_two, 0)
    b_near = jnp.concatenate([b_two, b_got], axis=0)
    b_far = hop(b_near, 0)
    r_got, i_got, b_far, b_near = tie(r_got, i_got, b_far, b_near)
    grad_w_back = in_order(1, place, b_far, in_order(0, place, b_near))
    r_two = jnp.concatenate([r_total, r_got], axis=0)
    r_got = turn(r_two, 0)
    i_near = jnp.concatenate([i_two, i_got], axis=0)
    i_far = hop(i_near, 0)
    grad_w_in = in_order(1, place, i_far, in_order(0, place, i_near, after=(r_two,)))
    grad_w_in, swapped[2] = tie(grad_w_in, swapped[2])
    grad_tokens = keep + jnp.concatenate(swapped, axis=0)
    r_got, grad_tokens, grad_w_back = tie(r_got, grad_tokens, grad_w_back)
    r_near = jnp.concatenate([r_two, r_got], axis=0)
    r_far = hop(r_near, 0)
    rest = order_rest(0, place, r_near, width)
    grad_w3, grad_w_out, rows = order_rest(1, place, r_far, width, rest)
    grad_bias, grad_gain, grad_shift, grad_b_in, grad_qv, loss = small_outputs(count, rows)
    return (
        output,
        logits_p[None],
        logits_c[None],
        grad_tokens,
        jnp.transpose(grad_w3, (1, 0, 2)),
        grad_qv,
        grad_w_out,
        grad_w_in,
        grad_b_in.reshape(units),
        grad_w_back,
        grad_bias,
        grad_gain,
        grad_shift,
        loss.reshape(()),
    )


def solution(mesh):
    in_specs = (
        P("dp", None),
        P("dp", None),
        P("dp", None),
        P("dp", "tensor", None, None),
        P("dp", None, "tensor", None, None),
        P(None, None, "tensor"),
        P(None, "tensor"),
        P("tensor", None),
        P(None, "tensor"),
        P("tensor"),
        P("tensor", None),
        P(),
        P(),
        P(),
    )
    out_specs = (
        P("dp", "tensor"),
        P("dp", "tensor", None, None),
        P("dp", None, "tensor", None, None),
        P("dp", "tensor"),
        P(None, None, "tensor"),
        P(None, "tensor"),
        P("tensor", None),
        P(None, "tensor"),
        P("tensor"),
        P("tensor", None),
        P(),
        P(),
        P(),
        P(),
    )
    return jax.shard_map(local, mesh=mesh, in_specs=in_specs, out_specs=out_specs, check_vma=False)
```

```python
import functools

import jax
import jax.numpy as jnp
from jax import lax
from jax.experimental import pallas as pl
from jax.experimental.pallas import tpu as pltpu
from jax.sharding import PartitionSpec as P

D = 768
HEAD = 64
PROMPT = 512
CONT = 8
CONT_LEN = 128
TOTAL = 576
KEYS = 640
SLOTS = 1536

NEG_FILL = -1e30
EPS_NORM = 1e-12
F32 = jnp.float32
BF16 = jnp.bfloat16
VMEM_CAP = 36 * 1024 * 1024
VMEM_WIDE = 60 * 1024 * 1024
CONT_CAP = 36 * 1024 * 1024
BACK_CAP = 24 * 1024 * 1024
ROWS = 256
UNITS = 1536
GROUP = 2
COST_DIV = 1000


def nn(a, b):
    return lax.dot_general(a, b, (((1,), (0,)), ((), ())), preferred_element_type=F32)


def nt(a, b):
    return lax.dot_general(a, b, (((1,), (1,)), ((), ())), preferred_element_type=F32)


def tn(a, b):
    return lax.dot_general(a, b, (((0,), (0,)), ((), ())), preferred_element_type=F32)


def whole(shape):
    return pl.BlockSpec(shape, lambda *_: (0,) * len(shape))


def const(a):
    return pl.BlockSpec(a.shape, lambda *_: (0,) * len(a.shape), pipeline_mode=pl.Buffered(1))


ANY = pl.BlockSpec(memory_space=pl.ANY)


def params(n, cap):
    return pltpu.CompilerParams(dimension_semantics=("arbitrary",) * n, vmem_limit_bytes=cap)


def cost(flops, nbytes, trans=0):
    return pl.CostEstimate(flops=int(flops / COST_DIV), bytes_accessed=int(nbytes / COST_DIV), transcendentals=0)


def run(kernel, operands, in_specs, out_specs, out_shape, grid, name, estimate, scalars=0, scratch=(),
        aliases=None, after=(), cap=VMEM_CAP):
    n, m = len(operands), len(after)

    def body(*refs):
        kernel(*refs[:n], *refs[n + m :])

    return pl.pallas_call(
        body,
        name=name,
        grid_spec=pltpu.PrefetchScalarGridSpec(
            num_scalar_prefetch=scalars,
            grid=grid,
            in_specs=list(in_specs) + [ANY] * m,
            out_specs=out_specs,
            scratch_shapes=scratch,
        ),
        out_shape=out_shape,
        input_output_aliases=aliases or {},
        compiler_params=params(len(grid), cap),
        cost_estimate=estimate,
    )(*operands, *after)


def qkv_kernel(tok, w, bias, q, k, v):
    x = tok[...]
    q[...] = (nn(x, w[0]) + bias[0:1]).astype(BF16) * jnp.asarray(0.125, BF16)
    k[...] = nn(x, w[1]).astype(BF16)
    v[...] = (nn(x, w[2]) + bias[1:2]).astype(BF16)


def project(tokens, w3, bias_qv):
    width = w3.shape[2]
    rows = 512
    spec = pl.BlockSpec((rows, width), lambda i: (i, 0))
    out = jax.ShapeDtypeStruct((SLOTS, width), BF16)
    return pl.pallas_call(
        qkv_kernel,
        name="qkv_proj",
        grid=(SLOTS // rows,),
        in_specs=[
            pl.BlockSpec((rows, D), lambda i: (i, 0)),
            whole((3, D, width)),
            whole((2, width)),
        ],
        out_specs=[spec] * 3,
        out_shape=[out] * 3,
        compiler_params=params(1, VMEM_CAP),
        cost_estimate=cost(2 * SLOTS * D * 3 * width, 2 * (SLOTS * D + 3 * D * width + 3 * SLOTS * width)),
    )(tokens, w3, bias_qv)


def half_mask(rows, h):
    lane = lax.broadcasted_iota(jnp.int32, (rows, 128), 1)
    return lane < HEAD if h == 0 else lane >= HEAD


def only(x, h):
    return jnp.where(half_mask(x.shape[0], h), x, jnp.zeros_like(x))


def pair(h):
    return slice(h // 2 * 128, h // 2 * 128 + 128)


def parts(groups):
    return [slice(g * CONT_LEN, (g + 1) * CONT_LEN) for g in range(groups)]


def own_keys(groups):
    return [slice(PROMPT + g * CONT_LEN, PROMPT + (g + 1) * CONT_LEN) for g in range(groups)]


def fill(kp, vp, kt, vx):
    kt[:, :PROMPT] = kp[...].T
    for p in range(kp.shape[1] // 128):
        vx[p, :PROMPT, :128] = vp[:, p * 128 : (p + 1) * 128]
        vx[p, :, 128:] = jnp.ones_like(vx[p, :, 128:])


def attend(q, kt, vx, soft, ctx, inv, groups):
    heads = q.shape[1] // HEAD

    def score(h):
        qm = only(q[:, pair(h)], h % 2)
        return nn(qm, kt[pair(h), :PROMPT]), [
            nn(qm[r], kt[pair(h), c]) for r, c in zip(parts(groups), own_keys(groups))
        ]

    def mix(h, e):
        out = nn(e[0], vx[h // 2, :PROMPT])
        if groups:
            out = out + jnp.concatenate(
                [nn(x, vx[h // 2, c]) for x, c in zip(e[1], own_keys(groups))], axis=0
            )
        return out

    s, e, outs = [score(0)], [], []
    for h in range(heads):
        if h + 1 < heads:
            s.append(score(h + 1))
        e.append(soft(h, *s[h]))
        if h:
            outs.append(mix(h - 1, e[h - 1]))
    outs.append(mix(heads - 1, e[-1]))
    mine = half_mask(q.shape[0], 0)
    for h in range(0, heads, 2):
        scale = 1.0 / jnp.where(mine, outs[h][:, 128:], outs[h + 1][:, 128:])
        inv[:, pair(h)] = scale
        ctx[:, pair(h)] = (
            (jnp.where(mine, outs[h][:, :128], outs[h + 1][:, :128]) * scale).astype(BF16).astype(F32)
        )


def prompt_fwd_kernel(q, k, v, prev, logits, weights, ctx, inv, kt, vx):
    @pl.when(pl.program_id(0) == 0)
    def _():
        fill(k, v, kt, vx)

    def soft(h, s, _):
        x = s + prev[h].astype(F32)
        logits[h] = x.astype(BF16)
        e = jnp.exp(x - jnp.max(x, axis=-1, keepdims=True)).astype(BF16)
        weights[h] = e
        return e, []

    attend(q[...], kt, vx, soft, ctx, inv, 0)


def prompt_forward(q, k, v, prev, after=()):
    heads = prev.shape[0]
    width = heads * HEAD
    rows = 256
    big = pl.BlockSpec((heads, rows, PROMPT), lambda r: (0, r, 0))
    row = pl.BlockSpec((rows, width), lambda r: (r, 0))
    front = pl.BlockSpec((PROMPT, width), lambda r: (0, 0))
    shape = jax.ShapeDtypeStruct((heads, PROMPT, PROMPT), BF16)
    n = heads * PROMPT * PROMPT
    return run(
        prompt_fwd_kernel,
        (q, k, v, prev),
        [row, front, front, big],
        [big, big, row, row],
        [shape, shape] + [jax.ShapeDtypeStruct((PROMPT, width), F32)] * 2,
        (PROMPT // rows,),
        "attn_prompt_fwd",
        cost(4 * n * HEAD, 6 * n, n),
        scratch=[pltpu.VMEM((width, PROMPT), BF16), pltpu.VMEM((heads // 2, PROMPT, 256), BF16)],
        after=after,
    )


def cont_fwd_kernel(c0, lens, q, kp, vp, ko, vo, prev, *refs):
    logits, weights, ctx, inv, kt, vx = refs[-6:]

    @pl.when(pl.program_id(0) == 0)
    def _():
        fill(kp, vp, kt, vx)

    kt[:, PROMPT:] = ko[...].T
    for p in range(ko.shape[1] // 128):
        vx[p, PROMPT:, :128] = vo[:, p * 128 : (p + 1) * 128]
    column = lax.broadcasted_iota(jnp.int32, (CONT_LEN, CONT_LEN), 1)
    first = c0 + pl.program_id(0) * GROUP
    live = [column < lens[0, first + g] for g in range(GROUP)]

    def soft(h, s1, s2):
        front, own = [], []
        for g, r in enumerate(parts(GROUP)):
            a = s1[r] + prev[g, h, :, :PROMPT].astype(F32)
            b = s2[g] + prev[g, h, :, PROMPT:].astype(F32)
            logits[g, h, :, :PROMPT] = a.astype(BF16)
            logits[g, h, :, PROMPT:] = b.astype(BF16)
            b = jnp.where(live[g], b, NEG_FILL)
            top = jnp.maximum(
                jnp.max(a, axis=-1, keepdims=True), jnp.max(b, axis=-1, keepdims=True)
            )
            front.append(jnp.exp(a - top).astype(BF16))
            own.append(jnp.exp(b - top).astype(BF16))
            weights[g, h, :, :PROMPT] = front[g]
            weights[g, h, :, PROMPT:] = own[g]
        return jnp.concatenate(front, axis=0), own

    attend(q[...], kt, vx, soft, ctx, inv, GROUP)


def cont_forward(c0, n, lens, q, k, v, prev, earlier=(), after=()):
    heads = prev.shape[1]
    width = heads * HEAD
    rows = GROUP * CONT_LEN
    first, at = (PROMPT // CONT_LEN + c0) // GROUP, c0 // GROUP
    own = pl.BlockSpec((rows, width), lambda c, *_: (c + first, 0))
    front = pl.BlockSpec((PROMPT, width), lambda c, *_: (0, 0))
    big = pl.BlockSpec((GROUP, heads, CONT_LEN, KEYS), lambda c, *_: (c + at, 0, 0, 0))
    row = pl.BlockSpec((rows, width), lambda c, *_: (c, 0))
    shape = jax.ShapeDtypeStruct((CONT, heads, CONT_LEN, KEYS), BF16)
    size = n * heads * CONT_LEN * KEYS
    return run(
        functools.partial(cont_fwd_kernel, c0),
        (lens, q, k, v, k, v, prev, *earlier),
        [own, front, front, own, own, big] + [ANY] * len(earlier),
        [big, big, row, row],
        [shape, shape] + [jax.ShapeDtypeStruct((n * CONT_LEN, width), F32)] * 2,
        (n // GROUP,),
        "attn_cont_fwd",
        cost(4 * size * HEAD, 6 * size, size),
        cap=CONT_CAP,
        scalars=1,
        scratch=[
            pltpu.VMEM((width, PROMPT + rows), BF16),
            pltpu.VMEM((heads // 2, PROMPT + rows, 256), BF16),
        ],
        aliases={7 + m: m for m in range(len(earlier))},
        after=after,
    )


def hop(x, bit):
    n = lax.axis_size("dp")
    return lax.ppermute(x, "dp", [(i, i ^ (1 << bit)) for i in range(n)])


def turn(x, step):
    n = lax.axis_size("dp")
    return lax.ppermute(x, "dp", [(i, i ^ (4 if (i & 1) ^ step else 2)) for i in range(n)])


def grad_back_kernel(flip, place, act, gffn, out):
    acc = tn(act[...], gffn[...])
    low = place[2] if flip else place[1]
    for m in range(2):
        out[pl.ds(jnp.bitwise_xor(low % 2, m), 1)] = acc[None, 192 * m : 192 * m + 192]


def grad_back(flip, place, act, gffn, after=()):
    low = lambda place: (place[2] if flip else place[1]) // 2 % 2
    return run(
        functools.partial(grad_back_kernel, flip),
        (place, act, gffn),
        [
            pl.BlockSpec((SLOTS, 384), lambda i, place: (0, 2 * ((place[1] // 4 + flip) % 2) + i)),
            whole((SLOTS, D)),
        ],
        pl.BlockSpec((2, 192, D), lambda i, place: (jnp.bitwise_xor(i, low(place)), 0, 0)),
        jax.ShapeDtypeStruct((4, 192, D), F32),
        (2,),
        "grad_w_back",
        cost(2 * SLOTS * 768 * D, 2 * SLOTS * 768 * 2 + 4 * 768 * D),
        cap=BACK_CAP,
        scalars=1,
        after=after,
    )


IN_BLOCK = 512


def grad_in_kernel(n, place, x, ghid, send, keep, xt):
    i = pl.program_id(0)

    @pl.when(i % n == 0)
    def _():
        xt[...] = x[...].T

    acc = nn(xt[...], ghid[...])

    def put(out, low):
        for m in range(4):
            out[pl.ds(jnp.bitwise_xor(low, m), 1)] = acc[None, 96 * m : 96 * m + 96]

    pl.when(i < n)(lambda: put(send, place[2]))
    pl.when(i >= n)(lambda: put(keep, place[1] % 4))


def grad_in(place, xlow, ghid, after=()):
    units = ghid.shape[1]
    n = units // IN_BLOCK
    shape = jax.ShapeDtypeStruct((4, 96, units), F32)
    return run(
        functools.partial(grad_in_kernel, n),
        (place, xlow, ghid),
        [
            pl.BlockSpec((SLOTS, 384), lambda i, place: (0, (place[1] // 4 + 1 - i // n) % 2)),
            pl.BlockSpec((SLOTS, IN_BLOCK), lambda i, *_: (0, i % n)),
        ],
        [
            pl.BlockSpec((4, 96, IN_BLOCK), lambda i, *_: (0, 0, jnp.minimum(i, n - 1))),
            pl.BlockSpec((4, 96, IN_BLOCK), lambda i, *_: (0, 0, jnp.maximum(i - n, 0))),
        ],
        [shape] * 2,
        (2 * n,),
        "grad_w_in",
        cost(4 * SLOTS * 384 * units, 2 * SLOTS * (768 + 2 * units) + 8 * 384 * units),
        scalars=1,
        scratch=[pltpu.VMEM((384, SLOTS), BF16)],
        after=after,
    )


def grad_rest_kernel(place, tok, gq, gk, gv, ctx_p, ctx_a, ctx_b, gattn, stats, other, *refs):
    send, keep, ao = refs
    i = pl.program_id(0)
    left = (place[1] // 4 + 1 - i) % 2 == 0

    @pl.when(i == 0)
    def _():
        ctx = jnp.concatenate([ctx_p[...], ctx_a[...], ctx_b[...]], axis=0).astype(BF16)
        ao[...] = nn(ctx.T, gattn[...])

    tok_t = tok[...].T
    aq = nn(tok_t, gq[...])
    ak = nn(tok_t, gk[...])
    av = nn(tok_t, gv[...])
    o = jnp.where(left, ao[:192], ao[192:])
    bias = jnp.concatenate(
        [jnp.sum(g[...].astype(F32), axis=0, keepdims=True) for g in (gq, gv)], axis=1
    )
    row = lax.broadcasted_iota(jnp.int32, (16, D), 0)
    half_of = lax.broadcasted_iota(jnp.int32, (16, D), 1) // (D // 2)
    small = jnp.where((half_of == place[0]) | (row >= 7), stats[...], other[...])
    small = jnp.where(row == 9, bias, small)

    def put(out, low):
        for m in range(4):
            j = jnp.bitwise_xor(low, m)
            out[pl.ds(j, 1), 0:96, 0:384] = aq[None, 96 * m : 96 * m + 96]
            out[pl.ds(j, 1), 0:96, 384:768] = ak[None, 96 * m : 96 * m + 96]
            out[pl.ds(j, 1), 96:144, 0:384] = av[None, 96 * m : 96 * m + 48]
            out[pl.ds(j, 1), 96:144, 384:768] = av[None, 96 * m + 48 : 96 * m + 96]
            out[pl.ds(j, 1), 144:192, :] = o[None, 48 * m : 48 * m + 48]
            out[pl.ds(j, 1), 192:200, :] = jnp.concatenate(
                [
                    jnp.where(left, small[2 * m : 2 * m + 2], small[8 + 2 * m : 10 + 2 * m]),
                    jnp.zeros((6, D), F32),
                ],
                axis=0,
            )[None]

    pl.when(i == 0)(lambda: put(send, place[2]))
    pl.when(i == 1)(lambda: put(keep, place[1] % 4))


def grad_rest(place, tokens, gq, gk, gv, ctx_p, ctx_a, ctx_b, gattn, stats, other, after=()):
    width = gq.shape[1]
    shape = jax.ShapeDtypeStruct((4, 200, D), F32)
    fixed = (gq, gk, gv, ctx_p, ctx_a, ctx_b, gattn, stats, other)
    return run(
        grad_rest_kernel,
        (place, tokens) + fixed,
        [pl.BlockSpec((SLOTS, 384), lambda i, place: (0, (place[1] // 4 + 1 - i) % 2))]
        + [const(x) for x in fixed],
        [const(shape)] * 2,
        [shape] * 2,
        (2,),
        "grad_w_rest",
        cost(2 * SLOTS * (D * 3 * width + width * D), 2 * SLOTS * (6 * width + 2 * D)),
        scalars=1,
        scratch=[pltpu.VMEM((width, D), F32)],
        after=after,
    )


def chunk_of(place, far, m):
    if far:
        return (1 - place[1] // 4) * 4 + jnp.bitwise_xor(place[2], m)
    return jnp.bitwise_xor(place[1], m)


def staged(moves):
    for first, _ in moves:
        first.start()
    for first, rest in moves:
        first.wait()
        for c in rest:
            c.start()
    for _, rest in moves:
        for c in rest:
            c.wait()


def order_kernel(rows, far, place, src, *refs):
    out, hold, sems_in, sems_out = refs[-4:]
    moves = []
    for m in range(4):
        at = pl.multiple_of(chunk_of(place, far, m) * rows, 8)
        moves.append(
            (
                pltpu.make_async_copy(src.at[m], hold.at[m], sems_in.at[m]),
                [pltpu.make_async_copy(hold.at[m], out.at[pl.ds(at, rows)], sems_out.at[m])],
            )
        )
    staged(moves)


def in_order(far, place, chunks, prev=None, after=()):
    _, rows, cols = chunks.shape
    return run(
        functools.partial(order_kernel, rows, far),
        (place, chunks) + (() if prev is None else (prev,)),
        [ANY] * (1 if prev is None else 2),
        ANY,
        jax.ShapeDtypeStruct((8 * rows, cols), F32),
        (1,),
        "in_order",
        cost(0, 8 * chunks.size),
        scalars=1,
        scratch=[pltpu.VMEM(chunks.shape, F32), pltpu.SemaphoreType.DMA((4,)), pltpu.SemaphoreType.DMA((4,))],
        aliases={} if prev is None else {2: 0},
        after=after,
    )


def order_rest_kernel(far, width, place, src, *refs):
    gw, go, small, hold, sems_in, sems_out = refs[-6:]
    moves, n = [], 0

    def copy(a, b):
        nonlocal n
        n += 1
        return pltpu.make_async_copy(a, b, sems_out.at[n - 1])

    left, right = pl.ds(0, width), pl.ds(width, width)
    for m in range(4):
        c = chunk_of(place, far, m)
        rows = hold.at[m]
        wide = pl.ds(pl.multiple_of(c * 96, 8), 96)
        out = [
            copy(rows.at[pl.ds(0, 96), left], gw.at[0, wide]),
            copy(rows.at[pl.ds(0, 96), right], gw.at[1, wide]),
            copy(rows.at[pl.ds(96, 48), left], gw.at[2, pl.ds(pl.multiple_of(c * 96, 8), 48)]),
            copy(rows.at[pl.ds(96, 48), right], gw.at[2, pl.ds(pl.multiple_of(c * 96 + 48, 8), 48)]),
            copy(rows.at[pl.ds(144, 48)], go.at[pl.ds(pl.multiple_of(c * 48, 8), 48)]),
            copy(rows.at[pl.ds(192, 8)], small.at[pl.ds(pl.multiple_of(c * 8, 8), 8)]),
        ]
        moves.append((pltpu.make_async_copy(src.at[m], rows, sems_in.at[m]), out))
    staged(moves)


def order_rest(far, place, chunks, width, prev=None, after=()):
    return run(
        functools.partial(order_rest_kernel, far, width),
        (place, chunks) + (() if prev is None else tuple(prev)),
        [ANY] * (1 if prev is None else 4),
        [ANY] * 3,
        [
            jax.ShapeDtypeStruct((3, D, width), F32),
            jax.ShapeDtypeStruct((width, D), F32),
            jax.ShapeDtypeStruct((64, D), F32),
        ],
        (1,),
        "order_rest",
        cost(0, 8 * chunks.size),
        scalars=1,
        scratch=[
            pltpu.VMEM(chunks.shape, F32),
            pltpu.SemaphoreType.DMA((4,)),
            pltpu.SemaphoreType.DMA((24,)),
        ],
        aliases={} if prev is None else {2: 0, 3: 1, 4: 2},
        after=after,
    )


def small_kernel(count, rows, bias, gain, shift, b_in, qv, loss):
    row = lambda n: rows[8 * (n // 2) + n % 2 : 8 * (n // 2) + n % 2 + 1]
    bias[0:1], bias[1:2] = row(4), row(1)
    gain[0:1], gain[1:2] = row(5), row(2)
    shift[0:1], shift[1:2] = row(6), row(3)
    b_in[0:1, :D], b_in[0:1, D:] = row(7), row(8)
    qv[0:1], qv[1:2] = row(9)[:, : D // 2], row(9)[:, D // 2 :]
    loss[...] = jnp.sum(row(0), axis=1, keepdims=True) / count


def small_outputs(count, rows):
    shapes = [(2, D)] * 3 + [(1, 2 * D), (2, D // 2), (1, 1)]
    return run(
        functools.partial(small_kernel, count),
        (rows,),
        [whole(rows.shape)],
        [whole(x) for x in shapes],
        [jax.ShapeDtypeStruct(x, F32) for x in shapes],
        (1,),
        "small_outputs",
        cost(0, 8 * rows.size),
    )


def lay_out(place, pieces, wi, wo, wb, b):
    for far in range(2):
        own_a, rest_a = pieces[2 * far : 2 * far + 2]
        most_b, cross_b = pieces[4 + 2 * far : 6 + 2 * far]
        for m in range(4):
            c = jnp.bitwise_xor(place[3], 4 * far + m)
            src_a = own_a if m == 0 else rest_a.at[pl.ds((m - 1) * 128, 128)]
            src_b = cross_b if m == 3 else most_b.at[pl.ds(m * 192, 192)]
            wi[pl.ds(pl.multiple_of(c * 96, 16), 96), :] = src_a[0:96, :].astype(BF16)
            tail = src_a[96:120, :]
            wo[pl.ds(pl.multiple_of(c * 48, 16), 48), :] = jnp.concatenate(
                [tail[:, :D], tail[:, D:]], axis=0
            ).astype(BF16)
            wb[pl.ds(pl.multiple_of(c * 192, 16), 192), :] = src_b[...].astype(BF16)
    b[...] = pieces[0][120:128, :]


def forward_kernel(first_block, count, has_prev, *refs):
    lens, place = refs[:2]
    if has_prev:
        ctx_own, ctx_oth, tok, teach, wo_own, wi_own, wb_own, b_own, bias_out, gain, shift = refs[2:13]
        wo_oth, wi_oth, wb_oth, b_oth = refs[13:17]
        out, act, gate, gffn, gsec, xlow, rstd, stats = refs[-8:]
        own, oth = ctx_own[...], ctx_oth[...]
    else:
        ctx_p, ctx_a, oth_p, oth_a, tok, teach, wo_own, wi_own, wb_own, b_own, bias_out, gain, shift = refs[2:15]
        pieces = refs[15:23]
        out, act, gate, gffn, gsec, xlow, rstd, stats, wo_oth, wi_oth, wb_oth, b_oth = refs[-12:]
        early = pl.program_id(0) < PROMPT // ROWS
        own = jnp.where(early, ctx_p[...], ctx_a[...])
        oth = jnp.where(early, oth_p[...], oth_a[...])

        @pl.when(pl.program_id(0) == 0)
        def _():
            lay_out(place, pieces, wi_oth, wo_oth, wb_oth, b_oth)

    i = pl.program_id(0)
    blk = i + first_block
    n_own = wi_own.shape[1] // UNITS

    @pl.when(i == 0)
    def _():
        stats[...] = jnp.zeros_like(stats)

    attn = nn(own.astype(BF16), wo_own[...]) + nn(oth.astype(BF16), wo_oth[...])
    fin = tok[...].astype(F32) + attn + bias_out[0:1]
    c1 = fin - jnp.mean(fin, axis=-1, keepdims=True)
    r1 = lax.rsqrt(jnp.mean(c1 * c1, axis=-1, keepdims=True) + EPS_NORM)
    rstd[...] = jnp.broadcast_to(r1, rstd.shape)
    first = c1 * r1 * gain[0:1] + shift[0:1]
    x = first.astype(BF16)
    xlow[...] = x
    ffn = None
    for side in range(2):
        wi, wb, bb = ((wi_own, wb_own, b_own), (wi_oth, wb_oth, b_oth))[side]
        for u in range(n_own):
            cols = slice(u * UNITS, (u + 1) * UNITS)
            h = nn(x, wi[:, cols]) + bb[0:1, cols]
            cdf = 0.5 + 0.5 * lax.erf(h * 0.7071067811865476)
            pdf = jnp.exp(-0.5 * h * h) * 0.3989422804014327
            a = (h * cdf).astype(BF16)
            at = (side * n_own + u) * UNITS
            gate[:, at : at + UNITS] = (cdf + h * pdf).astype(BF16)
            if side == 0:
                act[:, cols] = a
            part = nn(a, wb[cols, :])
            ffn = part if ffn is None else ffn + part
    sec = first + ffn + bias_out[1:2]
    c2 = sec - jnp.mean(sec, axis=-1, keepdims=True)
    r2 = lax.rsqrt(jnp.mean(c2 * c2, axis=-1, keepdims=True) + EPS_NORM)
    xh2 = c2 * r2
    result = xh2 * gain[1:2] + shift[1:2]
    left = place[0] == 0
    hd = D // 2
    out[...] = jnp.where(left, result[:, :hd], result[:, hd:]).astype(BF16)
    row = lax.broadcasted_iota(jnp.int32, (ROWS, 1), 0)
    per = ROWS // CONT_LEN
    cont0 = (blk - PROMPT // ROWS) * per
    valid = jnp.zeros((ROWS, 1), jnp.bool_)
    for m in range(per):
        length = jnp.where(cont0 < 0, CONT_LEN, lens[0, jnp.maximum(cont0 + m, 0)])
        valid = valid | ((row >= m * CONT_LEN) & (row < m * CONT_LEN + length))
    diff = jnp.where(valid, result - teach[...].astype(F32), 0.0)
    g = diff * (2.0 / count)
    gy = g * gain[1:2]
    g2 = r2 * (
        gy
        - jnp.mean(gy, axis=-1, keepdims=True)
        - xh2 * jnp.mean(gy * xh2, axis=-1, keepdims=True)
    )
    stats[0:1] += jnp.sum(diff * diff, axis=0, keepdims=True)
    stats[1:2] += jnp.sum(g2, axis=0, keepdims=True)
    stats[2:3] += jnp.sum(g * xh2, axis=0, keepdims=True)
    stats[3:4] += jnp.sum(g, axis=0, keepdims=True)
    gsec[...] = g2
    gffn[...] = g2.astype(BF16)


def rows_forward(first_block, blocks, count, lens, place, ctxs, tok, teach, fixed, more, prev=None, after=()):
    width = ctxs[0].shape[1]
    units = fixed[1].shape[1]
    row = lambda w: pl.BlockSpec((ROWS, w), lambda i, *_: (i + first_block, 0))
    split = PROMPT // ROWS
    if prev is None:
        low = pl.BlockSpec((ROWS, width), lambda i, *_: (jnp.minimum(i, split - 1), 0))
        high = pl.BlockSpec((ROWS, width), lambda i, *_: (jnp.maximum(i - split, 0), 0))
        ctx_specs = [low, high, low, high]
    else:
        ctx_specs = [pl.BlockSpec((ROWS, width), lambda i, *_: (i, 0))] * 2
    shapes = [(D // 2, BF16), (units, BF16), (2 * units, BF16), (D, BF16), (D, F32), (D, BF16), (128, F32)]
    operands = [lens, place, *ctxs, tok, teach, *fixed, *more]
    specs = ctx_specs + [row(D), row(D)] + [const(a) for a in fixed] + [const(a) for a in more]
    aliases = {}
    out_specs = [row(w) for w, _ in shapes] + [whole((16, D))]
    out_shape = [jax.ShapeDtypeStruct((SLOTS, w), t) for w, t in shapes] + [jax.ShapeDtypeStruct((16, D), F32)]
    if prev is None:
        weights = [
            jax.ShapeDtypeStruct((width, D), BF16),
            jax.ShapeDtypeStruct((D, units), BF16),
            jax.ShapeDtypeStruct((units, D), BF16),
            jax.ShapeDtypeStruct((8, units), F32),
        ]
        out_specs, out_shape = out_specs + [const(w) for w in weights], out_shape + weights
    else:
        aliases = {len(operands) + n: n for n in range(7)}
        operands, specs = operands + list(prev), specs + [ANY] * 7
    return run(
        functools.partial(forward_kernel, first_block, count, prev is not None),
        operands,
        specs,
        out_specs,
        out_shape,
        (blocks,),
        "rows_forward",
        cap=VMEM_WIDE,
        estimate=cost(2 * blocks * ROWS * D * (4 * units + 2 * width), 8 * D * units + blocks * ROWS * 24000),
        scalars=2,
        aliases=aliases,
        after=after,
    )


def backward_kernel(place, gate, gffn, gsec, xlow, rstd, wo, wi_own, wi_oth, wb_own, wb_oth, gain, shift,
                    stats_f, *refs):
    ghid, gattn, gctx, gfin, stats, gbin = refs[-6:]
    i = pl.program_id(0)
    n_own = wi_own.shape[1] // UNITS

    @pl.when(i == 0)
    def _():
        stats[...] = stats_f[...]
        gbin[0:1, :D] = stats_f[7:8]
        gbin[0:1, D:] = stats_f[8:9]

    gf = gffn[...]
    gfirst = gsec[...]
    for side in range(2):
        wi, wb = ((wi_own, wb_own), (wi_oth, wb_oth))[side]
        for u in range(n_own):
            cols = slice(u * UNITS, (u + 1) * UNITS)
            at = (side * n_own + u) * UNITS
            gh = (nt(gf, wb[cols, :]) * gate[:, at : at + UNITS].astype(F32)).astype(BF16)
            if side == 0:
                ghid[:, cols] = gh
                gbin[0:1, cols] += jnp.sum(gh.astype(F32), axis=0, keepdims=True)
            gfirst = gfirst + nt(gh, wi[:, cols])
    xh1 = (xlow[...].astype(F32) - shift[0:1]) * (1.0 / gain[0:1])
    gy1 = gfirst * gain[0:1]
    g1 = rstd[:, 0:1] * (
        gy1
        - jnp.mean(gy1, axis=-1, keepdims=True)
        - xh1 * jnp.mean(gy1 * xh1, axis=-1, keepdims=True)
    )
    stats[4:5] += jnp.sum(g1, axis=0, keepdims=True)
    stats[5:6] += jnp.sum(gfirst * xh1, axis=0, keepdims=True)
    stats[6:7] += jnp.sum(gfirst, axis=0, keepdims=True)

    @pl.when(i == pl.num_programs(0) - 1)
    def _():
        stats[7:8] = gbin[0:1, :D]
        stats[8:9] = gbin[0:1, D:]

    hd = D // 2
    gfin[...] = jnp.where(place[0] == 0, g1[:, :hd], g1[:, hd:])
    ga1 = g1.astype(BF16)
    gattn[...] = ga1
    gctx[...] = nt(ga1, wo[...]).astype(BF16)


def rows_backward(first, blocks, place, gate, gffn, gsec, xlow, rstd, fixed, prev=None, after=()):
    wo, wi_own = fixed[:2]
    width, units = wo.shape[0], wi_own.shape[1]
    row = lambda w: pl.BlockSpec((ROWS, w), lambda i, *_: (i + first, 0))
    shapes = [(units, BF16), (D, BF16), (width, BF16), (D // 2, F32)]
    operands = [place, gate, gffn, gsec, xlow, rstd] + list(fixed)
    specs = [row(2 * units), row(D), row(D), row(D), row(128)] + [const(a) for a in fixed]
    aliases = {}
    if prev is not None:
        aliases = {len(operands) + n: n for n in range(4)}
        operands, specs = operands + list(prev), specs + [ANY] * 4
    return run(
        backward_kernel,
        operands,
        specs,
        [row(w) for w, _ in shapes] + [whole((16, D))],
        [jax.ShapeDtypeStruct((SLOTS, w), t) for w, t in shapes] + [jax.ShapeDtypeStruct((16, D), F32)],
        (blocks,),
        "rows_backward",
        cost(2 * SLOTS * D * (4 * units + width), 8 * D * units + SLOTS * 20000),
        scalars=1,
        scratch=[pltpu.VMEM((8, units), F32)],
        aliases=aliases,
        after=after,
    )


def attend_back(q, gctx, ctx, inv, load, vt, kall, gq, take, groups):
    heads = q.shape[1] // HEAD
    g2, inner, qt, gt = [], [], [], []
    for p in range(heads // 2):
        cols = pair(2 * p)
        g = (gctx[:, cols].astype(F32) * inv[:, cols]).astype(BF16)
        prod = g.astype(F32) * ctx[:, cols]
        g2.append(g)
        qt.append(q[:, cols].T)
        gt.append(g.T)
        inner += [jnp.sum(only(prod, h), axis=-1, keepdims=True) for h in range(2)]

    def weigh(h):
        gm = only(g2[h // 2], h % 2)
        return nn(gm, vt[pair(h), :PROMPT]), [
            nn(gm[r], vt[pair(h), c]) for r, c in zip(parts(groups), own_keys(groups))
        ]

    def finish(h, e, l):
        part = slice(h % 2 * HEAD, (h % 2 + 1) * HEAD)
        q_h, g_h = qt[h // 2][part], gt[h // 2][part]
        dq = nn(l[0], kall[:PROMPT, pair(h)])
        own = []
        if groups:
            dq = dq + jnp.concatenate(
                [nn(x, kall[c, pair(h)]) for x, c in zip(l[1], own_keys(groups))], axis=0
            )
            own = [
                (nn(q_h[:, r], x), nn(g_h[:, r], y))
                for r, x, y in zip(parts(groups), l[1], e[1])
            ]
        return dq, (nn(q_h, l[0]), nn(g_h, e[0])), own

    mine = half_mask(q.shape[0], 0)
    done = []

    def flush(h):
        done.append(finish(h, *held[h]))
        if h % 2:
            a, b = done[h - 1], done[h]
            gq[:, pair(h)] = (jnp.where(mine, a[0], b[0]) * 0.125).astype(BF16)
            both = lambda x, y: tuple(jnp.concatenate(z, axis=0) for z in zip(x, y))
            take(pair(h), both(a[1], b[1]), [both(x, y) for x, y in zip(a[2], b[2])])

    raw, held = [weigh(0)], []
    for h in range(heads):
        if h + 1 < heads:
            raw.append(weigh(h + 1))
        e = load(h)
        l = [(e[0].astype(F32) * (raw[h][0] - inner[h])).astype(BF16)]
        l.append(
            [
                (y.astype(F32) * (x - inner[h][r])).astype(BF16)
                for y, x, r in zip(e[1], raw[h][1], parts(groups))
            ]
        )
        held.append((e, l))
        if h:
            flush(h - 1)
    flush(heads - 1)


def cont_bwd_kernel(split, q, kp, vp, ko, vo, weights, gctx, ctx_a, inv_a, ctx_b, inv_b,
                    gq, gk, gv, gkp, gvp, vt, kall):
    early = pl.program_id(0) < split
    ctx = jnp.where(early, ctx_a[...], ctx_b[...])
    inv = jnp.where(early, inv_a[...], inv_b[...])

    @pl.when(pl.program_id(0) == 0)
    def _():
        gkp[...] = jnp.zeros_like(gkp)
        gvp[...] = jnp.zeros_like(gvp)
        vt[:, :PROMPT] = vp[...].T
        kall[:PROMPT] = kp[...]

    vt[:, PROMPT:] = vo[...].T
    kall[PROMPT:] = ko[...]

    def load(h):
        return (
            jnp.concatenate([weights[g, h, :, :PROMPT] for g in range(GROUP)], axis=0),
            [weights[g, h, :, PROMPT:] for g in range(GROUP)],
        )

    def take(cols, front, own):
        gkp[cols, :] += front[0]
        gvp[cols, :] += front[1]
        for r, (dk, dv) in zip(parts(GROUP), own):
            gk[r, cols] = dk.T.astype(BF16)
            gv[r, cols] = dv.T.astype(BF16)

    attend_back(q[...], gctx[...], ctx, inv, load, vt, kall, gq, take, GROUP)


def cont_backward(q, k, v, weights, gctx, ctx_a, inv_a, ctx_b, inv_b, after=()):
    heads = weights.shape[1]
    width = heads * HEAD
    rows = GROUP * CONT_LEN
    first = PROMPT // rows
    own = pl.BlockSpec((rows, width), lambda c: (c + first, 0))
    front = pl.BlockSpec((PROMPT, width), lambda c: (0, 0))
    big = pl.BlockSpec((GROUP, heads, CONT_LEN, KEYS), lambda c: (c, 0, 0, 0))
    shape = jax.ShapeDtypeStruct((SLOTS, width), BF16)
    sums = jax.ShapeDtypeStruct((width, PROMPT), F32)
    n = CONT * heads * CONT_LEN * KEYS
    split = ctx_a.shape[0] // rows
    head = pl.BlockSpec((rows, width), lambda c: (jnp.minimum(c, split - 1), 0))
    tail = pl.BlockSpec((rows, width), lambda c: (jnp.maximum(c - split, 0), 0))
    return run(
        functools.partial(cont_bwd_kernel, split),
        (q, k, v, k, v, weights, gctx, ctx_a, inv_a, ctx_b, inv_b),
        [own, front, front, own, own, big, own, head, head, tail, tail],
        [own, own, own, whole((width, PROMPT)), whole((width, PROMPT))],
        [shape, shape, shape, sums, sums],
        (CONT // GROUP,),
        "attn_cont_bwd",
        cost(8 * n * HEAD, 2 * n + 8 * SLOTS * heads * HEAD * 2),
        scratch=[pltpu.VMEM((width, PROMPT + rows), BF16), pltpu.VMEM((PROMPT + rows, width), BF16)],
        after=after,
    )


def prompt_bwd_kernel(q, k, v, weights, gctx, ctx, inv, gkp, gvp, a, b, c, gq, gk, gv, vt, ak, av):
    r = pl.program_id(0)

    @pl.when(r == 0)
    def _():
        vt[...] = v[...].T
        ak[...] = gkp[...]
        av[...] = gvp[...]

    def take(cols, front, own):
        ak[cols, :] += front[0]
        av[cols, :] += front[1]

    attend_back(q[...], gctx[...], ctx[...], inv[...], lambda h: (weights[h], []), vt, k, gq, take, 0)

    @pl.when(r == pl.num_programs(0) - 1)
    def _():
        gk[...] = ak[...].T.astype(BF16)
        gv[...] = av[...].T.astype(BF16)


def prompt_backward(q, k, v, weights, gctx, ctx, inv, gkp, gvp, gq, gk, gv, after=()):
    heads = weights.shape[0]
    width = heads * HEAD
    rows = 256
    row = pl.BlockSpec((rows, width), lambda r: (r, 0))
    front = pl.BlockSpec((PROMPT, width), lambda r: (0, 0))
    acc = whole((width, PROMPT))
    shape = jax.ShapeDtypeStruct((SLOTS, width), BF16)
    n = heads * PROMPT * PROMPT
    return run(
        prompt_bwd_kernel,
        (q, k, v, weights, gctx, ctx, inv, gkp, gvp, gq, gk, gv),
        [row, front, front, pl.BlockSpec((heads, rows, PROMPT), lambda r: (0, r, 0)), row, row, row, acc, acc]
        + [ANY] * 3,
        [row, front, front],
        [shape] * 3,
        (PROMPT // rows,),
        "attn_prompt_bwd",
        cost(8 * n * HEAD, 2 * n + 8 * PROMPT * heads * HEAD * 2),
        scratch=[
            pltpu.VMEM((width, PROMPT), BF16),
            pltpu.VMEM((width, PROMPT), F32),
            pltpu.VMEM((width, PROMPT), F32),
        ],
        aliases={9: 0, 10: 1, 11: 2},
        after=after,
    )


def input_grad_kernel(place, gq, gk, gv, w, base, *refs):
    sends, keep = refs[:-1], refs[-1]
    hd = D // 2
    mine = place[0] == 0
    part = nt(gq[...], w[0]) + nt(gk[...], w[1]) + nt(gv[...], w[2])
    keep[...] = base[...] + jnp.where(mine, part[:, :hd], part[:, hd:])
    away = jnp.where(mine, part[:, hd:], part[:, :hd])

    def put(send):
        send[...] = away

    per = SLOTS // part.shape[0] // len(sends)
    for n, send in enumerate(sends):
        pl.when(pl.program_id(0) // per == n)(functools.partial(put, send))


def input_grad(place, gq, gk, gv, w3, base, after=()):
    width = w3.shape[2]
    rows, cuts = 384, 4
    per = SLOTS // rows // cuts
    row = lambda w: pl.BlockSpec((rows, w), lambda i, *_: (i, 0))
    cut = lambda n: pl.BlockSpec((rows, D // 2), lambda i, *_: (jnp.clip(i - n * per, 0, per - 1), 0))
    return run(
        input_grad_kernel,
        (place, gq, gk, gv, w3, base),
        [row(width)] * 3 + [whole((3, D, width)), row(D // 2)],
        [cut(n) for n in range(cuts)] + [row(D // 2)],
        [jax.ShapeDtypeStruct((SLOTS // cuts, D // 2), F32)] * cuts + [jax.ShapeDtypeStruct((SLOTS, D // 2), F32)],
        (SLOTS // rows,),
        "input_grad",
        cost(2 * SLOTS * D * 3 * width, 2 * (SLOTS * 3 * width) + 6 * SLOTS * D),
        scalars=1,
        after=after,
    )


def swap(x):
    n = lax.axis_size("tensor")
    return lax.ppermute(x, "tensor", [(i, n - 1 - i) for i in range(n)])


def tie(*values):
    return lax.optimization_barrier(values)


def far_exchange(total):
    bit = 4
    while (1 << bit) < lax.axis_size("dp"):
        total = total + hop(total, bit)
        bit += 1
    return total


def local(
    tokens, teacher, lengths, prev_prompt, prev_cont, w_qkv, bias_qv, w_out, w_in, b_in, w_back,
    bias_out, norm_gain, norm_bias,
):
    width = w_qkv.shape[2]
    units = w_in.shape[1]
    w3 = jnp.transpose(w_qkv, (1, 0, 2))
    t = lax.axis_index("tensor").astype(jnp.int32)
    i = lax.axis_index("dp").astype(jnp.int32)
    core, x, z = i % 2, (i // 2) % 2, (i // 4) % 2
    x_first, z_first = 2 * x + z, 2 * z + x
    chunk = core * 4 + x_first
    place = jnp.stack(
        [
            t,
            core * 4 + jnp.where(core == 0, x_first, z_first),
            jnp.where(core == 0, z_first, x_first),
            chunk,
        ]
    )
    count = float(lax.axis_size("dp") * (PROMPT + TOTAL))

    part_o = lax.dynamic_slice_in_dim(w_out, chunk * 48, 48, 0)
    part_i = lax.dynamic_slice_in_dim(w_in, chunk * 96, 96, 0)
    piece_a = jnp.concatenate(
        [
            part_i.astype(F32),
            jnp.concatenate([part_o[:24], part_o[24:]], axis=1).astype(F32),
            jnp.broadcast_to(b_in[None], (8, units)),
        ],
        axis=0,
    )
    piece_b = lax.dynamic_slice_in_dim(w_back, chunk * 192, 192, 0).astype(F32)
    own_a = swap(piece_a)
    own_b = swap(piece_b)
    q, k, v = project(tokens, w3, bias_qv)
    logits_p, probs_p, ctx_p, inv_p = prompt_forward(q, k, v, prev_prompt[0])
    own_a, ctx_p = tie(own_a, ctx_p)
    oth_p = swap(ctx_p)
    zs_a, xs_a, far_own_a = hop(own_a, 2), hop(own_a, 1), hop(own_a, 0)
    logits_c, probs_c, ctx_a, inv_a = cont_forward(0, 4, lengths, q, k, v, prev_cont[0], after=(own_a,))
    zs_a, xs_a, far_own_a, own_b, ctx_a = tie(zs_a, xs_a, far_own_a, own_b, ctx_a)
    oth_a = swap(ctx_a)
    logits_c, probs_c, ctx_b, inv_b = cont_forward(
        4, 4, lengths, q, k, v, prev_cont[0], (logits_c, probs_c)
    )
    zs_b, xs_b = hop(own_b, 2), hop(own_b, 1)
    cross_a = turn(jnp.where(core == 0, zs_a, xs_a), 0)
    cross_a, oth_p, zs_b, xs_b, ctx_b = tie(cross_a, oth_p, zs_b, xs_b, ctx_b)
    cross_b = turn(jnp.where(core == 0, zs_b, xs_b), 0)
    rest_a = jnp.concatenate([zs_a, xs_a, cross_a], axis=0)
    most_b = jnp.concatenate([own_b, zs_b, xs_b], axis=0)
    far_rest_a, far_most_b = hop(rest_a, 0), hop(most_b, 0)
    oth_a, cross_b, far_rest_a, far_most_b = tie(oth_a, cross_b, far_rest_a, far_most_b)
    oth_b = swap(ctx_b)
    far_cross_b = hop(cross_b, 0)

    fixed = (w_out, w_in, w_back, b_in[None], bias_out, norm_gain, norm_bias)
    pieces = (
        own_a, rest_a, far_own_a, far_rest_a, most_b, cross_b, far_most_b, far_cross_b,
    )
    n_blocks = SLOTS // ROWS
    lead = (PROMPT + 4 * CONT_LEN) // ROWS
    first = rows_forward(
        0, lead, count, lengths, place, (ctx_p, ctx_a, oth_p, oth_a), tokens, teacher, fixed, pieces
    )
    kept, stats_a, (wo_oth, wi_oth, wb_oth, b_oth) = list(first[:7]), first[7], first[8:]
    oth_b, kept[0] = tie(oth_b, kept[0])
    *kept, stats_f = rows_forward(
        lead, n_blocks - lead, count, lengths, place, (ctx_b, oth_b), tokens, teacher, fixed,
        (wo_oth, wi_oth, wb_oth, b_oth), kept,
    )
    output, act, gate, gffn, gsec, xlow, rstd = kept
    stats_f = stats_f + stats_a

    def split(keep, got, n):
        return keep[n:] + got[n:], keep[:n] + got[:n]

    w_fixed = (w_out, w_in, wi_oth, w_back, wb_oth, norm_gain, norm_bias, stats_f)
    b_send = grad_back(1, place, act, gffn)
    b_got = hop(b_send, 0)
    b_keep = grad_back(0, place, act, gffn, after=(b_send,))
    b_got, b_keep = tie(b_got, b_keep)
    b_out, b_keep = split(b_keep, b_got, 2)
    b_got = turn(b_out, 0)
    ghid, gattn, gctx, gfin_half, stats = rows_backward(
        0, n_blocks, place, gate, gffn, gsec, xlow, rstd, w_fixed, after=(b_out, b_keep)
    )
    b_got, ghid = tie(b_got, ghid)
    b_out, b_keep = split(b_keep, b_got, 1)
    b_got = turn(b_out, 1)
    other_stats = swap(stats)
    i_send, i_keep = grad_in(place, xlow, ghid, after=(b_out, b_keep))
    b_got, other_stats, i_send = tie(b_got, other_stats, i_send)
    b_top, b_end = b_keep[:, :96] + b_got[:, :96], b_keep[:, 96:] + b_got[:, 96:]
    b_got = hop(b_top, 3)
    i_got = hop(i_send, 0)
    gq, gk, gv, gkp, gvp = cont_backward(
        q, k, v, probs_c, gctx, ctx_a, inv_a, ctx_b, inv_b, after=(b_top, b_end)
    )
    i_got, b_got, gq = tie(i_got, b_got, gq)
    i_out, i_keep = split(i_keep, i_got, 2)
    i_got = turn(i_out, 0)
    b_more = hop(b_end, 3)
    gq, gk, gv = prompt_backward(
        q, k, v, probs_p, gctx, ctx_p, inv_p, gkp, gvp, gq, gk, gv, after=(i_out, i_keep)
    )
    r_send, r_keep = grad_rest(place, tokens, gq, gk, gv, ctx_p, ctx_a, ctx_b, gattn, stats, other_stats)
    i_got, b_more, r_send = tie(i_got, b_more, r_send)
    r_got = hop(r_send, 0)
    i_out, i_keep = split(i_keep, i_got, 1)
    i_got = turn(i_out, 1)
    b_total = far_exchange(jnp.concatenate([b_top + b_got, b_end + b_more], axis=1))
    b_got = turn(b_total, 1)
    r_got, i_got, b_got = tie(r_got, i_got, b_got)
    r_out, r_keep = split(r_keep, r_got, 2)
    r_got = turn(r_out, 0)
    i_top, i_end = i_keep[:, :48] + i_got[:, :48], i_keep[:, 48:] + i_got[:, 48:]
    i_got = hop(i_top, 3)
    b_two = jnp.concatenate([b_total, b_got], axis=0)
    *sends, keep = input_grad(place, gq, gk, gv, w3, gfin_half, after=(r_out, r_keep, i_top, i_end, b_two))
    r_got, i_got, keep = tie(r_got, i_got, keep)
    swapped = [swap(sends[0])]
    r_out, r_keep = split(r_keep, r_got, 1)
    r_got = turn(r_out, 1)
    i_more = hop(i_end, 3)
    r_got, i_more, swapped[0] = tie(r_got, i_more, swapped[0])
    swapped.append(swap(sends[1]))
    r_total = r_keep + r_got
    r_got = hop(r_total, 3)
    b_got = turn(b_two, 0)
    i_total = far_exchange(jnp.concatenate([i_top + i_got, i_end + i_more], axis=1))
    i_got = turn(i_total, 1)
    r_got, b_got, i_got, swapped[1] = tie(r_got, b_got, i_got, swapped[1])
    swapped.append(swap(sends[2]))
    r_total = far_exchange(r_total + r_got)
    r_got = turn(r_total, 1)
    i_two = jnp.concatenate([i_total, i_got], axis=0)
    i_got = turn(i_two, 0)
    b_near = jnp.concatenate([b_two, b_got], axis=0)
    b_far = hop(b_near, 0)
    r_got, i_got, b_far, b_near, swapped[2] = tie(r_got, i_got, b_far, b_near, swapped[2])
    swapped.append(swap(sends[3]))
    grad_w_back = in_order(1, place, b_far, in_order(0, place, b_near))
    r_two = jnp.concatenate([r_total, r_got], axis=0)
    r_got = turn(r_two, 0)
    i_near = jnp.concatenate([i_two, i_got], axis=0)
    i_far = hop(i_near, 0)
    grad_w_in = in_order(1, place, i_far, in_order(0, place, i_near, after=(r_two,)))
    grad_w_in, swapped[3] = tie(grad_w_in, swapped[3])
    grad_tokens = keep + jnp.concatenate(swapped, axis=0)
    r_got, grad_tokens, grad_w_back = tie(r_got, grad_tokens, grad_w_back)
    r_near = jnp.concatenate([r_two, r_got], axis=0)
    r_far = hop(r_near, 0)
    rest = order_rest(0, place, r_near, width)
    grad_w3, grad_w_out, rows = order_rest(1, place, r_far, width, rest)
    grad_bias, grad_gain, grad_shift, grad_b_in, grad_qv, loss = small_outputs(count, rows)
    return (
        output,
        logits_p[None],
        logits_c[None],
        grad_tokens,
        jnp.transpose(grad_w3, (1, 0, 2)),
        grad_qv,
        grad_w_out,
        grad_w_in,
        grad_b_in.reshape(units),
        grad_w_back,
        grad_bias,
        grad_gain,
        grad_shift,
        loss.reshape(()),
    )


def solution(mesh):
    in_specs = (
        P("dp", None),
        P("dp", None),
        P("dp", None),
        P("dp", "tensor", None, None),
        P("dp", None, "tensor", None, None),
        P(None, None, "tensor"),
        P(None, "tensor"),
        P("tensor", None),
        P(None, "tensor"),
        P("tensor"),
        P("tensor", None),
        P(),
        P(),
        P(),
    )
    out_specs = (
        P("dp", "tensor"),
        P("dp", "tensor", None, None),
        P("dp", None, "tensor", None, None),
        P("dp", "tensor"),
        P(None, None, "tensor"),
        P(None, "tensor"),
        P("tensor", None),
        P(None, "tensor"),
        P("tensor"),
        P("tensor", None),
        P(),
        P(),
        P(),
        P(),
    )
    return jax.shard_map(local, mesh=mesh, in_specs=in_specs, out_specs=out_specs, check_vma=False)
```

```python
import functools

import jax
import jax.numpy as jnp
from jax import lax
from jax.experimental import pallas as pl
from jax.experimental.pallas import tpu as pltpu
from jax.sharding import PartitionSpec as P

D = 768
HEAD = 64
PROMPT = 512
CONT = 8
CONT_LEN = 128
TOTAL = 576
KEYS = 640
SLOTS = 1536

NEG_FILL = -1e30
EPS_NORM = 1e-12
F32 = jnp.float32
BF16 = jnp.bfloat16
VMEM_CAP = 36 * 1024 * 1024
VMEM_WIDE = 60 * 1024 * 1024
CONT_CAP = 36 * 1024 * 1024
ROWS_CAP = 60 * 1024 * 1024
BACK_CAP = 24 * 1024 * 1024
ROWS = 256
UNITS = 1536
GROUP = 2
EARLY = 2
COST_DIV = 1000


def nn(a, b):
    return lax.dot_general(a, b, (((1,), (0,)), ((), ())), preferred_element_type=F32)


def nt(a, b):
    return lax.dot_general(a, b, (((1,), (1,)), ((), ())), preferred_element_type=F32)


def tn(a, b):
    return lax.dot_general(a, b, (((0,), (0,)), ((), ())), preferred_element_type=F32)


def whole(shape):
    return pl.BlockSpec(shape, lambda *_: (0,) * len(shape))


def const(a):
    return pl.BlockSpec(a.shape, lambda *_: (0,) * len(a.shape), pipeline_mode=pl.Buffered(1))


ANY = pl.BlockSpec(memory_space=pl.ANY)
IN_HBM = pl.BlockSpec(memory_space=pltpu.HBM)


def params(n, cap):
    return pltpu.CompilerParams(dimension_semantics=("arbitrary",) * n, vmem_limit_bytes=cap)


def cost(flops, nbytes, trans=0):
    return pl.CostEstimate(flops=int(flops / COST_DIV), bytes_accessed=int(nbytes / COST_DIV), transcendentals=0)


def run(kernel, operands, in_specs, out_specs, out_shape, grid, name, estimate, scalars=0, scratch=(),
        aliases=None, after=(), cap=VMEM_CAP):
    n, m = len(operands), len(after)

    def body(*refs):
        kernel(*refs[:n], *refs[n + m :])

    return pl.pallas_call(
        body,
        name=name,
        grid_spec=pltpu.PrefetchScalarGridSpec(
            num_scalar_prefetch=scalars,
            grid=grid,
            in_specs=list(in_specs) + [ANY] * m,
            out_specs=out_specs,
            scratch_shapes=scratch,
        ),
        out_shape=out_shape,
        input_output_aliases=aliases or {},
        compiler_params=params(len(grid), cap),
        cost_estimate=estimate,
    )(*operands, *after)


def qkv_kernel(tok, w, bias, q, k, v):
    x = tok[...]
    q[...] = (nn(x, w[0]) + bias[0:1]).astype(BF16) * jnp.asarray(0.125, BF16)
    k[...] = nn(x, w[1]).astype(BF16)
    v[...] = (nn(x, w[2]) + bias[1:2]).astype(BF16)


def project(tokens, w3, bias_qv):
    width = w3.shape[2]
    rows = 512
    spec = pl.BlockSpec((rows, width), lambda i: (i, 0))
    out = jax.ShapeDtypeStruct((SLOTS, width), BF16)
    return pl.pallas_call(
        qkv_kernel,
        name="qkv_proj",
        grid=(SLOTS // rows,),
        in_specs=[
            pl.BlockSpec((rows, D), lambda i: (i, 0)),
            whole((3, D, width)),
            whole((2, width)),
        ],
        out_specs=[spec] * 3,
        out_shape=[out] * 3,
        compiler_params=params(1, VMEM_CAP),
        cost_estimate=cost(2 * SLOTS * D * 3 * width, 2 * (SLOTS * D + 3 * D * width + 3 * SLOTS * width)),
    )(tokens, w3, bias_qv)


def half_mask(rows, h):
    lane = lax.broadcasted_iota(jnp.int32, (rows, 128), 1)
    return lane < HEAD if h == 0 else lane >= HEAD


def only(x, h):
    return jnp.where(half_mask(x.shape[0], h), x, jnp.zeros_like(x))


def pair(h):
    return slice(h // 2 * 128, h // 2 * 128 + 128)


def parts(groups):
    return [slice(g * CONT_LEN, (g + 1) * CONT_LEN) for g in range(groups)]


def own_keys(groups):
    return [slice(PROMPT + g * CONT_LEN, PROMPT + (g + 1) * CONT_LEN) for g in range(groups)]


def fill(kp, vp, kt, vx):
    kt[:, :PROMPT] = kp[...].T
    for p in range(kp.shape[1] // 128):
        vx[p, :PROMPT, :128] = vp[:, p * 128 : (p + 1) * 128]
        vx[p, :, 128:] = jnp.ones_like(vx[p, :, 128:])


def attend(q, kt, vx, soft, ctx, inv, groups):
    heads = q.shape[1] // HEAD

    def score(h):
        qm = only(q[:, pair(h)], h % 2)
        return nn(qm, kt[pair(h), :PROMPT]), [
            nn(qm[r], kt[pair(h), c]) for r, c in zip(parts(groups), own_keys(groups))
        ]

    def mix(h, e):
        out = nn(e[0], vx[h // 2, :PROMPT])
        if groups:
            out = out + jnp.concatenate(
                [nn(x, vx[h // 2, c]) for x, c in zip(e[1], own_keys(groups))], axis=0
            )
        return out

    s, e, outs = [score(0)], [], []
    for h in range(heads):
        if h + 1 < heads:
            s.append(score(h + 1))
        e.append(soft(h, *s[h]))
        if h:
            outs.append(mix(h - 1, e[h - 1]))
    outs.append(mix(heads - 1, e[-1]))
    mine = half_mask(q.shape[0], 0)
    for h in range(0, heads, 2):
        scale = 1.0 / jnp.where(mine, outs[h][:, 128:], outs[h + 1][:, 128:])
        inv[:, pair(h)] = scale
        ctx[:, pair(h)] = (
            (jnp.where(mine, outs[h][:, :128], outs[h + 1][:, :128]) * scale).astype(BF16).astype(F32)
        )


def prompt_fwd_kernel(q, k, v, prev, logits, weights, ctx, inv, kt, vx):
    @pl.when(pl.program_id(0) == 0)
    def _():
        fill(k, v, kt, vx)

    def soft(h, s, _):
        x = s + prev[h].astype(F32)
        logits[h] = x.astype(BF16)
        e = jnp.exp(x - jnp.max(x, axis=-1, keepdims=True)).astype(BF16)
        weights[h] = e
        return e, []

    attend(q[...], kt, vx, soft, ctx, inv, 0)


def prompt_forward(q, k, v, prev, after=()):
    heads = prev.shape[0]
    width = heads * HEAD
    rows = 256
    big = pl.BlockSpec((heads, rows, PROMPT), lambda r: (0, r, 0))
    row = pl.BlockSpec((rows, width), lambda r: (r, 0))
    front = pl.BlockSpec((PROMPT, width), lambda r: (0, 0))
    shape = jax.ShapeDtypeStruct((heads, PROMPT, PROMPT), BF16)
    n = heads * PROMPT * PROMPT
    return run(
        prompt_fwd_kernel,
        (q, k, v, prev),
        [row, front, front, big],
        [big, big, row, row],
        [shape, shape] + [jax.ShapeDtypeStruct((PROMPT, width), F32)] * 2,
        (PROMPT // rows,),
        "attn_prompt_fwd",
        cost(4 * n * HEAD, 6 * n, n),
        scratch=[pltpu.VMEM((width, PROMPT), BF16), pltpu.VMEM((heads // 2, PROMPT, 256), BF16)],
        after=after,
    )


def cont_fwd_kernel(c0, lens, q, kp, vp, ko, vo, prev, *refs):
    logits, weights, ctx, inv, kt, vx = refs[-6:]

    @pl.when(pl.program_id(0) == 0)
    def _():
        fill(kp, vp, kt, vx)

    kt[:, PROMPT:] = ko[...].T
    for p in range(ko.shape[1] // 128):
        vx[p, PROMPT:, :128] = vo[:, p * 128 : (p + 1) * 128]
    column = lax.broadcasted_iota(jnp.int32, (CONT_LEN, CONT_LEN), 1)
    first = c0 + pl.program_id(0) * GROUP
    live = [column < lens[0, first + g] for g in range(GROUP)]

    def soft(h, s1, s2):
        front, own = [], []
        for g, r in enumerate(parts(GROUP)):
            a = s1[r] + prev[g, h, :, :PROMPT].astype(F32)
            b = s2[g] + prev[g, h, :, PROMPT:].astype(F32)
            logits[g, h, :, :PROMPT] = a.astype(BF16)
            logits[g, h, :, PROMPT:] = b.astype(BF16)
            b = jnp.where(live[g], b, NEG_FILL)
            top = jnp.maximum(
                jnp.max(a, axis=-1, keepdims=True), jnp.max(b, axis=-1, keepdims=True)
            )
            front.append(jnp.exp(a - top).astype(BF16))
            own.append(jnp.exp(b - top).astype(BF16))
            weights[g, h, :, :PROMPT] = front[g]
            weights[g, h, :, PROMPT:] = own[g]
        return jnp.concatenate(front, axis=0), own

    attend(q[...], kt, vx, soft, ctx, inv, GROUP)


def cont_forward(c0, n, lens, q, k, v, prev, earlier=(), after=()):
    heads = prev.shape[1]
    width = heads * HEAD
    rows = GROUP * CONT_LEN
    first, at = (PROMPT // CONT_LEN + c0) // GROUP, c0 // GROUP
    own = pl.BlockSpec((rows, width), lambda c, *_: (c + first, 0))
    front = pl.BlockSpec((PROMPT, width), lambda c, *_: (0, 0))
    big = pl.BlockSpec((GROUP, heads, CONT_LEN, KEYS), lambda c, *_: (c + at, 0, 0, 0))
    row = pl.BlockSpec((rows, width), lambda c, *_: (c, 0))
    shape = jax.ShapeDtypeStruct((CONT, heads, CONT_LEN, KEYS), BF16)
    size = n * heads * CONT_LEN * KEYS
    return run(
        functools.partial(cont_fwd_kernel, c0),
        (lens, q, k, v, k, v, prev, *earlier),
        [own, front, front, own, own, big] + [ANY] * len(earlier),
        [big, big, row, row],
        [shape, shape] + [jax.ShapeDtypeStruct((n * CONT_LEN, width), F32)] * 2,
        (n // GROUP,),
        "attn_cont_fwd",
        cost(4 * size * HEAD, 6 * size, size),
        cap=CONT_CAP,
        scalars=1,
        scratch=[
            pltpu.VMEM((width, PROMPT + rows), BF16),
            pltpu.VMEM((heads // 2, PROMPT + rows, 256), BF16),
        ],
        aliases={7 + m: m for m in range(len(earlier))},
        after=after,
    )


def hop(x, bit):
    n = lax.axis_size("dp")
    return lax.ppermute(x, "dp", [(i, i ^ (1 << bit)) for i in range(n)])


def turn(x, step):
    n = lax.axis_size("dp")
    return lax.ppermute(x, "dp", [(i, i ^ (4 if (i & 1) ^ step else 2)) for i in range(n)])


def grad_back_kernel(flip, place, act, gffn, out):
    acc = tn(act[...], gffn[...])
    low = place[2] if flip else place[1]
    for m in range(2):
        out[pl.ds(jnp.bitwise_xor(low % 2, m), 1)] = acc[None, 192 * m : 192 * m + 192]


def grad_back(flip, place, act, gffn, after=()):
    low = lambda place: (place[2] if flip else place[1]) // 2 % 2
    return run(
        functools.partial(grad_back_kernel, flip),
        (place, act, gffn),
        [
            pl.BlockSpec((SLOTS, 384), lambda i, place: (0, 2 * ((place[1] // 4 + flip) % 2) + i)),
            whole((SLOTS, D)),
        ],
        pl.BlockSpec((2, 192, D), lambda i, place: (jnp.bitwise_xor(i, low(place)), 0, 0)),
        jax.ShapeDtypeStruct((4, 192, D), F32),
        (2,),
        "grad_w_back",
        cost(2 * SLOTS * 768 * D, 2 * SLOTS * 768 * 2 + 4 * 768 * D),
        cap=BACK_CAP,
        scalars=1,
        after=after,
    )


IN_BLOCK = 512


def grad_in_kernel(n, place, x, ghid, send, keep, xt):
    i = pl.program_id(0)

    @pl.when(i % n == 0)
    def _():
        xt[...] = x[...].T

    acc = nn(xt[...], ghid[...])

    def put(out, low):
        for m in range(4):
            out[pl.ds(jnp.bitwise_xor(low, m), 1)] = acc[None, 96 * m : 96 * m + 96]

    pl.when(i < n)(lambda: put(send, place[2]))
    pl.when(i >= n)(lambda: put(keep, place[1] % 4))


def grad_in(place, xlow, ghid, after=()):
    units = ghid.shape[1]
    n = units // IN_BLOCK
    shape = jax.ShapeDtypeStruct((4, 96, units), F32)
    return run(
        functools.partial(grad_in_kernel, n),
        (place, xlow, ghid),
        [
            pl.BlockSpec((SLOTS, 384), lambda i, place: (0, (place[1] // 4 + 1 - i // n) % 2)),
            pl.BlockSpec((SLOTS, IN_BLOCK), lambda i, *_: (0, i % n)),
        ],
        [
            pl.BlockSpec((4, 96, IN_BLOCK), lambda i, *_: (0, 0, jnp.minimum(i, n - 1))),
            pl.BlockSpec((4, 96, IN_BLOCK), lambda i, *_: (0, 0, jnp.maximum(i - n, 0))),
        ],
        [shape] * 2,
        (2 * n,),
        "grad_w_in",
        cost(4 * SLOTS * 384 * units, 2 * SLOTS * (768 + 2 * units) + 8 * 384 * units),
        scalars=1,
        scratch=[pltpu.VMEM((384, SLOTS), BF16)],
        after=after,
    )


def grad_rest_kernel(place, tok, gq, gk, gv, ctx_p, ctx_a, ctx_b, gattn, stats, other, *refs):
    send, keep, ao = refs
    i = pl.program_id(0)
    left = (place[1] // 4 + 1 - i) % 2 == 0

    @pl.when(i == 0)
    def _():
        ctx = jnp.concatenate([ctx_p[...], ctx_a[...], ctx_b[...]], axis=0).astype(BF16)
        ao[...] = nn(ctx.T, gattn[...])

    tok_t = tok[...].T
    aq = nn(tok_t, gq[...])
    ak = nn(tok_t, gk[...])
    av = nn(tok_t, gv[...])
    o = jnp.where(left, ao[:192], ao[192:])
    bias = jnp.concatenate(
        [jnp.sum(g[...].astype(F32), axis=0, keepdims=True) for g in (gq, gv)], axis=1
    )
    row = lax.broadcasted_iota(jnp.int32, (16, D), 0)
    half_of = lax.broadcasted_iota(jnp.int32, (16, D), 1) // (D // 2)
    small = jnp.where((half_of == place[0]) | (row >= 7), stats[...], other[...])
    small = jnp.where(row == 9, bias, small)

    def put(out, low):
        for m in range(4):
            j = jnp.bitwise_xor(low, m)
            out[pl.ds(j, 1), 0:96, 0:384] = aq[None, 96 * m : 96 * m + 96]
            out[pl.ds(j, 1), 0:96, 384:768] = ak[None, 96 * m : 96 * m + 96]
            out[pl.ds(j, 1), 96:144, 0:384] = av[None, 96 * m : 96 * m + 48]
            out[pl.ds(j, 1), 96:144, 384:768] = av[None, 96 * m + 48 : 96 * m + 96]
            out[pl.ds(j, 1), 144:192, :] = o[None, 48 * m : 48 * m + 48]
            out[pl.ds(j, 1), 192:200, :] = jnp.concatenate(
                [
                    jnp.where(left, small[2 * m : 2 * m + 2], small[8 + 2 * m : 10 + 2 * m]),
                    jnp.zeros((6, D), F32),
                ],
                axis=0,
            )[None]

    pl.when(i == 0)(lambda: put(send, place[2]))
    pl.when(i == 1)(lambda: put(keep, place[1] % 4))


def grad_rest(place, tokens, gq, gk, gv, ctx_p, ctx_a, ctx_b, gattn, stats, other, after=()):
    width = gq.shape[1]
    shape = jax.ShapeDtypeStruct((4, 200, D), F32)
    fixed = (gq, gk, gv, ctx_p, ctx_a, ctx_b, gattn, stats, other)
    return run(
        grad_rest_kernel,
        (place, tokens) + fixed,
        [pl.BlockSpec((SLOTS, 384), lambda i, place: (0, (place[1] // 4 + 1 - i) % 2))]
        + [const(x) for x in fixed],
        [const(shape)] * 2,
        [shape] * 2,
        (2,),
        "grad_w_rest",
        cost(2 * SLOTS * (D * 3 * width + width * D), 2 * SLOTS * (6 * width + 2 * D)),
        scalars=1,
        scratch=[pltpu.VMEM((width, D), F32)],
        after=after,
    )


def chunk_of(place, far, m):
    if far:
        return (1 - place[1] // 4) * 4 + jnp.bitwise_xor(place[2], m)
    return jnp.bitwise_xor(place[1], m)


def staged(moves):
    for first, _ in moves:
        first.start()
    for first, rest in moves:
        first.wait()
        for c in rest:
            c.start()
    for _, rest in moves:
        for c in rest:
            c.wait()


def order_kernel(rows, far, place, src, *refs):
    out, hold, sems_in, sems_out = refs[-4:]
    moves = []
    for m in range(4):
        at = pl.multiple_of(chunk_of(place, far, m) * rows, 8)
        moves.append(
            (
                pltpu.make_async_copy(src.at[m], hold.at[m], sems_in.at[m]),
                [pltpu.make_async_copy(hold.at[m], out.at[pl.ds(at, rows)], sems_out.at[m])],
            )
        )
    staged(moves)


def in_order(far, place, chunks, prev=None, after=()):
    _, rows, cols = chunks.shape
    return run(
        functools.partial(order_kernel, rows, far),
        (place, chunks) + (() if prev is None else (prev,)),
        [ANY] * (1 if prev is None else 2),
        ANY,
        jax.ShapeDtypeStruct((8 * rows, cols), F32),
        (1,),
        "in_order",
        cost(0, 8 * chunks.size),
        scalars=1,
        scratch=[pltpu.VMEM(chunks.shape, F32), pltpu.SemaphoreType.DMA((4,)), pltpu.SemaphoreType.DMA((4,))],
        aliases={} if prev is None else {2: 0},
        after=after,
    )


def order_rest_kernel(far, first, width, place, src, *refs):
    gw, go, small, hold, sems_in, sems_out = refs[-6:]
    moves, n = [], 0

    def copy(a, b):
        nonlocal n
        n += 1
        return pltpu.make_async_copy(a, b, sems_out.at[n - 1])

    left, right = pl.ds(0, width), pl.ds(width, width)
    for m in range(2):
        c = chunk_of(place, far, first + m)
        rows = hold.at[m]
        wide = pl.ds(pl.multiple_of(c * 96, 8), 96)
        out = [
            copy(rows.at[pl.ds(0, 96), left], gw.at[0, wide]),
            copy(rows.at[pl.ds(0, 96), right], gw.at[1, wide]),
            copy(rows.at[pl.ds(96, 48), left], gw.at[2, pl.ds(pl.multiple_of(c * 96, 8), 48)]),
            copy(rows.at[pl.ds(96, 48), right], gw.at[2, pl.ds(pl.multiple_of(c * 96 + 48, 8), 48)]),
            copy(rows.at[pl.ds(144, 48)], go.at[pl.ds(pl.multiple_of(c * 48, 8), 48)]),
            copy(rows.at[pl.ds(192, 8)], small.at[pl.ds(pl.multiple_of(c * 8, 8), 8)]),
        ]
        moves.append((pltpu.make_async_copy(src.at[m], rows, sems_in.at[m]), out))
    staged(moves)


def order_rest(far, first, place, chunks, width, prev=None, after=()):
    return run(
        functools.partial(order_rest_kernel, far, first, width),
        (place, chunks) + (() if prev is None else tuple(prev)),
        [ANY] * (1 if prev is None else 4),
        [ANY] * 3,
        [
            jax.ShapeDtypeStruct((3, D, width), F32),
            jax.ShapeDtypeStruct((width, D), F32),
            jax.ShapeDtypeStruct((64, D), F32),
        ],
        (1,),
        "order_rest",
        cost(0, 8 * chunks.size),
        scalars=1,
        scratch=[
            pltpu.VMEM(chunks.shape, F32),
            pltpu.SemaphoreType.DMA((2,)),
            pltpu.SemaphoreType.DMA((12,)),
        ],
        aliases={} if prev is None else {2: 0, 3: 1, 4: 2},
        after=after,
    )


def small_kernel(count, rows, bias, gain, shift, b_in, qv, loss):
    row = lambda n: rows[8 * (n // 2) + n % 2 : 8 * (n // 2) + n % 2 + 1]
    bias[0:1], bias[1:2] = row(4), row(1)
    gain[0:1], gain[1:2] = row(5), row(2)
    shift[0:1], shift[1:2] = row(6), row(3)
    b_in[0:1, :D], b_in[0:1, D:] = row(7), row(8)
    qv[0:1], qv[1:2] = row(9)[:, : D // 2], row(9)[:, D // 2 :]
    loss[...] = jnp.sum(row(0), axis=1, keepdims=True) / count


def small_outputs(count, rows):
    shapes = [(2, D)] * 3 + [(1, 2 * D), (2, D // 2), (1, 1)]
    return run(
        functools.partial(small_kernel, count),
        (rows,),
        [whole(rows.shape)],
        [whole(x) for x in shapes],
        [jax.ShapeDtypeStruct(x, F32) for x in shapes],
        (1,),
        "small_outputs",
        cost(0, 8 * rows.size),
    )


def lay_out(place, pieces, wi, wo, wb, b, stage_a, stage_b, sems):
    moves = []
    for far in range(2):
        own_a, rest_a = pieces[2 * far : 2 * far + 2]
        most_b, cross_b = pieces[4 + 2 * far : 6 + 2 * far]
        for m in range(4):
            k = 4 * far + m
            src_a = own_a if m == 0 else rest_a.at[pl.ds((m - 1) * 128, 128)]
            src_b = cross_b if m == 3 else most_b.at[pl.ds(m * 192, 192)]
            moves.append(pltpu.make_async_copy(src_a, stage_a.at[k], sems.at[k]))
            moves.append(pltpu.make_async_copy(src_b, stage_b.at[k], sems.at[8 + k]))
    for copy in moves:
        copy.start()
    for k in range(8):
        c = jnp.bitwise_xor(place[3], k)
        moves[2 * k].wait()
        wi[pl.ds(pl.multiple_of(c * 96, 16), 96), :] = stage_a[k, 0:96, :].astype(BF16)
        tail = stage_a[k, 96:120, :]
        wo[pl.ds(pl.multiple_of(c * 48, 16), 48), :] = jnp.concatenate(
            [tail[:, :D], tail[:, D:]], axis=0
        ).astype(BF16)
        moves[2 * k + 1].wait()
        wb[pl.ds(pl.multiple_of(c * 192, 16), 192), :] = stage_b[k].astype(BF16)
    b[...] = stage_a[0, 120:128, :]


def forward_kernel(first_block, count, has_prev, *refs):
    lens, place = refs[:2]
    if has_prev:
        ctx_own, ctx_oth, tok, teach, wo_own, wi_own, wb_own, b_own, bias_out, gain, shift = refs[2:13]
        wo_oth, wi_oth, wb_oth, b_oth = refs[13:17]
        out, act, gate, gffn, gsec, xlow, rstd, stats = refs[-8:]
        own, oth = ctx_own[...], ctx_oth[...]
    else:
        ctx_p, ctx_a, oth_p, oth_a, tok, teach, wo_own, wi_own, wb_own, b_own, bias_out, gain, shift = refs[2:15]
        pieces = refs[15:23]
        out, act, gate, gffn, gsec, xlow, rstd, stats, wo_oth, wi_oth, wb_oth, b_oth = refs[-15:-3]
        early = pl.program_id(0) < PROMPT // ROWS
        own = jnp.where(early, ctx_p[...], ctx_a[...])
        oth = jnp.where(early, oth_p[...], oth_a[...])

        @pl.when(pl.program_id(0) == 0)
        def _():
            lay_out(place, pieces, wi_oth, wo_oth, wb_oth, b_oth, *refs[-3:])

    i = pl.program_id(0)
    blk = i + first_block
    n_own = wi_own.shape[1] // UNITS

    @pl.when(i == 0)
    def _():
        stats[...] = jnp.zeros_like(stats)

    attn = nn(own.astype(BF16), wo_own[...]) + nn(oth.astype(BF16), wo_oth[...])
    fin = tok[...].astype(F32) + attn + bias_out[0:1]
    c1 = fin - jnp.mean(fin, axis=-1, keepdims=True)
    r1 = lax.rsqrt(jnp.mean(c1 * c1, axis=-1, keepdims=True) + EPS_NORM)
    rstd[...] = jnp.broadcast_to(r1, rstd.shape)
    first = c1 * r1 * gain[0:1] + shift[0:1]
    x = first.astype(BF16)
    xlow[...] = x
    ffn = None
    for side in range(2):
        wi, wb, bb = ((wi_own, wb_own, b_own), (wi_oth, wb_oth, b_oth))[side]
        for u in range(n_own):
            cols = slice(u * UNITS, (u + 1) * UNITS)
            h = nn(x, wi[:, cols]) + bb[0:1, cols]
            cdf = 0.5 + 0.5 * lax.erf(h * 0.7071067811865476)
            pdf = jnp.exp(-0.5 * h * h) * 0.3989422804014327
            a = (h * cdf).astype(BF16)
            at = (side * n_own + u) * UNITS
            gate[:, at : at + UNITS] = (cdf + h * pdf).astype(BF16)
            if side == 0:
                act[:, cols] = a
            part = nn(a, wb[cols, :])
            ffn = part if ffn is None else ffn + part
    sec = first + ffn + bias_out[1:2]
    c2 = sec - jnp.mean(sec, axis=-1, keepdims=True)
    r2 = lax.rsqrt(jnp.mean(c2 * c2, axis=-1, keepdims=True) + EPS_NORM)
    xh2 = c2 * r2
    result = xh2 * gain[1:2] + shift[1:2]
    left = place[0] == 0
    hd = D // 2
    out[...] = jnp.where(left, result[:, :hd], result[:, hd:]).astype(BF16)
    row = lax.broadcasted_iota(jnp.int32, (ROWS, 1), 0)
    per = ROWS // CONT_LEN
    cont0 = (blk - PROMPT // ROWS) * per
    valid = jnp.zeros((ROWS, 1), jnp.bool_)
    for m in range(per):
        length = jnp.where(cont0 < 0, CONT_LEN, lens[0, jnp.maximum(cont0 + m, 0)])
        valid = valid | ((row >= m * CONT_LEN) & (row < m * CONT_LEN + length))
    diff = jnp.where(valid, result - teach[...].astype(F32), 0.0)
    g = diff * (2.0 / count)
    gy = g * gain[1:2]
    g2 = r2 * (
        gy
        - jnp.mean(gy, axis=-1, keepdims=True)
        - xh2 * jnp.mean(gy * xh2, axis=-1, keepdims=True)
    )
    stats[0:1] += jnp.sum(diff * diff, axis=0, keepdims=True)
    stats[1:2] += jnp.sum(g2, axis=0, keepdims=True)
    stats[2:3] += jnp.sum(g * xh2, axis=0, keepdims=True)
    stats[3:4] += jnp.sum(g, axis=0, keepdims=True)
    gsec[...] = g2
    gffn[...] = g2.astype(BF16)


def rows_forward(first_block, blocks, count, lens, place, ctxs, tok, teach, fixed, more, prev=None, after=()):
    width = ctxs[0].shape[1]
    units = fixed[1].shape[1]
    row = lambda w: pl.BlockSpec((ROWS, w), lambda i, *_: (i + first_block, 0))
    split = PROMPT // ROWS
    if prev is None:
        low = pl.BlockSpec((ROWS, width), lambda i, *_: (jnp.minimum(i, split - 1), 0))
        high = pl.BlockSpec((ROWS, width), lambda i, *_: (jnp.maximum(i - split, 0), 0))
        ctx_specs = [low, high, low, high]
    else:
        ctx_specs = [pl.BlockSpec((ROWS, width), lambda i, *_: (i, 0))] * 2
    shapes = [(D // 2, BF16), (units, BF16), (2 * units, BF16), (D, BF16), (D, F32), (D, BF16), (128, F32)]
    operands = [lens, place, *ctxs, tok, teach, *fixed, *more]
    specs = ctx_specs + [row(D), row(D)] + [const(a) for a in fixed]
    specs += [IN_HBM if prev is None else const(a) for a in more]
    aliases, scratch = {}, []
    out_specs = [row(w) for w, _ in shapes] + [whole((16, D))]
    out_shape = [jax.ShapeDtypeStruct((SLOTS, w), t) for w, t in shapes] + [jax.ShapeDtypeStruct((16, D), F32)]
    if prev is None:
        weights = [
            jax.ShapeDtypeStruct((width, D), BF16),
            jax.ShapeDtypeStruct((D, units), BF16),
            jax.ShapeDtypeStruct((units, D), BF16),
            jax.ShapeDtypeStruct((8, units), F32),
        ]
        out_specs, out_shape = out_specs + [const(w) for w in weights], out_shape + weights
        scratch = [
            pltpu.VMEM((8, 128, units), F32),
            pltpu.VMEM((8, 192, D), F32),
            pltpu.SemaphoreType.DMA((16,)),
        ]
    else:
        aliases = {len(operands) + n: n for n in range(7)}
        operands, specs = operands + list(prev), specs + [ANY] * 7
    return run(
        functools.partial(forward_kernel, first_block, count, prev is not None),
        operands,
        specs,
        out_specs,
        out_shape,
        (blocks,),
        "rows_forward",
        cap=ROWS_CAP,
        scratch=scratch,
        estimate=cost(2 * blocks * ROWS * D * (4 * units + 2 * width), 8 * D * units + blocks * ROWS * 24000),
        scalars=2,
        aliases=aliases,
        after=after,
    )


def backward_kernel(place, gate, gffn, gsec, xlow, rstd, wo, wi_own, wi_oth, wb_own, wb_oth, gain, shift,
                    stats_f, *refs):
    ghid, gattn, gctx, gfin, stats, gbin = refs[-6:]
    i = pl.program_id(0)
    n_own = wi_own.shape[1] // UNITS

    @pl.when(i == 0)
    def _():
        stats[...] = stats_f[...]
        gbin[0:1, :D] = stats_f[7:8]
        gbin[0:1, D:] = stats_f[8:9]

    gf = gffn[...]
    gfirst = gsec[...]
    for side in range(2):
        wi, wb = ((wi_own, wb_own), (wi_oth, wb_oth))[side]
        for u in range(n_own):
            cols = slice(u * UNITS, (u + 1) * UNITS)
            at = (side * n_own + u) * UNITS
            gh = (nt(gf, wb[cols, :]) * gate[:, at : at + UNITS].astype(F32)).astype(BF16)
            if side == 0:
                ghid[:, cols] = gh
                gbin[0:1, cols] += jnp.sum(gh.astype(F32), axis=0, keepdims=True)
            gfirst = gfirst + nt(gh, wi[:, cols])
    xh1 = (xlow[...].astype(F32) - shift[0:1]) * (1.0 / gain[0:1])
    gy1 = gfirst * gain[0:1]
    g1 = rstd[:, 0:1] * (
        gy1
        - jnp.mean(gy1, axis=-1, keepdims=True)
        - xh1 * jnp.mean(gy1 * xh1, axis=-1, keepdims=True)
    )
    stats[4:5] += jnp.sum(g1, axis=0, keepdims=True)
    stats[5:6] += jnp.sum(gfirst * xh1, axis=0, keepdims=True)
    stats[6:7] += jnp.sum(gfirst, axis=0, keepdims=True)

    @pl.when(i == pl.num_programs(0) - 1)
    def _():
        stats[7:8] = gbin[0:1, :D]
        stats[8:9] = gbin[0:1, D:]

    hd = D // 2
    gfin[...] = jnp.where(place[0] == 0, g1[:, :hd], g1[:, hd:])
    ga1 = g1.astype(BF16)
    gattn[...] = ga1
    gctx[...] = nt(ga1, wo[...]).astype(BF16)


def rows_backward(first, blocks, place, gate, gffn, gsec, xlow, rstd, fixed, prev=None, after=()):
    wo, wi_own = fixed[:2]
    width, units = wo.shape[0], wi_own.shape[1]
    row = lambda w: pl.BlockSpec((ROWS, w), lambda i, *_: (i + first, 0))
    shapes = [(units, BF16), (D, BF16), (width, BF16), (D // 2, F32)]
    operands = [place, gate, gffn, gsec, xlow, rstd] + list(fixed)
    specs = [row(2 * units), row(D), row(D), row(D), row(128)] + [const(a) for a in fixed]
    aliases = {}
    if prev is not None:
        aliases = {len(operands) + n: n for n in range(4)}
        operands, specs = operands + list(prev), specs + [ANY] * 4
    return run(
        backward_kernel,
        operands,
        specs,
        [row(w) for w, _ in shapes] + [whole((16, D))],
        [jax.ShapeDtypeStruct((SLOTS, w), t) for w, t in shapes] + [jax.ShapeDtypeStruct((16, D), F32)],
        (blocks,),
        "rows_backward",
        cost(2 * SLOTS * D * (4 * units + width), 8 * D * units + SLOTS * 20000),
        scalars=1,
        scratch=[pltpu.VMEM((8, units), F32)],
        aliases=aliases,
        after=after,
    )


def attend_back(q, gctx, ctx, inv, load, vt, kall, gq, take, groups):
    heads = q.shape[1] // HEAD
    g2, inner, qt, gt = [], [], [], []
    for p in range(heads // 2):
        cols = pair(2 * p)
        g = (gctx[:, cols].astype(F32) * inv[:, cols]).astype(BF16)
        prod = g.astype(F32) * ctx[:, cols]
        g2.append(g)
        qt.append(q[:, cols].T)
        gt.append(g.T)
        inner += [jnp.sum(only(prod, h), axis=-1, keepdims=True) for h in range(2)]

    def weigh(h):
        gm = only(g2[h // 2], h % 2)
        return nn(gm, vt[pair(h), :PROMPT]), [
            nn(gm[r], vt[pair(h), c]) for r, c in zip(parts(groups), own_keys(groups))
        ]

    def finish(h, e, l):
        part = slice(h % 2 * HEAD, (h % 2 + 1) * HEAD)
        q_h, g_h = qt[h // 2][part], gt[h // 2][part]
        dq = nn(l[0], kall[:PROMPT, pair(h)])
        own = []
        if groups:
            dq = dq + jnp.concatenate(
                [nn(x, kall[c, pair(h)]) for x, c in zip(l[1], own_keys(groups))], axis=0
            )
            own = [
                (nn(q_h[:, r], x), nn(g_h[:, r], y))
                for r, x, y in zip(parts(groups), l[1], e[1])
            ]
        return dq, (nn(q_h, l[0]), nn(g_h, e[0])), own

    mine = half_mask(q.shape[0], 0)
    done = []

    def flush(h):
        done.append(finish(h, *held[h]))
        if h % 2:
            a, b = done[h - 1], done[h]
            gq[:, pair(h)] = (jnp.where(mine, a[0], b[0]) * 0.125).astype(BF16)
            both = lambda x, y: tuple(jnp.concatenate(z, axis=0) for z in zip(x, y))
            take(pair(h), both(a[1], b[1]), [both(x, y) for x, y in zip(a[2], b[2])])

    raw, held = [weigh(0)], []
    for h in range(heads):
        if h + 1 < heads:
            raw.append(weigh(h + 1))
        e = load(h)
        l = [(e[0].astype(F32) * (raw[h][0] - inner[h])).astype(BF16)]
        l.append(
            [
                (y.astype(F32) * (x - inner[h][r])).astype(BF16)
                for y, x, r in zip(e[1], raw[h][1], parts(groups))
            ]
        )
        held.append((e, l))
        if h:
            flush(h - 1)
    flush(heads - 1)


def cont_bwd_kernel(split, q, kp, vp, ko, vo, weights, gctx, ctx_a, inv_a, ctx_b, inv_b,
                    gq, gk, gv, gkp, gvp, vt, kall):
    early = pl.program_id(0) < split
    ctx = jnp.where(early, ctx_a[...], ctx_b[...])
    inv = jnp.where(early, inv_a[...], inv_b[...])

    @pl.when(pl.program_id(0) == 0)
    def _():
        gkp[...] = jnp.zeros_like(gkp)
        gvp[...] = jnp.zeros_like(gvp)
        vt[:, :PROMPT] = vp[...].T
        kall[:PROMPT] = kp[...]

    vt[:, PROMPT:] = vo[...].T
    kall[PROMPT:] = ko[...]

    def load(h):
        return (
            jnp.concatenate([weights[g, h, :, :PROMPT] for g in range(GROUP)], axis=0),
            [weights[g, h, :, PROMPT:] for g in range(GROUP)],
        )

    def take(cols, front, own):
        gkp[cols, :] += front[0]
        gvp[cols, :] += front[1]
        for r, (dk, dv) in zip(parts(GROUP), own):
            gk[r, cols] = dk.T.astype(BF16)
            gv[r, cols] = dv.T.astype(BF16)

    attend_back(q[...], gctx[...], ctx, inv, load, vt, kall, gq, take, GROUP)


def cont_backward(q, k, v, weights, gctx, ctx_a, inv_a, ctx_b, inv_b, after=()):
    heads = weights.shape[1]
    width = heads * HEAD
    rows = GROUP * CONT_LEN
    first = PROMPT // rows
    own = pl.BlockSpec((rows, width), lambda c: (c + first, 0))
    front = pl.BlockSpec((PROMPT, width), lambda c: (0, 0))
    big = pl.BlockSpec((GROUP, heads, CONT_LEN, KEYS), lambda c: (c, 0, 0, 0))
    shape = jax.ShapeDtypeStruct((SLOTS, width), BF16)
    sums = jax.ShapeDtypeStruct((width, PROMPT), F32)
    n = CONT * heads * CONT_LEN * KEYS
    split = ctx_a.shape[0] // rows
    head = pl.BlockSpec((rows, width), lambda c: (jnp.minimum(c, split - 1), 0))
    tail = pl.BlockSpec((rows, width), lambda c: (jnp.maximum(c - split, 0), 0))
    return run(
        functools.partial(cont_bwd_kernel, split),
        (q, k, v, k, v, weights, gctx, ctx_a, inv_a, ctx_b, inv_b),
        [own, front, front, own, own, big, own, head, head, tail, tail],
        [own, own, own, whole((width, PROMPT)), whole((width, PROMPT))],
        [shape, shape, shape, sums, sums],
        (CONT // GROUP,),
        "attn_cont_bwd",
        cost(8 * n * HEAD, 2 * n + 8 * SLOTS * heads * HEAD * 2),
        scratch=[pltpu.VMEM((width, PROMPT + rows), BF16), pltpu.VMEM((PROMPT + rows, width), BF16)],
        after=after,
    )


def prompt_bwd_kernel(q, k, v, weights, gctx, ctx, inv, gkp, gvp, a, b, c, gq, gk, gv, vt, ak, av):
    r = pl.program_id(0)

    @pl.when(r == 0)
    def _():
        vt[...] = v[...].T
        ak[...] = gkp[...]
        av[...] = gvp[...]

    def take(cols, front, own):
        ak[cols, :] += front[0]
        av[cols, :] += front[1]

    attend_back(q[...], gctx[...], ctx[...], inv[...], lambda h: (weights[h], []), vt, k, gq, take, 0)

    @pl.when(r == pl.num_programs(0) - 1)
    def _():
        gk[...] = ak[...].T.astype(BF16)
        gv[...] = av[...].T.astype(BF16)


def prompt_backward(q, k, v, weights, gctx, ctx, inv, gkp, gvp, gq, gk, gv, after=()):
    heads = weights.shape[0]
    width = heads * HEAD
    rows = 256
    row = pl.BlockSpec((rows, width), lambda r: (r, 0))
    front = pl.BlockSpec((PROMPT, width), lambda r: (0, 0))
    acc = whole((width, PROMPT))
    shape = jax.ShapeDtypeStruct((SLOTS, width), BF16)
    n = heads * PROMPT * PROMPT
    return run(
        prompt_bwd_kernel,
        (q, k, v, weights, gctx, ctx, inv, gkp, gvp, gq, gk, gv),
        [row, front, front, pl.BlockSpec((heads, rows, PROMPT), lambda r: (0, r, 0)), row, row, row, acc, acc]
        + [ANY] * 3,
        [row, front, front],
        [shape] * 3,
        (PROMPT // rows,),
        "attn_prompt_bwd",
        cost(8 * n * HEAD, 2 * n + 8 * PROMPT * heads * HEAD * 2),
        scratch=[
            pltpu.VMEM((width, PROMPT), BF16),
            pltpu.VMEM((width, PROMPT), F32),
            pltpu.VMEM((width, PROMPT), F32),
        ],
        aliases={9: 0, 10: 1, 11: 2},
        after=after,
    )


def input_grad_kernel(place, gq, gk, gv, w, base, *refs):
    sends, keep = refs[:-1], refs[-1]
    hd = D // 2
    mine = place[0] == 0
    part = nt(gq[...], w[0]) + nt(gk[...], w[1]) + nt(gv[...], w[2])
    keep[...] = base[...] + jnp.where(mine, part[:, :hd], part[:, hd:])
    away = jnp.where(mine, part[:, hd:], part[:, :hd])

    def put(send):
        send[...] = away

    per = SLOTS // part.shape[0] // len(sends)
    for n, send in enumerate(sends):
        pl.when(pl.program_id(0) // per == n)(functools.partial(put, send))


def input_grad(place, gq, gk, gv, w3, base, after=()):
    width = w3.shape[2]
    rows, cuts = 384, 4
    per = SLOTS // rows // cuts
    row = lambda w: pl.BlockSpec((rows, w), lambda i, *_: (i, 0))
    cut = lambda n: pl.BlockSpec((rows, D // 2), lambda i, *_: (jnp.clip(i - n * per, 0, per - 1), 0))
    return run(
        input_grad_kernel,
        (place, gq, gk, gv, w3, base),
        [row(width)] * 3 + [whole((3, D, width)), row(D // 2)],
        [cut(n) for n in range(cuts)] + [row(D // 2)],
        [jax.ShapeDtypeStruct((SLOTS // cuts, D // 2), F32)] * cuts + [jax.ShapeDtypeStruct((SLOTS, D // 2), F32)],
        (SLOTS // rows,),
        "input_grad",
        cost(2 * SLOTS * D * 3 * width, 2 * (SLOTS * 3 * width) + 6 * SLOTS * D),
        scalars=1,
        after=after,
    )


def swap(x):
    n = lax.axis_size("tensor")
    return lax.ppermute(x, "tensor", [(i, n - 1 - i) for i in range(n)])


def tie(*values):
    return lax.optimization_barrier(values)


def far_exchange(total):
    bit = 4
    while (1 << bit) < lax.axis_size("dp"):
        total = total + hop(total, bit)
        bit += 1
    return total


def local(
    tokens, teacher, lengths, prev_prompt, prev_cont, w_qkv, bias_qv, w_out, w_in, b_in, w_back,
    bias_out, norm_gain, norm_bias,
):
    width = w_qkv.shape[2]
    units = w_in.shape[1]
    w3 = jnp.transpose(w_qkv, (1, 0, 2))
    t = lax.axis_index("tensor").astype(jnp.int32)
    i = lax.axis_index("dp").astype(jnp.int32)
    core, x, z = i % 2, (i // 2) % 2, (i // 4) % 2
    x_first, z_first = 2 * x + z, 2 * z + x
    chunk = core * 4 + x_first
    place = jnp.stack(
        [
            t,
            core * 4 + jnp.where(core == 0, x_first, z_first),
            jnp.where(core == 0, z_first, x_first),
            chunk,
        ]
    )
    count = float(lax.axis_size("dp") * (PROMPT + TOTAL))

    part_o = lax.dynamic_slice_in_dim(w_out, chunk * 48, 48, 0)
    part_i = lax.dynamic_slice_in_dim(w_in, chunk * 96, 96, 0)
    piece_a = jnp.concatenate(
        [
            part_i.astype(F32),
            jnp.concatenate([part_o[:24], part_o[24:]], axis=1).astype(F32),
            jnp.broadcast_to(b_in[None], (8, units)),
        ],
        axis=0,
    )
    piece_b = lax.dynamic_slice_in_dim(w_back, chunk * 192, 192, 0).astype(F32)
    own_a = swap(piece_a)
    own_b = swap(piece_b)
    q, k, v = project(tokens, w3, bias_qv)
    logits_p, probs_p, ctx_p, inv_p = prompt_forward(q, k, v, prev_prompt[0])
    own_a, ctx_p = tie(own_a, ctx_p)
    oth_p = swap(ctx_p)
    zs_a, xs_a, far_own_a = hop(own_a, 2), hop(own_a, 1), hop(own_a, 0)
    logits_c, probs_c, ctx_a, inv_a = cont_forward(0, EARLY, lengths, q, k, v, prev_cont[0], after=(own_a,))
    zs_a, xs_a, far_own_a, own_b, ctx_a = tie(zs_a, xs_a, far_own_a, own_b, ctx_a)
    oth_a = swap(ctx_a)
    logits_c, probs_c, ctx_b, inv_b = cont_forward(
        EARLY, CONT - EARLY, lengths, q, k, v, prev_cont[0], (logits_c, probs_c)
    )
    zs_b, xs_b = hop(own_b, 2), hop(own_b, 1)
    cross_a = turn(jnp.where(core == 0, zs_a, xs_a), 0)
    cross_a, oth_p, zs_b, xs_b, ctx_b = tie(cross_a, oth_p, zs_b, xs_b, ctx_b)
    cross_b = turn(jnp.where(core == 0, zs_b, xs_b), 0)
    rest_a = jnp.concatenate([zs_a, xs_a, cross_a], axis=0)
    most_b = jnp.concatenate([own_b, zs_b, xs_b], axis=0)
    far_rest_a, far_most_b = hop(rest_a, 0), hop(most_b, 0)
    oth_a, cross_b, far_rest_a, far_most_b, ctx_b = tie(oth_a, cross_b, far_rest_a, far_most_b, ctx_b)
    oth_b = swap(ctx_b)
    far_cross_b = hop(cross_b, 0)

    fixed = (w_out, w_in, w_back, b_in[None], bias_out, norm_gain, norm_bias)
    pieces = (
        own_a, rest_a, far_own_a, far_rest_a, most_b, cross_b, far_most_b, far_cross_b,
    )
    n_blocks = SLOTS // ROWS
    lead = (PROMPT + EARLY * CONT_LEN) // ROWS
    first = rows_forward(
        0, lead, count, lengths, place, (ctx_p, ctx_a, oth_p, oth_a), tokens, teacher, fixed, pieces
    )
    kept, stats_a, (wo_oth, wi_oth, wb_oth, b_oth) = list(first[:7]), first[7], first[8:]
    oth_b, kept[0] = tie(oth_b, kept[0])
    *kept, stats_f = rows_forward(
        lead, n_blocks - lead, count, lengths, place, (ctx_b, oth_b), tokens, teacher, fixed,
        (wo_oth, wi_oth, wb_oth, b_oth), kept,
    )
    output, act, gate, gffn, gsec, xlow, rstd = kept
    stats_f = stats_f + stats_a

    def split(keep, got, n):
        return keep[n:] + got[n:], keep[:n] + got[:n]

    w_fixed = (w_out, w_in, wi_oth, w_back, wb_oth, norm_gain, norm_bias, stats_f)
    b_send = grad_back(1, place, act, gffn)
    b_got = hop(b_send, 0)
    b_keep = grad_back(0, place, act, gffn, after=(b_send,))
    b_got, b_keep = tie(b_got, b_keep)
    b_out, b_keep = split(b_keep, b_got, 2)
    b_got = turn(b_out, 0)
    ghid, gattn, gctx, gfin_half, stats = rows_backward(
        0, n_blocks, place, gate, gffn, gsec, xlow, rstd, w_fixed, after=(b_out, b_keep)
    )
    b_got, ghid = tie(b_got, ghid)
    b_out, b_keep = split(b_keep, b_got, 1)
    b_got = turn(b_out, 1)
    other_stats = swap(stats)
    i_send, i_keep = grad_in(place, xlow, ghid, after=(b_out, b_keep))
    b_got, other_stats, i_send = tie(b_got, other_stats, i_send)
    b_top, b_end = b_keep[:, :96] + b_got[:, :96], b_keep[:, 96:] + b_got[:, 96:]
    b_got = hop(b_top, 3)
    i_got = hop(i_send, 0)
    gq, gk, gv, gkp, gvp = cont_backward(
        q, k, v, probs_c, gctx, ctx_a, inv_a, ctx_b, inv_b, after=(b_top, b_end)
    )
    i_got, b_got, gq = tie(i_got, b_got, gq)
    i_out, i_keep = split(i_keep, i_got, 2)
    i_got = turn(i_out, 0)
    b_more = hop(b_end, 3)
    gq, gk, gv = prompt_backward(
        q, k, v, probs_p, gctx, ctx_p, inv_p, gkp, gvp, gq, gk, gv, after=(i_out, i_keep)
    )
    r_send, r_keep = grad_rest(place, tokens, gq, gk, gv, ctx_p, ctx_a, ctx_b, gattn, stats, other_stats)
    i_got, b_more, r_send = tie(i_got, b_more, r_send)
    r_got = hop(r_send, 0)
    i_out, i_keep = split(i_keep, i_got, 1)
    i_got = turn(i_out, 1)
    b_total = far_exchange(jnp.concatenate([b_top + b_got, b_end + b_more], axis=1))
    b_got = turn(b_total, 1)
    r_got, i_got, b_got = tie(r_got, i_got, b_got)
    r_out, r_keep = split(r_keep, r_got, 2)
    r_got = turn(r_out, 0)
    i_top, i_end = i_keep[:, :48] + i_got[:, :48], i_keep[:, 48:] + i_got[:, 48:]
    i_got = hop(i_top, 3)
    b_two = jnp.concatenate([b_total, b_got], axis=0)
    *sends, keep = input_grad(place, gq, gk, gv, w3, gfin_half, after=(r_out, r_keep, i_top, i_end, b_two))
    r_got, i_got, keep = tie(r_got, i_got, keep)
    swapped = [swap(sends[0])]
    r_out, r_keep = split(r_keep, r_got, 1)
    r_got = turn(r_out, 1)
    i_more = hop(i_end, 3)
    r_got, i_more, swapped[0] = tie(r_got, i_more, swapped[0])
    swapped.append(swap(sends[1]))
    r_total = r_keep + r_got
    r_got = hop(r_total, 3)
    b_got = turn(b_two, 0)
    i_total = far_exchange(jnp.concatenate([i_top + i_got, i_end + i_more], axis=1))
    i_got = turn(i_total, 1)
    r_got, b_got, i_got, swapped[1] = tie(r_got, b_got, i_got, swapped[1])
    swapped.append(swap(sends[2]))
    r_total = far_exchange(r_total + r_got)
    r_got = turn(r_total, 1)
    i_two = jnp.concatenate([i_total, i_got], axis=0)
    i_got = turn(i_two, 0)
    b_near = jnp.concatenate([b_two, b_got], axis=0)
    b_far = hop(b_near, 0)
    r_got, i_got, b_far, b_near, swapped[2] = tie(r_got, i_got, b_far, b_near, swapped[2])
    swapped.append(swap(sends[3]))
    grad_w_back = in_order(1, place, b_far, in_order(0, place, b_near))
    r_two = jnp.concatenate([r_total, r_got], axis=0)
    r_got = turn(r_two, 0)
    r_far = hop(r_two, 0)
    i_near = jnp.concatenate([i_two, i_got], axis=0)
    i_far = hop(i_near, 0)
    grad_w_in = in_order(1, place, i_far, in_order(0, place, i_near, after=(r_two,)))
    rest = order_rest(1, 0, place, r_far, width, order_rest(0, 0, place, r_two, width))
    grad_w_in, swapped[3] = tie(grad_w_in, swapped[3])
    grad_tokens = keep + jnp.concatenate(swapped, axis=0)
    r_got, grad_tokens, grad_w_back, *rest = tie(r_got, grad_tokens, grad_w_back, *rest)
    r_far = hop(r_got, 0)
    rest = order_rest(0, 2, place, r_got, width, rest)
    grad_w3, grad_w_out, rows = order_rest(1, 2, place, r_far, width, rest)
    grad_bias, grad_gain, grad_shift, grad_b_in, grad_qv, loss = small_outputs(count, rows)
    return (
        output,
        logits_p[None],
        logits_c[None],
        grad_tokens,
        jnp.transpose(grad_w3, (1, 0, 2)),
        grad_qv,
        grad_w_out,
        grad_w_in,
        grad_b_in.reshape(units),
        grad_w_back,
        grad_bias,
        grad_gain,
        grad_shift,
        loss.reshape(()),
    )


def solution(mesh):
    in_specs = (
        P("dp", None),
        P("dp", None),
        P("dp", None),
        P("dp", "tensor", None, None),
        P("dp", None, "tensor", None, None),
        P(None, None, "tensor"),
        P(None, "tensor"),
        P("tensor", None),
        P(None, "tensor"),
        P("tensor"),
        P("tensor", None),
        P(),
        P(),
        P(),
    )
    out_specs = (
        P("dp", "tensor"),
        P("dp", "tensor", None, None),
        P("dp", None, "tensor", None, None),
        P("dp", "tensor"),
        P(None, None, "tensor"),
        P(None, "tensor"),
        P("tensor", None),
        P(None, "tensor"),
        P("tensor"),
        P("tensor", None),
        P(),
        P(),
        P(),
        P(),
    )
    return jax.shard_map(local, mesh=mesh, in_specs=in_specs, out_specs=out_specs, check_vma=False)
```

```python
import functools

import jax
import jax.numpy as jnp
from jax import lax
from jax.experimental import pallas as pl
from jax.experimental.pallas import tpu as pltpu
from jax.sharding import PartitionSpec as P

D = 768
HEAD = 64
PROMPT = 512
CONT = 8
CONT_LEN = 128
TOTAL = 576
KEYS = 640
SLOTS = 1536

NEG_FILL = -1e30
EPS_NORM = 1e-12
F32 = jnp.float32
BF16 = jnp.bfloat16
VMEM_CAP = 36 * 1024 * 1024
VMEM_WIDE = 60 * 1024 * 1024
CONT_CAP = 36 * 1024 * 1024
ROWS_CAP = 60 * 1024 * 1024
BACK_CAP = 24 * 1024 * 1024
ROWS = 256
UNITS = 1536
GROUP = 2
BACK_ROWS = 384
EARLY = 2
COST_DIV = 1000


def nn(a, b):
    return lax.dot_general(a, b, (((1,), (0,)), ((), ())), preferred_element_type=F32)


def nt(a, b):
    return lax.dot_general(a, b, (((1,), (1,)), ((), ())), preferred_element_type=F32)


def tn(a, b):
    return lax.dot_general(a, b, (((0,), (0,)), ((), ())), preferred_element_type=F32)


def whole(shape):
    return pl.BlockSpec(shape, lambda *_: (0,) * len(shape))


def const(a):
    return pl.BlockSpec(a.shape, lambda *_: (0,) * len(a.shape), pipeline_mode=pl.Buffered(1))


ANY = pl.BlockSpec(memory_space=pl.ANY)
IN_HBM = pl.BlockSpec(memory_space=pltpu.HBM)


def params(n, cap):
    return pltpu.CompilerParams(dimension_semantics=("arbitrary",) * n, vmem_limit_bytes=cap)


def cost(flops, nbytes, trans=0):
    return pl.CostEstimate(flops=int(flops / COST_DIV), bytes_accessed=int(nbytes / COST_DIV), transcendentals=0)


def run(kernel, operands, in_specs, out_specs, out_shape, grid, name, estimate, scalars=0, scratch=(),
        aliases=None, after=(), cap=VMEM_CAP):
    n, m = len(operands), len(after)

    def body(*refs):
        kernel(*refs[:n], *refs[n + m :])

    return pl.pallas_call(
        body,
        name=name,
        grid_spec=pltpu.PrefetchScalarGridSpec(
            num_scalar_prefetch=scalars,
            grid=grid,
            in_specs=list(in_specs) + [ANY] * m,
            out_specs=out_specs,
            scratch_shapes=scratch,
        ),
        out_shape=out_shape,
        input_output_aliases=aliases or {},
        compiler_params=params(len(grid), cap),
        cost_estimate=estimate,
    )(*operands, *after)


def qkv_kernel(tok, w, bias, q, k, v):
    x = tok[...]
    q[...] = (nn(x, w[0]) + bias[0:1]).astype(BF16) * jnp.asarray(0.125, BF16)
    k[...] = nn(x, w[1]).astype(BF16)
    v[...] = (nn(x, w[2]) + bias[1:2]).astype(BF16)


def project(tokens, w3, bias_qv):
    width = w3.shape[2]
    rows = 512
    spec = pl.BlockSpec((rows, width), lambda i: (i, 0))
    out = jax.ShapeDtypeStruct((SLOTS, width), BF16)
    return pl.pallas_call(
        qkv_kernel,
        name="qkv_proj",
        grid=(SLOTS // rows,),
        in_specs=[
            pl.BlockSpec((rows, D), lambda i: (i, 0)),
            whole((3, D, width)),
            whole((2, width)),
        ],
        out_specs=[spec] * 3,
        out_shape=[out] * 3,
        compiler_params=params(1, VMEM_CAP),
        cost_estimate=cost(2 * SLOTS * D * 3 * width, 2 * (SLOTS * D + 3 * D * width + 3 * SLOTS * width)),
    )(tokens, w3, bias_qv)


def half_mask(rows, h):
    lane = lax.broadcasted_iota(jnp.int32, (rows, 128), 1)
    return lane < HEAD if h == 0 else lane >= HEAD


def only(x, h):
    return jnp.where(half_mask(x.shape[0], h), x, jnp.zeros_like(x))


def pair(h):
    return slice(h // 2 * 128, h // 2 * 128 + 128)


def parts(groups):
    return [slice(g * CONT_LEN, (g + 1) * CONT_LEN) for g in range(groups)]


def own_keys(groups):
    return [slice(PROMPT + g * CONT_LEN, PROMPT + (g + 1) * CONT_LEN) for g in range(groups)]


def fill(kp, vp, kt, vx):
    kt[:, :PROMPT] = kp[...].T
    for p in range(kp.shape[1] // 128):
        vx[p, :PROMPT, :128] = vp[:, p * 128 : (p + 1) * 128]
        vx[p, :, 128:] = jnp.ones_like(vx[p, :, 128:])


def attend(q, kt, vx, soft, ctx, inv, groups):
    heads = q.shape[1] // HEAD

    def score(h):
        qm = only(q[:, pair(h)], h % 2)
        return nn(qm, kt[pair(h), :PROMPT]), [
            nn(qm[r], kt[pair(h), c]) for r, c in zip(parts(groups), own_keys(groups))
        ]

    def mix(h, e):
        out = nn(e[0], vx[h // 2, :PROMPT])
        if groups:
            out = out + jnp.concatenate(
                [nn(x, vx[h // 2, c]) for x, c in zip(e[1], own_keys(groups))], axis=0
            )
        return out

    s, e, outs = [score(0)], [], []
    for h in range(heads):
        if h + 1 < heads:
            s.append(score(h + 1))
        e.append(soft(h, *s[h]))
        if h:
            outs.append(mix(h - 1, e[h - 1]))
    outs.append(mix(heads - 1, e[-1]))
    mine = half_mask(q.shape[0], 0)
    for h in range(0, heads, 2):
        scale = 1.0 / jnp.where(mine, outs[h][:, 128:], outs[h + 1][:, 128:])
        inv[:, pair(h)] = scale
        ctx[:, pair(h)] = (
            (jnp.where(mine, outs[h][:, :128], outs[h + 1][:, :128]) * scale).astype(BF16).astype(F32)
        )


def prompt_fwd_kernel(q, k, v, prev, logits, weights, ctx, inv, kt, vx):
    @pl.when(pl.program_id(0) == 0)
    def _():
        fill(k, v, kt, vx)

    def soft(h, s, _):
        x = s + prev[h].astype(F32)
        logits[h] = x.astype(BF16)
        e = jnp.exp(x - jnp.max(x, axis=-1, keepdims=True)).astype(BF16)
        weights[h] = e
        return e, []

    attend(q[...], kt, vx, soft, ctx, inv, 0)


def prompt_forward(q, k, v, prev, after=()):
    heads = prev.shape[0]
    width = heads * HEAD
    rows = 256
    big = pl.BlockSpec((heads, rows, PROMPT), lambda r: (0, r, 0))
    row = pl.BlockSpec((rows, width), lambda r: (r, 0))
    front = pl.BlockSpec((PROMPT, width), lambda r: (0, 0))
    shape = jax.ShapeDtypeStruct((heads, PROMPT, PROMPT), BF16)
    n = heads * PROMPT * PROMPT
    return run(
        prompt_fwd_kernel,
        (q, k, v, prev),
        [row, front, front, big],
        [big, big, row, row],
        [shape, shape] + [jax.ShapeDtypeStruct((PROMPT, width), F32)] * 2,
        (PROMPT // rows,),
        "attn_prompt_fwd",
        cost(4 * n * HEAD, 6 * n, n),
        scratch=[pltpu.VMEM((width, PROMPT), BF16), pltpu.VMEM((heads // 2, PROMPT, 256), BF16)],
        after=after,
    )


def cont_fwd_kernel(c0, lens, q, kp, vp, ko, vo, prev, *refs):
    logits, weights, ctx, inv, kt, vx = refs[-6:]

    @pl.when(pl.program_id(0) == 0)
    def _():
        fill(kp, vp, kt, vx)

    kt[:, PROMPT:] = ko[...].T
    for p in range(ko.shape[1] // 128):
        vx[p, PROMPT:, :128] = vo[:, p * 128 : (p + 1) * 128]
    column = lax.broadcasted_iota(jnp.int32, (CONT_LEN, CONT_LEN), 1)
    first = c0 + pl.program_id(0) * GROUP
    live = [column < lens[0, first + g] for g in range(GROUP)]

    def soft(h, s1, s2):
        front, own = [], []
        for g, r in enumerate(parts(GROUP)):
            a = s1[r] + prev[g, h, :, :PROMPT].astype(F32)
            b = s2[g] + prev[g, h, :, PROMPT:].astype(F32)
            logits[g, h, :, :PROMPT] = a.astype(BF16)
            logits[g, h, :, PROMPT:] = b.astype(BF16)
            b = jnp.where(live[g], b, NEG_FILL)
            top = jnp.maximum(
                jnp.max(a, axis=-1, keepdims=True), jnp.max(b, axis=-1, keepdims=True)
            )
            front.append(jnp.exp(a - top).astype(BF16))
            own.append(jnp.exp(b - top).astype(BF16))
            weights[g, h, :, :PROMPT] = front[g]
            weights[g, h, :, PROMPT:] = own[g]
        return jnp.concatenate(front, axis=0), own

    attend(q[...], kt, vx, soft, ctx, inv, GROUP)


def cont_forward(c0, n, lens, q, k, v, prev, earlier=(), after=()):
    heads = prev.shape[1]
    width = heads * HEAD
    rows = GROUP * CONT_LEN
    first, at = (PROMPT // CONT_LEN + c0) // GROUP, c0 // GROUP
    own = pl.BlockSpec((rows, width), lambda c, *_: (c + first, 0))
    front = pl.BlockSpec((PROMPT, width), lambda c, *_: (0, 0))
    big = pl.BlockSpec((GROUP, heads, CONT_LEN, KEYS), lambda c, *_: (c + at, 0, 0, 0))
    row = pl.BlockSpec((rows, width), lambda c, *_: (c, 0))
    shape = jax.ShapeDtypeStruct((CONT, heads, CONT_LEN, KEYS), BF16)
    size = n * heads * CONT_LEN * KEYS
    return run(
        functools.partial(cont_fwd_kernel, c0),
        (lens, q, k, v, k, v, prev, *earlier),
        [own, front, front, own, own, big] + [ANY] * len(earlier),
        [big, big, row, row],
        [shape, shape] + [jax.ShapeDtypeStruct((n * CONT_LEN, width), F32)] * 2,
        (n // GROUP,),
        "attn_cont_fwd",
        cost(4 * size * HEAD, 6 * size, size),
        cap=CONT_CAP,
        scalars=1,
        scratch=[
            pltpu.VMEM((width, PROMPT + rows), BF16),
            pltpu.VMEM((heads // 2, PROMPT + rows, 256), BF16),
        ],
        aliases={7 + m: m for m in range(len(earlier))},
        after=after,
    )


def hop(x, bit):
    n = lax.axis_size("dp")
    return lax.ppermute(x, "dp", [(i, i ^ (1 << bit)) for i in range(n)])


def turn(x, step):
    n = lax.axis_size("dp")
    return lax.ppermute(x, "dp", [(i, i ^ (4 if (i & 1) ^ step else 2)) for i in range(n)])


def grad_back_kernel(flip, place, act, gffn, out):
    acc = tn(act[...], gffn[...])
    low = place[2] if flip else place[1]
    for m in range(2):
        out[pl.ds(jnp.bitwise_xor(low % 2, m), 1)] = acc[None, 192 * m : 192 * m + 192]


def grad_back(flip, place, act, gffn, after=()):
    low = lambda place: (place[2] if flip else place[1]) // 2 % 2
    return run(
        functools.partial(grad_back_kernel, flip),
        (place, act, gffn),
        [
            pl.BlockSpec((SLOTS, 384), lambda i, place: (0, 2 * ((place[1] // 4 + flip) % 2) + i)),
            whole((SLOTS, D)),
        ],
        pl.BlockSpec((2, 192, D), lambda i, place: (jnp.bitwise_xor(i, low(place)), 0, 0)),
        jax.ShapeDtypeStruct((4, 192, D), F32),
        (2,),
        "grad_w_back",
        cost(2 * SLOTS * 768 * D, 2 * SLOTS * 768 * 2 + 4 * 768 * D),
        cap=BACK_CAP,
        scalars=1,
        after=after,
    )


IN_BLOCK = 512


def grad_in_kernel(n, place, x, ghid, send, keep, xt):
    i = pl.program_id(0)

    @pl.when(i % n == 0)
    def _():
        xt[...] = x[...].T

    acc = nn(xt[...], ghid[...])

    def put(out, low):
        for m in range(4):
            out[pl.ds(jnp.bitwise_xor(low, m), 1)] = acc[None, 96 * m : 96 * m + 96]

    pl.when(i < n)(lambda: put(send, place[2]))
    pl.when(i >= n)(lambda: put(keep, place[1] % 4))


def grad_in(place, xlow, ghid, after=()):
    units = ghid.shape[1]
    n = units // IN_BLOCK
    shape = jax.ShapeDtypeStruct((4, 96, units), F32)
    return run(
        functools.partial(grad_in_kernel, n),
        (place, xlow, ghid),
        [
            pl.BlockSpec((SLOTS, 384), lambda i, place: (0, (place[1] // 4 + 1 - i // n) % 2)),
            pl.BlockSpec((SLOTS, IN_BLOCK), lambda i, *_: (0, i % n)),
        ],
        [
            pl.BlockSpec((4, 96, IN_BLOCK), lambda i, *_: (0, 0, jnp.minimum(i, n - 1))),
            pl.BlockSpec((4, 96, IN_BLOCK), lambda i, *_: (0, 0, jnp.maximum(i - n, 0))),
        ],
        [shape] * 2,
        (2 * n,),
        "grad_w_in",
        cost(4 * SLOTS * 384 * units, 2 * SLOTS * (768 + 2 * units) + 8 * 384 * units),
        scalars=1,
        scratch=[pltpu.VMEM((384, SLOTS), BF16)],
        after=after,
    )


def grad_rest_kernel(place, tok, gq, gk, gv, ctx_p, ctx_a, ctx_b, gattn, stats, other, *refs):
    send, keep, ao = refs
    i = pl.program_id(0)
    left = (place[1] // 4 + 1 - i) % 2 == 0

    @pl.when(i == 0)
    def _():
        ctx = jnp.concatenate([ctx_p[...], ctx_a[...], ctx_b[...]], axis=0).astype(BF16)
        ao[...] = nn(ctx.T, gattn[...])

    tok_t = tok[...].T
    aq = nn(tok_t, gq[...])
    ak = nn(tok_t, gk[...])
    av = nn(tok_t, gv[...])
    o = jnp.where(left, ao[:192], ao[192:])
    bias = jnp.concatenate(
        [jnp.sum(g[...].astype(F32), axis=0, keepdims=True) for g in (gq, gv)], axis=1
    )
    row = lax.broadcasted_iota(jnp.int32, (16, D), 0)
    half_of = lax.broadcasted_iota(jnp.int32, (16, D), 1) // (D // 2)
    small = jnp.where((half_of == place[0]) | (row >= 7), stats[...], other[...])
    small = jnp.where(row == 9, bias, small)

    def put(out, low):
        for m in range(4):
            j = jnp.bitwise_xor(low, m)
            out[pl.ds(j, 1), 0:96, 0:384] = aq[None, 96 * m : 96 * m + 96]
            out[pl.ds(j, 1), 0:96, 384:768] = ak[None, 96 * m : 96 * m + 96]
            out[pl.ds(j, 1), 96:144, 0:384] = av[None, 96 * m : 96 * m + 48]
            out[pl.ds(j, 1), 96:144, 384:768] = av[None, 96 * m + 48 : 96 * m + 96]
            out[pl.ds(j, 1), 144:192, :] = o[None, 48 * m : 48 * m + 48]
            out[pl.ds(j, 1), 192:200, :] = jnp.concatenate(
                [
                    jnp.where(left, small[2 * m : 2 * m + 2], small[8 + 2 * m : 10 + 2 * m]),
                    jnp.zeros((6, D), F32),
                ],
                axis=0,
            )[None]

    pl.when(i == 0)(lambda: put(send, place[2]))
    pl.when(i == 1)(lambda: put(keep, place[1] % 4))


def grad_rest(place, tokens, gq, gk, gv, ctx_p, ctx_a, ctx_b, gattn, stats, other, after=()):
    width = gq.shape[1]
    shape = jax.ShapeDtypeStruct((4, 200, D), F32)
    fixed = (gq, gk, gv, ctx_p, ctx_a, ctx_b, gattn, stats, other)
    return run(
        grad_rest_kernel,
        (place, tokens) + fixed,
        [pl.BlockSpec((SLOTS, 384), lambda i, place: (0, (place[1] // 4 + 1 - i) % 2))]
        + [const(x) for x in fixed],
        [const(shape)] * 2,
        [shape] * 2,
        (2,),
        "grad_w_rest",
        cost(2 * SLOTS * (D * 3 * width + width * D), 2 * SLOTS * (6 * width + 2 * D)),
        scalars=1,
        scratch=[pltpu.VMEM((width, D), F32)],
        after=after,
    )


def chunk_of(place, far, m):
    if far:
        return (1 - place[1] // 4) * 4 + jnp.bitwise_xor(place[2], m)
    return jnp.bitwise_xor(place[1], m)


def staged(moves):
    for first, _ in moves:
        first.start()
    for first, rest in moves:
        first.wait()
        for c in rest:
            c.start()
    for _, rest in moves:
        for c in rest:
            c.wait()


def order_kernel(rows, far, place, src, *refs):
    out, hold, sems_in, sems_out = refs[-4:]
    moves = []
    for m in range(4):
        at = pl.multiple_of(chunk_of(place, far, m) * rows, 8)
        moves.append(
            (
                pltpu.make_async_copy(src.at[m], hold.at[m], sems_in.at[m]),
                [pltpu.make_async_copy(hold.at[m], out.at[pl.ds(at, rows)], sems_out.at[m])],
            )
        )
    staged(moves)


def in_order(far, place, chunks, prev=None, after=()):
    _, rows, cols = chunks.shape
    return run(
        functools.partial(order_kernel, rows, far),
        (place, chunks) + (() if prev is None else (prev,)),
        [ANY] * (1 if prev is None else 2),
        ANY,
        jax.ShapeDtypeStruct((8 * rows, cols), F32),
        (1,),
        "in_order",
        cost(0, 8 * chunks.size),
        scalars=1,
        scratch=[pltpu.VMEM(chunks.shape, F32), pltpu.SemaphoreType.DMA((4,)), pltpu.SemaphoreType.DMA((4,))],
        aliases={} if prev is None else {2: 0},
        after=after,
    )


def order_rest_kernel(far, first, width, place, src, *refs):
    gw, go, small, hold, sems_in, sems_out = refs[-6:]
    moves, n = [], 0

    def copy(a, b):
        nonlocal n
        n += 1
        return pltpu.make_async_copy(a, b, sems_out.at[n - 1])

    left, right = pl.ds(0, width), pl.ds(width, width)
    for m in range(2):
        c = chunk_of(place, far, first + m)
        rows = hold.at[m]
        wide = pl.ds(pl.multiple_of(c * 96, 8), 96)
        out = [
            copy(rows.at[pl.ds(0, 96), left], gw.at[0, wide]),
            copy(rows.at[pl.ds(0, 96), right], gw.at[1, wide]),
            copy(rows.at[pl.ds(96, 48), left], gw.at[2, pl.ds(pl.multiple_of(c * 96, 8), 48)]),
            copy(rows.at[pl.ds(96, 48), right], gw.at[2, pl.ds(pl.multiple_of(c * 96 + 48, 8), 48)]),
            copy(rows.at[pl.ds(144, 48)], go.at[pl.ds(pl.multiple_of(c * 48, 8), 48)]),
            copy(rows.at[pl.ds(192, 8)], small.at[pl.ds(pl.multiple_of(c * 8, 8), 8)]),
        ]
        moves.append((pltpu.make_async_copy(src.at[m], rows, sems_in.at[m]), out))
    staged(moves)


def order_rest(far, first, place, chunks, width, prev=None, after=()):
    return run(
        functools.partial(order_rest_kernel, far, first, width),
        (place, chunks) + (() if prev is None else tuple(prev)),
        [ANY] * (1 if prev is None else 4),
        [ANY] * 3,
        [
            jax.ShapeDtypeStruct((3, D, width), F32),
            jax.ShapeDtypeStruct((width, D), F32),
            jax.ShapeDtypeStruct((64, D), F32),
        ],
        (1,),
        "order_rest",
        cost(0, 8 * chunks.size),
        scalars=1,
        scratch=[
            pltpu.VMEM(chunks.shape, F32),
            pltpu.SemaphoreType.DMA((2,)),
            pltpu.SemaphoreType.DMA((12,)),
        ],
        aliases={} if prev is None else {2: 0, 3: 1, 4: 2},
        after=after,
    )


def small_kernel(count, rows, bias, gain, shift, b_in, qv, loss):
    row = lambda n: rows[8 * (n // 2) + n % 2 : 8 * (n // 2) + n % 2 + 1]
    bias[0:1], bias[1:2] = row(4), row(1)
    gain[0:1], gain[1:2] = row(5), row(2)
    shift[0:1], shift[1:2] = row(6), row(3)
    b_in[0:1, :D], b_in[0:1, D:] = row(7), row(8)
    qv[0:1], qv[1:2] = row(9)[:, : D // 2], row(9)[:, D // 2 :]
    loss[...] = jnp.sum(row(0), axis=1, keepdims=True) / count


def small_outputs(count, rows):
    shapes = [(2, D)] * 3 + [(1, 2 * D), (2, D // 2), (1, 1)]
    return run(
        functools.partial(small_kernel, count),
        (rows,),
        [whole(rows.shape)],
        [whole(x) for x in shapes],
        [jax.ShapeDtypeStruct(x, F32) for x in shapes],
        (1,),
        "small_outputs",
        cost(0, 8 * rows.size),
    )


def piece_copies(pieces, stage_a, stage_b, sems):
    first, second = [], []
    for far in range(2):
        own_a, rest_a = pieces[2 * far : 2 * far + 2]
        most_b, cross_b = pieces[4 + 2 * far : 6 + 2 * far]
        for m in range(4):
            k = 4 * far + m
            src_a = own_a if m == 0 else rest_a.at[pl.ds((m - 1) * 128, 128)]
            src_b = cross_b if m == 3 else most_b.at[pl.ds(m * 192, 192)]
            first.append(pltpu.make_async_copy(src_a, stage_a.at[k], sems.at[k]))
            second.append(pltpu.make_async_copy(src_b, stage_b.at[k], sems.at[8 + k]))
    return first, second


def lay_out_in(place, first, second, wi, wo, b, stage_a):
    for copy in first + second:
        copy.start()
    for k, copy in enumerate(first):
        c = jnp.bitwise_xor(place[3], k)
        copy.wait()
        wi[pl.ds(pl.multiple_of(c * 96, 16), 96), :] = stage_a[k, 0:96, :].astype(BF16)
        tail = stage_a[k, 96:120, :]
        wo[pl.ds(pl.multiple_of(c * 48, 16), 48), :] = jnp.concatenate(
            [tail[:, :D], tail[:, D:]], axis=0
        ).astype(BF16)
    b[...] = stage_a[0, 120:128, :]


def lay_out_back(place, second, wb, stage_b):
    for k, copy in enumerate(second):
        c = jnp.bitwise_xor(place[3], k)
        copy.wait()
        wb[pl.ds(pl.multiple_of(c * 192, 16), 192), :] = stage_b[k].astype(BF16)


def forward_kernel(first_block, count, has_prev, *refs):
    lens, place = refs[:2]
    if has_prev:
        ctx_own, ctx_oth, tok, teach, wo_own, wi_own, wb_own, b_own, bias_out, gain, shift = refs[2:13]
        wo_oth, wi_oth, wb_oth, b_oth = refs[13:17]
        out, act, gate, gffn, gsec, xlow, rstd, stats = refs[-8:]
        own, oth = ctx_own[...], ctx_oth[...]
    else:
        ctx_p, ctx_a, oth_p, oth_a, tok, teach, wo_own, wi_own, wb_own, b_own, bias_out, gain, shift = refs[2:15]
        pieces = refs[15:23]
        out, act, gate, gffn, gsec, xlow, rstd, stats, wo_oth, wi_oth, wb_oth, b_oth = refs[-15:-3]
        early = pl.program_id(0) < PROMPT // ROWS
        own = jnp.where(early, ctx_p[...], ctx_a[...])
        oth = jnp.where(early, oth_p[...], oth_a[...])

        stage_a, stage_b, sems = refs[-3:]
        first_copies, second_copies = piece_copies(pieces, stage_a, stage_b, sems)

        @pl.when(pl.program_id(0) == 0)
        def _():
            lay_out_in(place, first_copies, second_copies, wi_oth, wo_oth, b_oth, stage_a)

    i = pl.program_id(0)
    blk = i + first_block
    n_own = wi_own.shape[1] // UNITS

    @pl.when(i == 0)
    def _():
        stats[...] = jnp.zeros_like(stats)

    attn = nn(own.astype(BF16), wo_own[...]) + nn(oth.astype(BF16), wo_oth[...])
    fin = tok[...].astype(F32) + attn + bias_out[0:1]
    c1 = fin - jnp.mean(fin, axis=-1, keepdims=True)
    r1 = lax.rsqrt(jnp.mean(c1 * c1, axis=-1, keepdims=True) + EPS_NORM)
    rstd[...] = jnp.broadcast_to(r1, rstd.shape)
    first = c1 * r1 * gain[0:1] + shift[0:1]
    x = first.astype(BF16)
    xlow[...] = x
    ffn = None
    for side in range(2):
        wi, wb, bb = ((wi_own, wb_own, b_own), (wi_oth, wb_oth, b_oth))[side]
        if side == 1 and not has_prev:
            pl.when(i == 0)(functools.partial(lay_out_back, place, second_copies, wb_oth, stage_b))
        for u in range(n_own):
            cols = slice(u * UNITS, (u + 1) * UNITS)
            h = nn(x, wi[:, cols]) + bb[0:1, cols]
            cdf = 0.5 + 0.5 * lax.erf(h * 0.7071067811865476)
            pdf = jnp.exp(-0.5 * h * h) * 0.3989422804014327
            a = (h * cdf).astype(BF16)
            at = (side * n_own + u) * UNITS
            gate[:, at : at + UNITS] = (cdf + h * pdf).astype(BF16)
            if side == 0:
                act[:, cols] = a
            part = nn(a, wb[cols, :])
            ffn = part if ffn is None else ffn + part
    sec = first + ffn + bias_out[1:2]
    c2 = sec - jnp.mean(sec, axis=-1, keepdims=True)
    r2 = lax.rsqrt(jnp.mean(c2 * c2, axis=-1, keepdims=True) + EPS_NORM)
    xh2 = c2 * r2
    result = xh2 * gain[1:2] + shift[1:2]
    left = place[0] == 0
    hd = D // 2
    out[...] = jnp.where(left, result[:, :hd], result[:, hd:]).astype(BF16)
    row = lax.broadcasted_iota(jnp.int32, (ROWS, 1), 0)
    per = ROWS // CONT_LEN
    cont0 = (blk - PROMPT // ROWS) * per
    valid = jnp.zeros((ROWS, 1), jnp.bool_)
    for m in range(per):
        length = jnp.where(cont0 < 0, CONT_LEN, lens[0, jnp.maximum(cont0 + m, 0)])
        valid = valid | ((row >= m * CONT_LEN) & (row < m * CONT_LEN + length))
    diff = jnp.where(valid, result - teach[...].astype(F32), 0.0)
    g = diff * (2.0 / count)
    gy = g * gain[1:2]
    g2 = r2 * (
        gy
        - jnp.mean(gy, axis=-1, keepdims=True)
        - xh2 * jnp.mean(gy * xh2, axis=-1, keepdims=True)
    )
    stats[0:1] += jnp.sum(diff * diff, axis=0, keepdims=True)
    stats[1:2] += jnp.sum(g2, axis=0, keepdims=True)
    stats[2:3] += jnp.sum(g * xh2, axis=0, keepdims=True)
    stats[3:4] += jnp.sum(g, axis=0, keepdims=True)
    gsec[...] = g2
    gffn[...] = g2.astype(BF16)


def rows_forward(first_block, blocks, count, lens, place, ctxs, tok, teach, fixed, more, prev=None, after=()):
    width = ctxs[0].shape[1]
    units = fixed[1].shape[1]
    row = lambda w: pl.BlockSpec((ROWS, w), lambda i, *_: (i + first_block, 0))
    split = PROMPT // ROWS
    if prev is None:
        low = pl.BlockSpec((ROWS, width), lambda i, *_: (jnp.minimum(i, split - 1), 0))
        high = pl.BlockSpec((ROWS, width), lambda i, *_: (jnp.maximum(i - split, 0), 0))
        ctx_specs = [low, high, low, high]
    else:
        ctx_specs = [pl.BlockSpec((ROWS, width), lambda i, *_: (i, 0))] * 2
    shapes = [(D // 2, BF16), (units, BF16), (2 * units, BF16), (D, BF16), (D, F32), (D, BF16), (128, F32)]
    operands = [lens, place, *ctxs, tok, teach, *fixed, *more]
    specs = ctx_specs + [row(D), row(D)] + [const(a) for a in fixed]
    specs += [IN_HBM if prev is None else const(a) for a in more]
    aliases, scratch = {}, []
    out_specs = [row(w) for w, _ in shapes] + [whole((16, D))]
    out_shape = [jax.ShapeDtypeStruct((SLOTS, w), t) for w, t in shapes] + [jax.ShapeDtypeStruct((16, D), F32)]
    if prev is None:
        weights = [
            jax.ShapeDtypeStruct((width, D), BF16),
            jax.ShapeDtypeStruct((D, units), BF16),
            jax.ShapeDtypeStruct((units, D), BF16),
            jax.ShapeDtypeStruct((8, units), F32),
        ]
        out_specs, out_shape = out_specs + [const(w) for w in weights], out_shape + weights
        scratch = [
            pltpu.VMEM((8, 128, units), F32),
            pltpu.VMEM((8, 192, D), F32),
            pltpu.SemaphoreType.DMA((16,)),
        ]
    else:
        aliases = {len(operands) + n: n for n in range(7)}
        operands, specs = operands + list(prev), specs + [ANY] * 7
    return run(
        functools.partial(forward_kernel, first_block, count, prev is not None),
        operands,
        specs,
        out_specs,
        out_shape,
        (blocks,),
        "rows_forward",
        cap=ROWS_CAP,
        scratch=scratch,
        estimate=cost(2 * blocks * ROWS * D * (4 * units + 2 * width), 8 * D * units + blocks * ROWS * 24000),
        scalars=2,
        aliases=aliases,
        after=after,
    )


def backward_kernel(place, gate, gffn, gsec, xlow, rstd, wo, wi_own, wi_oth, wb_own, wb_oth, gain, shift,
                    stats_f, *refs):
    ghid, gattn, gctx, gfin, stats, gbin = refs[-6:]
    i = pl.program_id(0)
    n_own = wi_own.shape[1] // UNITS

    @pl.when(i == 0)
    def _():
        stats[...] = stats_f[...]
        gbin[0:1, :D] = stats_f[7:8]
        gbin[0:1, D:] = stats_f[8:9]

    gf = gffn[...]
    gfirst = gsec[...]
    for side in range(2):
        wi, wb = ((wi_own, wb_own), (wi_oth, wb_oth))[side]
        for u in range(n_own):
            cols = slice(u * UNITS, (u + 1) * UNITS)
            at = (side * n_own + u) * UNITS
            gh = (nt(gf, wb[cols, :]) * gate[:, at : at + UNITS].astype(F32)).astype(BF16)
            if side == 0:
                ghid[:, cols] = gh
                gbin[0:1, cols] += jnp.sum(gh.astype(F32), axis=0, keepdims=True)
            gfirst = gfirst + nt(gh, wi[:, cols])
    xh1 = (xlow[...].astype(F32) - shift[0:1]) * (1.0 / gain[0:1])
    gy1 = gfirst * gain[0:1]
    g1 = rstd[:, 0:1] * (
        gy1
        - jnp.mean(gy1, axis=-1, keepdims=True)
        - xh1 * jnp.mean(gy1 * xh1, axis=-1, keepdims=True)
    )
    stats[4:5] += jnp.sum(g1, axis=0, keepdims=True)
    stats[5:6] += jnp.sum(gfirst * xh1, axis=0, keepdims=True)
    stats[6:7] += jnp.sum(gfirst, axis=0, keepdims=True)

    @pl.when(i == pl.num_programs(0) - 1)
    def _():
        stats[7:8] = gbin[0:1, :D]
        stats[8:9] = gbin[0:1, D:]

    hd = D // 2
    gfin[...] = jnp.where(place[0] == 0, g1[:, :hd], g1[:, hd:])
    ga1 = g1.astype(BF16)
    gattn[...] = ga1
    gctx[...] = nt(ga1, wo[...]).astype(BF16)


def rows_backward(first, blocks, place, gate, gffn, gsec, xlow, rstd, fixed, prev=None, after=()):
    wo, wi_own = fixed[:2]
    width, units = wo.shape[0], wi_own.shape[1]
    row = lambda w: pl.BlockSpec((BACK_ROWS, w), lambda i, *_: (i + first, 0))
    shapes = [(units, BF16), (D, BF16), (width, BF16), (D // 2, F32)]
    operands = [place, gate, gffn, gsec, xlow, rstd] + list(fixed)
    specs = [row(2 * units), row(D), row(D), row(D), row(128)] + [const(a) for a in fixed]
    aliases = {}
    if prev is not None:
        aliases = {len(operands) + n: n for n in range(4)}
        operands, specs = operands + list(prev), specs + [ANY] * 4
    return run(
        backward_kernel,
        operands,
        specs,
        [row(w) for w, _ in shapes] + [whole((16, D))],
        [jax.ShapeDtypeStruct((SLOTS, w), t) for w, t in shapes] + [jax.ShapeDtypeStruct((16, D), F32)],
        (blocks,),
        "rows_backward",
        cost(2 * SLOTS * D * (4 * units + width), 8 * D * units + SLOTS * 20000),
        scalars=1,
        scratch=[pltpu.VMEM((8, units), F32)],
        aliases=aliases,
        after=after,
    )


def attend_back(q, gctx, ctx, inv, load, vt, kall, gq, take, groups):
    heads = q.shape[1] // HEAD
    g2, inner, qt, gt = [], [], [], []
    for p in range(heads // 2):
        cols = pair(2 * p)
        g = (gctx[:, cols].astype(F32) * inv[:, cols]).astype(BF16)
        prod = g.astype(F32) * ctx[:, cols]
        g2.append(g)
        qt.append(q[:, cols].T)
        gt.append(g.T)
        inner += [jnp.sum(only(prod, h), axis=-1, keepdims=True) for h in range(2)]

    def weigh(h):
        gm = only(g2[h // 2], h % 2)
        return nn(gm, vt[pair(h), :PROMPT]), [
            nn(gm[r], vt[pair(h), c]) for r, c in zip(parts(groups), own_keys(groups))
        ]

    def finish(h, e, l):
        part = slice(h % 2 * HEAD, (h % 2 + 1) * HEAD)
        q_h, g_h = qt[h // 2][part], gt[h // 2][part]
        dq = nn(l[0], kall[:PROMPT, pair(h)])
        own = []
        if groups:
            dq = dq + jnp.concatenate(
                [nn(x, kall[c, pair(h)]) for x, c in zip(l[1], own_keys(groups))], axis=0
            )
            own = [
                (nn(q_h[:, r], x), nn(g_h[:, r], y))
                for r, x, y in zip(parts(groups), l[1], e[1])
            ]
        return dq, (nn(q_h, l[0]), nn(g_h, e[0])), own

    mine = half_mask(q.shape[0], 0)
    done = []

    def flush(h):
        done.append(finish(h, *held[h]))
        if h % 2:
            a, b = done[h - 1], done[h]
            gq[:, pair(h)] = (jnp.where(mine, a[0], b[0]) * 0.125).astype(BF16)
            both = lambda x, y: tuple(jnp.concatenate(z, axis=0) for z in zip(x, y))
            take(pair(h), both(a[1], b[1]), [both(x, y) for x, y in zip(a[2], b[2])])

    raw, held = [weigh(0)], []
    for h in range(heads):
        if h + 1 < heads:
            raw.append(weigh(h + 1))
        e = load(h)
        l = [(e[0].astype(F32) * (raw[h][0] - inner[h])).astype(BF16)]
        l.append(
            [
                (y.astype(F32) * (x - inner[h][r])).astype(BF16)
                for y, x, r in zip(e[1], raw[h][1], parts(groups))
            ]
        )
        held.append((e, l))
        if h:
            flush(h - 1)
    flush(heads - 1)


def cont_bwd_kernel(split, q, kp, vp, ko, vo, weights, gctx, ctx_a, inv_a, ctx_b, inv_b,
                    gq, gk, gv, gkp, gvp, vt, kall):
    early = pl.program_id(0) < split
    ctx = jnp.where(early, ctx_a[...], ctx_b[...])
    inv = jnp.where(early, inv_a[...], inv_b[...])

    @pl.when(pl.program_id(0) == 0)
    def _():
        gkp[...] = jnp.zeros_like(gkp)
        gvp[...] = jnp.zeros_like(gvp)
        vt[:, :PROMPT] = vp[...].T
        kall[:PROMPT] = kp[...]

    vt[:, PROMPT:] = vo[...].T
    kall[PROMPT:] = ko[...]

    def load(h):
        return (
            jnp.concatenate([weights[g, h, :, :PROMPT] for g in range(GROUP)], axis=0),
            [weights[g, h, :, PROMPT:] for g in range(GROUP)],
        )

    def take(cols, front, own):
        gkp[cols, :] += front[0]
        gvp[cols, :] += front[1]
        for r, (dk, dv) in zip(parts(GROUP), own):
            gk[r, cols] = dk.T.astype(BF16)
            gv[r, cols] = dv.T.astype(BF16)

    attend_back(q[...], gctx[...], ctx, inv, load, vt, kall, gq, take, GROUP)


def cont_backward(q, k, v, weights, gctx, ctx_a, inv_a, ctx_b, inv_b, after=()):
    heads = weights.shape[1]
    width = heads * HEAD
    rows = GROUP * CONT_LEN
    first = PROMPT // rows
    own = pl.BlockSpec((rows, width), lambda c: (c + first, 0))
    front = pl.BlockSpec((PROMPT, width), lambda c: (0, 0))
    big = pl.BlockSpec((GROUP, heads, CONT_LEN, KEYS), lambda c: (c, 0, 0, 0))
    shape = jax.ShapeDtypeStruct((SLOTS, width), BF16)
    sums = jax.ShapeDtypeStruct((width, PROMPT), F32)
    n = CONT * heads * CONT_LEN * KEYS
    split = ctx_a.shape[0] // rows
    head = pl.BlockSpec((rows, width), lambda c: (jnp.minimum(c, split - 1), 0))
    tail = pl.BlockSpec((rows, width), lambda c: (jnp.maximum(c - split, 0), 0))
    return run(
        functools.partial(cont_bwd_kernel, split),
        (q, k, v, k, v, weights, gctx, ctx_a, inv_a, ctx_b, inv_b),
        [own, front, front, own, own, big, own, head, head, tail, tail],
        [own, own, own, whole((width, PROMPT)), whole((width, PROMPT))],
        [shape, shape, shape, sums, sums],
        (CONT // GROUP,),
        "attn_cont_bwd",
        cost(8 * n * HEAD, 2 * n + 8 * SLOTS * heads * HEAD * 2),
        scratch=[pltpu.VMEM((width, PROMPT + rows), BF16), pltpu.VMEM((PROMPT + rows, width), BF16)],
        after=after,
    )


def prompt_bwd_kernel(q, k, v, weights, gctx, ctx, inv, gkp, gvp, a, b, c, gq, gk, gv, vt, ak, av):
    r = pl.program_id(0)

    @pl.when(r == 0)
    def _():
        vt[...] = v[...].T
        ak[...] = gkp[...]
        av[...] = gvp[...]

    def take(cols, front, own):
        ak[cols, :] += front[0]
        av[cols, :] += front[1]

    attend_back(q[...], gctx[...], ctx[...], inv[...], lambda h: (weights[h], []), vt, k, gq, take, 0)

    @pl.when(r == pl.num_programs(0) - 1)
    def _():
        gk[...] = ak[...].T.astype(BF16)
        gv[...] = av[...].T.astype(BF16)


def prompt_backward(q, k, v, weights, gctx, ctx, inv, gkp, gvp, gq, gk, gv, after=()):
    heads = weights.shape[0]
    width = heads * HEAD
    rows = 256
    row = pl.BlockSpec((rows, width), lambda r: (r, 0))
    front = pl.BlockSpec((PROMPT, width), lambda r: (0, 0))
    acc = whole((width, PROMPT))
    shape = jax.ShapeDtypeStruct((SLOTS, width), BF16)
    n = heads * PROMPT * PROMPT
    return run(
        prompt_bwd_kernel,
        (q, k, v, weights, gctx, ctx, inv, gkp, gvp, gq, gk, gv),
        [row, front, front, pl.BlockSpec((heads, rows, PROMPT), lambda r: (0, r, 0)), row, row, row, acc, acc]
        + [ANY] * 3,
        [row, front, front],
        [shape] * 3,
        (PROMPT // rows,),
        "attn_prompt_bwd",
        cost(8 * n * HEAD, 2 * n + 8 * PROMPT * heads * HEAD * 2),
        scratch=[
            pltpu.VMEM((width, PROMPT), BF16),
            pltpu.VMEM((width, PROMPT), F32),
            pltpu.VMEM((width, PROMPT), F32),
        ],
        aliases={9: 0, 10: 1, 11: 2},
        after=after,
    )


def input_grad_kernel(place, gq, gk, gv, w, base, *refs):
    sends, keep = refs[:-1], refs[-1]
    hd = D // 2
    mine = place[0] == 0
    part = nt(gq[...], w[0]) + nt(gk[...], w[1]) + nt(gv[...], w[2])
    keep[...] = base[...] + jnp.where(mine, part[:, :hd], part[:, hd:])
    away = jnp.where(mine, part[:, hd:], part[:, :hd])

    def put(send):
        send[...] = away

    per = SLOTS // part.shape[0] // len(sends)
    for n, send in enumerate(sends):
        pl.when(pl.program_id(0) // per == n)(functools.partial(put, send))


def input_grad(place, gq, gk, gv, w3, base, after=()):
    width = w3.shape[2]
    rows, cuts = 384, 4
    per = SLOTS // rows // cuts
    row = lambda w: pl.BlockSpec((rows, w), lambda i, *_: (i, 0))
    cut = lambda n: pl.BlockSpec((rows, D // 2), lambda i, *_: (jnp.clip(i - n * per, 0, per - 1), 0))
    return run(
        input_grad_kernel,
        (place, gq, gk, gv, w3, base),
        [row(width)] * 3 + [whole((3, D, width)), row(D // 2)],
        [cut(n) for n in range(cuts)] + [row(D // 2)],
        [jax.ShapeDtypeStruct((SLOTS // cuts, D // 2), F32)] * cuts + [jax.ShapeDtypeStruct((SLOTS, D // 2), F32)],
        (SLOTS // rows,),
        "input_grad",
        cost(2 * SLOTS * D * 3 * width, 2 * (SLOTS * 3 * width) + 6 * SLOTS * D),
        scalars=1,
        after=after,
    )


def swap(x):
    n = lax.axis_size("tensor")
    return lax.ppermute(x, "tensor", [(i, n - 1 - i) for i in range(n)])


def tie(*values):
    return lax.optimization_barrier(values)


def far_exchange(total):
    bit = 4
    while (1 << bit) < lax.axis_size("dp"):
        total = total + hop(total, bit)
        bit += 1
    return total


def local(
    tokens, teacher, lengths, prev_prompt, prev_cont, w_qkv, bias_qv, w_out, w_in, b_in, w_back,
    bias_out, norm_gain, norm_bias,
):
    width = w_qkv.shape[2]
    units = w_in.shape[1]
    w3 = jnp.transpose(w_qkv, (1, 0, 2))
    t = lax.axis_index("tensor").astype(jnp.int32)
    i = lax.axis_index("dp").astype(jnp.int32)
    core, x, z = i % 2, (i // 2) % 2, (i // 4) % 2
    x_first, z_first = 2 * x + z, 2 * z + x
    chunk = core * 4 + x_first
    place = jnp.stack(
        [
            t,
            core * 4 + jnp.where(core == 0, x_first, z_first),
            jnp.where(core == 0, z_first, x_first),
            chunk,
        ]
    )
    count = float(lax.axis_size("dp") * (PROMPT + TOTAL))

    part_o = lax.dynamic_slice_in_dim(w_out, chunk * 48, 48, 0)
    part_i = lax.dynamic_slice_in_dim(w_in, chunk * 96, 96, 0)
    piece_a = jnp.concatenate(
        [
            part_i.astype(F32),
            jnp.concatenate([part_o[:24], part_o[24:]], axis=1).astype(F32),
            jnp.broadcast_to(b_in[None], (8, units)),
        ],
        axis=0,
    )
    piece_b = lax.dynamic_slice_in_dim(w_back, chunk * 192, 192, 0).astype(F32)
    own_a = swap(piece_a)
    own_b = swap(piece_b)
    q, k, v = project(tokens, w3, bias_qv)
    logits_p, probs_p, ctx_p, inv_p = prompt_forward(q, k, v, prev_prompt[0])
    own_a, ctx_p = tie(own_a, ctx_p)
    oth_p = swap(ctx_p)
    zs_a, xs_a, far_own_a = hop(own_a, 2), hop(own_a, 1), hop(own_a, 0)
    logits_c, probs_c, ctx_a, inv_a = cont_forward(0, EARLY, lengths, q, k, v, prev_cont[0], after=(own_a,))
    zs_a, xs_a, far_own_a, own_b, ctx_a = tie(zs_a, xs_a, far_own_a, own_b, ctx_a)
    oth_a = swap(ctx_a)
    logits_c, probs_c, ctx_b, inv_b = cont_forward(
        EARLY, CONT - EARLY, lengths, q, k, v, prev_cont[0], (logits_c, probs_c)
    )
    zs_b, xs_b = hop(own_b, 2), hop(own_b, 1)
    cross_a = turn(jnp.where(core == 0, zs_a, xs_a), 0)
    cross_a, oth_p, zs_b, xs_b, ctx_b = tie(cross_a, oth_p, zs_b, xs_b, ctx_b)
    cross_b = turn(jnp.where(core == 0, zs_b, xs_b), 0)
    rest_a = jnp.concatenate([zs_a, xs_a, cross_a], axis=0)
    most_b = jnp.concatenate([own_b, zs_b, xs_b], axis=0)
    far_rest_a, far_most_b = hop(rest_a, 0), hop(most_b, 0)
    oth_a, cross_b, far_rest_a, far_most_b, ctx_b = tie(oth_a, cross_b, far_rest_a, far_most_b, ctx_b)
    oth_b = swap(ctx_b)
    far_cross_b = hop(cross_b, 0)

    fixed = (w_out, w_in, w_back, b_in[None], bias_out, norm_gain, norm_bias)
    pieces = (
        own_a, rest_a, far_own_a, far_rest_a, most_b, cross_b, far_most_b, far_cross_b,
    )
    n_blocks = SLOTS // ROWS
    lead = (PROMPT + EARLY * CONT_LEN) // ROWS
    first = rows_forward(
        0, lead, count, lengths, place, (ctx_p, ctx_a, oth_p, oth_a), tokens, teacher, fixed, pieces
    )
    kept, stats_a, (wo_oth, wi_oth, wb_oth, b_oth) = list(first[:7]), first[7], first[8:]
    oth_b, kept[0] = tie(oth_b, kept[0])
    *kept, stats_f = rows_forward(
        lead, n_blocks - lead, count, lengths, place, (ctx_b, oth_b), tokens, teacher, fixed,
        (wo_oth, wi_oth, wb_oth, b_oth), kept,
    )
    output, act, gate, gffn, gsec, xlow, rstd = kept
    stats_f = stats_f + stats_a

    def split(keep, got, n):
        return keep[n:] + got[n:], keep[:n] + got[:n]

    w_fixed = (w_out, w_in, wi_oth, w_back, wb_oth, norm_gain, norm_bias, stats_f)
    b_send = grad_back(1, place, act, gffn)
    b_got = hop(b_send, 0)
    b_keep = grad_back(0, place, act, gffn, after=(b_send,))
    b_got, b_keep = tie(b_got, b_keep)
    b_out, b_keep = split(b_keep, b_got, 2)
    b_got = turn(b_out, 0)
    ghid, gattn, gctx, gfin_half, stats = rows_backward(
        0, SLOTS // BACK_ROWS, place, gate, gffn, gsec, xlow, rstd, w_fixed, after=(b_out, b_keep)
    )
    b_got, ghid = tie(b_got, ghid)
    b_out, b_keep = split(b_keep, b_got, 1)
    b_got = turn(b_out, 1)
    other_stats = swap(stats)
    i_send, i_keep = grad_in(place, xlow, ghid, after=(b_out, b_keep))
    b_got, other_stats, i_send = tie(b_got, other_stats, i_send)
    b_top, b_end = b_keep[:, :96] + b_got[:, :96], b_keep[:, 96:] + b_got[:, 96:]
    b_got = hop(b_top, 3)
    i_got = hop(i_send, 0)
    gq, gk, gv, gkp, gvp = cont_backward(
        q, k, v, probs_c, gctx, ctx_a, inv_a, ctx_b, inv_b, after=(b_top, b_end)
    )
    i_got, b_got, gq = tie(i_got, b_got, gq)
    i_out, i_keep = split(i_keep, i_got, 2)
    i_got = turn(i_out, 0)
    b_more = hop(b_end, 3)
    gq, gk, gv = prompt_backward(
        q, k, v, probs_p, gctx, ctx_p, inv_p, gkp, gvp, gq, gk, gv, after=(i_out, i_keep)
    )
    r_send, r_keep = grad_rest(place, tokens, gq, gk, gv, ctx_p, ctx_a, ctx_b, gattn, stats, other_stats)
    i_got, b_more, r_send = tie(i_got, b_more, r_send)
    r_got = hop(r_send, 0)
    i_out, i_keep = split(i_keep, i_got, 1)
    i_got = turn(i_out, 1)
    b_total = far_exchange(jnp.concatenate([b_top + b_got, b_end + b_more], axis=1))
    b_got = turn(b_total, 1)
    r_got, i_got, b_got = tie(r_got, i_got, b_got)
    r_out, r_keep = split(r_keep, r_got, 2)
    r_got = turn(r_out, 0)
    i_top, i_end = i_keep[:, :48] + i_got[:, :48], i_keep[:, 48:] + i_got[:, 48:]
    i_got = hop(i_top, 3)
    b_two = jnp.concatenate([b_total, b_got], axis=0)
    *sends, keep = input_grad(place, gq, gk, gv, w3, gfin_half, after=(r_out, r_keep, i_top, i_end, b_two))
    r_got, i_got, keep = tie(r_got, i_got, keep)
    swapped = [swap(sends[0])]
    r_out, r_keep = split(r_keep, r_got, 1)
    r_got = turn(r_out, 1)
    i_more = hop(i_end, 3)
    r_got, i_more, swapped[0] = tie(r_got, i_more, swapped[0])
    swapped.append(swap(sends[1]))
    r_total = r_keep + r_got
    r_got = hop(r_total, 3)
    b_got = turn(b_two, 0)
    i_total = far_exchange(jnp.concatenate([i_top + i_got, i_end + i_more], axis=1))
    i_got = turn(i_total, 1)
    r_got, b_got, i_got, swapped[1] = tie(r_got, b_got, i_got, swapped[1])
    swapped.append(swap(sends[2]))
    r_total = far_exchange(r_total + r_got)
    r_got = turn(r_total, 1)
    i_two = jnp.concatenate([i_total, i_got], axis=0)
    i_got = turn(i_two, 0)
    b_near = jnp.concatenate([b_two, b_got], axis=0)
    b_far = hop(b_near, 0)
    r_got, i_got, b_far, b_near, swapped[2] = tie(r_got, i_got, b_far, b_near, swapped[2])
    swapped.append(swap(sends[3]))
    grad_w_back = in_order(1, place, b_far, in_order(0, place, b_near))
    r_two = jnp.concatenate([r_total, r_got], axis=0)
    r_got = turn(r_two, 0)
    r_far = hop(r_two, 0)
    i_near = jnp.concatenate([i_two, i_got], axis=0)
    i_far = hop(i_near, 0)
    grad_w_in = in_order(1, place, i_far, in_order(0, place, i_near, after=(r_two,)))
    rest = order_rest(1, 0, place, r_far, width, order_rest(0, 0, place, r_two, width))
    grad_w_in, swapped[3] = tie(grad_w_in, swapped[3])
    grad_tokens = keep + jnp.concatenate(swapped, axis=0)
    r_got, grad_tokens, grad_w_back, *rest = tie(r_got, grad_tokens, grad_w_back, *rest)
    r_far = hop(r_got, 0)
    rest = order_rest(0, 2, place, r_got, width, rest)
    grad_w3, grad_w_out, rows = order_rest(1, 2, place, r_far, width, rest)
    grad_bias, grad_gain, grad_shift, grad_b_in, grad_qv, loss = small_outputs(count, rows)
    return (
        output,
        logits_p[None],
        logits_c[None],
        grad_tokens,
        jnp.transpose(grad_w3, (1, 0, 2)),
        grad_qv,
        grad_w_out,
        grad_w_in,
        grad_b_in.reshape(units),
        grad_w_back,
        grad_bias,
        grad_gain,
        grad_shift,
        loss.reshape(()),
    )


def solution(mesh):
    in_specs = (
        P("dp", None),
        P("dp", None),
        P("dp", None),
        P("dp", "tensor", None, None),
        P("dp", None, "tensor", None, None),
        P(None, None, "tensor"),
        P(None, "tensor"),
        P("tensor", None),
        P(None, "tensor"),
        P("tensor"),
        P("tensor", None),
        P(),
        P(),
        P(),
    )
    out_specs = (
        P("dp", "tensor"),
        P("dp", "tensor", None, None),
        P("dp", None, "tensor", None, None),
        P("dp", "tensor"),
        P(None, None, "tensor"),
        P(None, "tensor"),
        P("tensor", None),
        P(None, "tensor"),
        P("tensor"),
        P("tensor", None),
        P(),
        P(),
        P(),
        P(),
    )
    return jax.shard_map(local, mesh=mesh, in_specs=in_specs, out_specs=out_specs, check_vma=False)
```

```python
import functools

import jax
import jax.numpy as jnp
from jax import lax
from jax.experimental import pallas as pl
from jax.experimental.pallas import tpu as pltpu
from jax.sharding import PartitionSpec as P

D = 768
HEAD = 64
PROMPT = 512
CONT = 8
CONT_LEN = 128
TOTAL = 576
KEYS = 640
SLOTS = 1536

NEG_FILL = -1e30
EPS_NORM = 1e-12
F32 = jnp.float32
BF16 = jnp.bfloat16
VMEM_CAP = 36 * 1024 * 1024
VMEM_WIDE = 60 * 1024 * 1024
CONT_CAP = 36 * 1024 * 1024
ROWS_CAP = 60 * 1024 * 1024
BACK_CAP = 24 * 1024 * 1024
ROWS = 256
UNITS = 1536
GROUP = 2
BACK_ROWS = 384
EARLY = 2
COST_DIV = 1000


def nn(a, b):
    return lax.dot_general(a, b, (((1,), (0,)), ((), ())), preferred_element_type=F32)


def nt(a, b):
    return lax.dot_general(a, b, (((1,), (1,)), ((), ())), preferred_element_type=F32)


def tn(a, b):
    return lax.dot_general(a, b, (((0,), (0,)), ((), ())), preferred_element_type=F32)


def whole(shape):
    return pl.BlockSpec(shape, lambda *_: (0,) * len(shape))


def const(a):
    return pl.BlockSpec(a.shape, lambda *_: (0,) * len(a.shape), pipeline_mode=pl.Buffered(1))


ANY = pl.BlockSpec(memory_space=pl.ANY)
IN_HBM = pl.BlockSpec(memory_space=pltpu.HBM)


def params(n, cap):
    return pltpu.CompilerParams(dimension_semantics=("arbitrary",) * n, vmem_limit_bytes=cap)


def cost(flops, nbytes, trans=0):
    return pl.CostEstimate(flops=int(flops / COST_DIV), bytes_accessed=int(nbytes / COST_DIV), transcendentals=0)


def run(kernel, operands, in_specs, out_specs, out_shape, grid, name, estimate, scalars=0, scratch=(),
        aliases=None, after=(), cap=VMEM_CAP):
    n, m = len(operands), len(after)

    def body(*refs):
        kernel(*refs[:n], *refs[n + m :])

    return pl.pallas_call(
        body,
        name=name,
        grid_spec=pltpu.PrefetchScalarGridSpec(
            num_scalar_prefetch=scalars,
            grid=grid,
            in_specs=list(in_specs) + [ANY] * m,
            out_specs=out_specs,
            scratch_shapes=scratch,
        ),
        out_shape=out_shape,
        input_output_aliases=aliases or {},
        compiler_params=params(len(grid), cap),
        cost_estimate=estimate,
    )(*operands, *after)


def qkv_kernel(tok, w, bias, q, k, v):
    x = tok[...]
    q[...] = (nn(x, w[0]) + bias[0:1]).astype(BF16) * jnp.asarray(0.125, BF16)
    k[...] = nn(x, w[1]).astype(BF16)
    v[...] = (nn(x, w[2]) + bias[1:2]).astype(BF16)


def project(tokens, w3, bias_qv):
    width = w3.shape[2]
    rows = 512
    spec = pl.BlockSpec((rows, width), lambda i: (i, 0))
    out = jax.ShapeDtypeStruct((SLOTS, width), BF16)
    return pl.pallas_call(
        qkv_kernel,
        name="qkv_proj",
        grid=(SLOTS // rows,),
        in_specs=[
            pl.BlockSpec((rows, D), lambda i: (i, 0)),
            whole((3, D, width)),
            whole((2, width)),
        ],
        out_specs=[spec] * 3,
        out_shape=[out] * 3,
        compiler_params=params(1, VMEM_CAP),
        cost_estimate=cost(2 * SLOTS * D * 3 * width, 2 * (SLOTS * D + 3 * D * width + 3 * SLOTS * width)),
    )(tokens, w3, bias_qv)


def half_mask(rows, h):
    lane = lax.broadcasted_iota(jnp.int32, (rows, 128), 1)
    return lane < HEAD if h == 0 else lane >= HEAD


def only(x, h):
    return jnp.where(half_mask(x.shape[0], h), x, jnp.zeros_like(x))


def pair(h):
    return slice(h // 2 * 128, h // 2 * 128 + 128)


def parts(groups):
    return [slice(g * CONT_LEN, (g + 1) * CONT_LEN) for g in range(groups)]


def own_keys(groups):
    return [slice(PROMPT + g * CONT_LEN, PROMPT + (g + 1) * CONT_LEN) for g in range(groups)]


def fill(kp, vp, kt, vx):
    kt[:, :PROMPT] = kp[...].T
    for p in range(kp.shape[1] // 128):
        vx[p, :PROMPT, :128] = vp[:, p * 128 : (p + 1) * 128]
        vx[p, :, 128:] = jnp.ones_like(vx[p, :, 128:])


def attend(q, kt, vx, soft, ctx, inv, groups):
    heads = q.shape[1] // HEAD

    def score(h):
        qm = only(q[:, pair(h)], h % 2)
        return nn(qm, kt[pair(h), :PROMPT]), [
            nn(qm[r], kt[pair(h), c]) for r, c in zip(parts(groups), own_keys(groups))
        ]

    def mix(h, e):
        out = nn(e[0], vx[h // 2, :PROMPT])
        if groups:
            out = out + jnp.concatenate(
                [nn(x, vx[h // 2, c]) for x, c in zip(e[1], own_keys(groups))], axis=0
            )
        return out

    s, e, outs = [score(0)], [], []
    for h in range(heads):
        if h + 1 < heads:
            s.append(score(h + 1))
        e.append(soft(h, *s[h]))
        if h:
            outs.append(mix(h - 1, e[h - 1]))
    outs.append(mix(heads - 1, e[-1]))
    mine = half_mask(q.shape[0], 0)
    for h in range(0, heads, 2):
        scale = 1.0 / jnp.where(mine, outs[h][:, 128:], outs[h + 1][:, 128:])
        inv[:, pair(h)] = scale
        ctx[:, pair(h)] = (
            (jnp.where(mine, outs[h][:, :128], outs[h + 1][:, :128]) * scale).astype(BF16).astype(F32)
        )


def prompt_fwd_kernel(q, k, v, prev, logits, weights, ctx, inv, kt, vx):
    @pl.when(pl.program_id(0) == 0)
    def _():
        fill(k, v, kt, vx)

    def soft(h, s, _):
        x = s + prev[h].astype(F32)
        logits[h] = x.astype(BF16)
        e = jnp.exp(x - jnp.max(x, axis=-1, keepdims=True)).astype(BF16)
        weights[h] = e
        return e, []

    attend(q[...], kt, vx, soft, ctx, inv, 0)


def prompt_forward(q, k, v, prev, after=()):
    heads = prev.shape[0]
    width = heads * HEAD
    rows = 256
    big = pl.BlockSpec((heads, rows, PROMPT), lambda r: (0, r, 0))
    row = pl.BlockSpec((rows, width), lambda r: (r, 0))
    front = pl.BlockSpec((PROMPT, width), lambda r: (0, 0))
    shape = jax.ShapeDtypeStruct((heads, PROMPT, PROMPT), BF16)
    n = heads * PROMPT * PROMPT
    return run(
        prompt_fwd_kernel,
        (q, k, v, prev),
        [row, front, front, big],
        [big, big, row, row],
        [shape, shape] + [jax.ShapeDtypeStruct((PROMPT, width), F32)] * 2,
        (PROMPT // rows,),
        "attn_prompt_fwd",
        cost(4 * n * HEAD, 6 * n, n),
        scratch=[pltpu.VMEM((width, PROMPT), BF16), pltpu.VMEM((heads // 2, PROMPT, 256), BF16)],
        after=after,
    )


def cont_fwd_kernel(c0, lens, q, kp, vp, ko, vo, prev, *refs):
    logits, weights, ctx, inv, kt, vx = refs[-6:]

    @pl.when(pl.program_id(0) == 0)
    def _():
        fill(kp, vp, kt, vx)

    kt[:, PROMPT:] = ko[...].T
    for p in range(ko.shape[1] // 128):
        vx[p, PROMPT:, :128] = vo[:, p * 128 : (p + 1) * 128]
    column = lax.broadcasted_iota(jnp.int32, (CONT_LEN, CONT_LEN), 1)
    first = c0 + pl.program_id(0) * GROUP
    live = [column < lens[0, first + g] for g in range(GROUP)]

    def soft(h, s1, s2):
        front, own = [], []
        for g, r in enumerate(parts(GROUP)):
            a = s1[r] + prev[g, h, :, :PROMPT].astype(F32)
            b = s2[g] + prev[g, h, :, PROMPT:].astype(F32)
            logits[g, h, :, :PROMPT] = a.astype(BF16)
            logits[g, h, :, PROMPT:] = b.astype(BF16)
            b = jnp.where(live[g], b, NEG_FILL)
            top = jnp.maximum(
                jnp.max(a, axis=-1, keepdims=True), jnp.max(b, axis=-1, keepdims=True)
            )
            front.append(jnp.exp(a - top).astype(BF16))
            own.append(jnp.exp(b - top).astype(BF16))
            weights[g, h, :, :PROMPT] = front[g]
            weights[g, h, :, PROMPT:] = own[g]
        return jnp.concatenate(front, axis=0), own

    attend(q[...], kt, vx, soft, ctx, inv, GROUP)


def cont_forward(c0, n, lens, q, k, v, prev, earlier=(), after=()):
    heads = prev.shape[1]
    width = heads * HEAD
    rows = GROUP * CONT_LEN
    first, at = (PROMPT // CONT_LEN + c0) // GROUP, c0 // GROUP
    own = pl.BlockSpec((rows, width), lambda c, *_: (c + first, 0))
    front = pl.BlockSpec((PROMPT, width), lambda c, *_: (0, 0))
    big = pl.BlockSpec((GROUP, heads, CONT_LEN, KEYS), lambda c, *_: (c + at, 0, 0, 0))
    row = pl.BlockSpec((rows, width), lambda c, *_: (c, 0))
    shape = jax.ShapeDtypeStruct((CONT, heads, CONT_LEN, KEYS), BF16)
    size = n * heads * CONT_LEN * KEYS
    return run(
        functools.partial(cont_fwd_kernel, c0),
        (lens, q, k, v, k, v, prev, *earlier),
        [own, front, front, own, own, big] + [ANY] * len(earlier),
        [big, big, row, row],
        [shape, shape] + [jax.ShapeDtypeStruct((n * CONT_LEN, width), F32)] * 2,
        (n // GROUP,),
        "attn_cont_fwd",
        cost(4 * size * HEAD, 6 * size, size),
        cap=CONT_CAP,
        scalars=1,
        scratch=[
            pltpu.VMEM((width, PROMPT + rows), BF16),
            pltpu.VMEM((heads // 2, PROMPT + rows, 256), BF16),
        ],
        aliases={7 + m: m for m in range(len(earlier))},
        after=after,
    )


def hop(x, bit):
    n = lax.axis_size("dp")
    return lax.ppermute(x, "dp", [(i, i ^ (1 << bit)) for i in range(n)])


def turn(x, step):
    n = lax.axis_size("dp")
    return lax.ppermute(x, "dp", [(i, i ^ (4 if (i & 1) ^ step else 2)) for i in range(n)])


def grad_back_kernel(flip, place, act, gffn, out):
    acc = tn(act[...], gffn[...])
    low = place[2] if flip else place[1]
    for m in range(2):
        out[pl.ds(jnp.bitwise_xor(low % 2, m), 1)] = acc[None, 192 * m : 192 * m + 192]


def grad_back(flip, place, act, gffn, after=()):
    low = lambda place: (place[2] if flip else place[1]) // 2 % 2
    return run(
        functools.partial(grad_back_kernel, flip),
        (place, act, gffn),
        [
            pl.BlockSpec((SLOTS, 384), lambda i, place: (0, 2 * ((place[1] // 4 + flip) % 2) + i)),
            whole((SLOTS, D)),
        ],
        pl.BlockSpec((2, 192, D), lambda i, place: (jnp.bitwise_xor(i, low(place)), 0, 0)),
        jax.ShapeDtypeStruct((4, 192, D), F32),
        (2,),
        "grad_w_back",
        cost(2 * SLOTS * 768 * D, 2 * SLOTS * 768 * 2 + 4 * 768 * D),
        cap=BACK_CAP,
        scalars=1,
        after=after,
    )


IN_BLOCK = 512


def grad_in_kernel(n, place, x, ghid, send, keep, xt):
    i = pl.program_id(0)

    @pl.when(i % n == 0)
    def _():
        xt[...] = x[...].T

    acc = nn(xt[...], ghid[...])

    def put(out, low):
        for m in range(4):
            out[pl.ds(jnp.bitwise_xor(low, m), 1)] = acc[None, 96 * m : 96 * m + 96]

    pl.when(i < n)(lambda: put(send, place[2]))
    pl.when(i >= n)(lambda: put(keep, place[1] % 4))


def grad_in(place, xlow, ghid, after=()):
    units = ghid.shape[1]
    n = units // IN_BLOCK
    shape = jax.ShapeDtypeStruct((4, 96, units), F32)
    return run(
        functools.partial(grad_in_kernel, n),
        (place, xlow, ghid),
        [
            pl.BlockSpec((SLOTS, 384), lambda i, place: (0, (place[1] // 4 + 1 - i // n) % 2)),
            pl.BlockSpec((SLOTS, IN_BLOCK), lambda i, *_: (0, i % n)),
        ],
        [
            pl.BlockSpec((4, 96, IN_BLOCK), lambda i, *_: (0, 0, jnp.minimum(i, n - 1))),
            pl.BlockSpec((4, 96, IN_BLOCK), lambda i, *_: (0, 0, jnp.maximum(i - n, 0))),
        ],
        [shape] * 2,
        (2 * n,),
        "grad_w_in",
        cost(4 * SLOTS * 384 * units, 2 * SLOTS * (768 + 2 * units) + 8 * 384 * units),
        scalars=1,
        scratch=[pltpu.VMEM((384, SLOTS), BF16)],
        after=after,
    )


def grad_rest_kernel(place, tok, gq, gk, gv, ctx_p, ctx_a, ctx_b, gattn, stats, other, *refs):
    send, keep, ao = refs
    i = pl.program_id(0)
    left = (place[1] // 4 + 1 - i) % 2 == 0

    @pl.when(i == 0)
    def _():
        ctx = jnp.concatenate([ctx_p[...], ctx_a[...], ctx_b[...]], axis=0).astype(BF16)
        ao[...] = nn(ctx.T, gattn[...])

    tok_t = tok[...].T
    aq = nn(tok_t, gq[...])
    ak = nn(tok_t, gk[...])
    av = nn(tok_t, gv[...])
    o = jnp.where(left, ao[:192], ao[192:])
    bias = jnp.concatenate(
        [jnp.sum(g[...].astype(F32), axis=0, keepdims=True) for g in (gq, gv)], axis=1
    )
    row = lax.broadcasted_iota(jnp.int32, (16, D), 0)
    half_of = lax.broadcasted_iota(jnp.int32, (16, D), 1) // (D // 2)
    small = jnp.where((half_of == place[0]) | (row >= 7), stats[...], other[...])
    small = jnp.where(row == 9, bias, small)

    def put(out, low):
        for m in range(4):
            j = jnp.bitwise_xor(low, m)
            out[pl.ds(j, 1), 0:96, 0:384] = aq[None, 96 * m : 96 * m + 96]
            out[pl.ds(j, 1), 0:96, 384:768] = ak[None, 96 * m : 96 * m + 96]
            out[pl.ds(j, 1), 96:144, 0:384] = av[None, 96 * m : 96 * m + 48]
            out[pl.ds(j, 1), 96:144, 384:768] = av[None, 96 * m + 48 : 96 * m + 96]
            out[pl.ds(j, 1), 144:192, :] = o[None, 48 * m : 48 * m + 48]
            out[pl.ds(j, 1), 192:200, :] = jnp.concatenate(
                [
                    jnp.where(left, small[2 * m : 2 * m + 2], small[8 + 2 * m : 10 + 2 * m]),
                    jnp.zeros((6, D), F32),
                ],
                axis=0,
            )[None]

    pl.when(i == 0)(lambda: put(send, place[2]))
    pl.when(i == 1)(lambda: put(keep, place[1] % 4))


def grad_rest(place, tokens, gq, gk, gv, ctx_p, ctx_a, ctx_b, gattn, stats, other, after=()):
    width = gq.shape[1]
    shape = jax.ShapeDtypeStruct((4, 200, D), F32)
    fixed = (gq, gk, gv, ctx_p, ctx_a, ctx_b, gattn, stats, other)
    return run(
        grad_rest_kernel,
        (place, tokens) + fixed,
        [pl.BlockSpec((SLOTS, 384), lambda i, place: (0, (place[1] // 4 + 1 - i) % 2))]
        + [const(x) for x in fixed],
        [const(shape)] * 2,
        [shape] * 2,
        (2,),
        "grad_w_rest",
        cost(2 * SLOTS * (D * 3 * width + width * D), 2 * SLOTS * (6 * width + 2 * D)),
        scalars=1,
        scratch=[pltpu.VMEM((width, D), F32)],
        after=after,
    )


def chunk_of(place, far, m):
    if far:
        return (1 - place[1] // 4) * 4 + jnp.bitwise_xor(place[2], m)
    return jnp.bitwise_xor(place[1], m)


def staged(moves):
    for first, _ in moves:
        first.start()
    for first, rest in moves:
        first.wait()
        for c in rest:
            c.start()
    for _, rest in moves:
        for c in rest:
            c.wait()


def order_kernel(rows, far, place, src, *refs):
    out, hold, sems_in, sems_out = refs[-4:]
    moves = []
    for m in range(4):
        at = pl.multiple_of(chunk_of(place, far, m) * rows, 8)
        moves.append(
            (
                pltpu.make_async_copy(src.at[m], hold.at[m], sems_in.at[m]),
                [pltpu.make_async_copy(hold.at[m], out.at[pl.ds(at, rows)], sems_out.at[m])],
            )
        )
    staged(moves)


def in_order(far, place, chunks, prev=None, after=()):
    _, rows, cols = chunks.shape
    return run(
        functools.partial(order_kernel, rows, far),
        (place, chunks) + (() if prev is None else (prev,)),
        [ANY] * (1 if prev is None else 2),
        ANY,
        jax.ShapeDtypeStruct((8 * rows, cols), F32),
        (1,),
        "in_order",
        cost(0, 8 * chunks.size),
        scalars=1,
        scratch=[pltpu.VMEM(chunks.shape, F32), pltpu.SemaphoreType.DMA((4,)), pltpu.SemaphoreType.DMA((4,))],
        aliases={} if prev is None else {2: 0},
        after=after,
    )


def order_rest_kernel(far, first, width, place, src, *refs):
    gw, go, small, hold, sems_in, sems_out = refs[-6:]
    moves, n = [], 0

    def copy(a, b):
        nonlocal n
        n += 1
        return pltpu.make_async_copy(a, b, sems_out.at[n - 1])

    left, right = pl.ds(0, width), pl.ds(width, width)
    for m in range(2):
        c = chunk_of(place, far, first + m)
        rows = hold.at[m]
        wide = pl.ds(pl.multiple_of(c * 96, 8), 96)
        out = [
            copy(rows.at[pl.ds(0, 96), left], gw.at[0, wide]),
            copy(rows.at[pl.ds(0, 96), right], gw.at[1, wide]),
            copy(rows.at[pl.ds(96, 48), left], gw.at[2, pl.ds(pl.multiple_of(c * 96, 8), 48)]),
            copy(rows.at[pl.ds(96, 48), right], gw.at[2, pl.ds(pl.multiple_of(c * 96 + 48, 8), 48)]),
            copy(rows.at[pl.ds(144, 48)], go.at[pl.ds(pl.multiple_of(c * 48, 8), 48)]),
            copy(rows.at[pl.ds(192, 8)], small.at[pl.ds(pl.multiple_of(c * 8, 8), 8)]),
        ]
        moves.append((pltpu.make_async_copy(src.at[m], rows, sems_in.at[m]), out))
    staged(moves)


def order_rest(far, first, place, chunks, width, prev=None, after=()):
    return run(
        functools.partial(order_rest_kernel, far, first, width),
        (place, chunks) + (() if prev is None else tuple(prev)),
        [ANY] * (1 if prev is None else 4),
        [ANY] * 3,
        [
            jax.ShapeDtypeStruct((3, D, width), F32),
            jax.ShapeDtypeStruct((width, D), F32),
            jax.ShapeDtypeStruct((64, D), F32),
        ],
        (1,),
        "order_rest",
        cost(0, 8 * chunks.size),
        scalars=1,
        scratch=[
            pltpu.VMEM(chunks.shape, F32),
            pltpu.SemaphoreType.DMA((2,)),
            pltpu.SemaphoreType.DMA((12,)),
        ],
        aliases={} if prev is None else {2: 0, 3: 1, 4: 2},
        after=after,
    )


def small_kernel(count, rows, bias, gain, shift, b_in, qv, loss):
    row = lambda n: rows[8 * (n // 2) + n % 2 : 8 * (n // 2) + n % 2 + 1]
    bias[0:1], bias[1:2] = row(4), row(1)
    gain[0:1], gain[1:2] = row(5), row(2)
    shift[0:1], shift[1:2] = row(6), row(3)
    b_in[0:1, :D], b_in[0:1, D:] = row(7), row(8)
    qv[0:1], qv[1:2] = row(9)[:, : D // 2], row(9)[:, D // 2 :]
    loss[...] = jnp.sum(row(0), axis=1, keepdims=True) / count


def small_outputs(count, rows):
    shapes = [(2, D)] * 3 + [(1, 2 * D), (2, D // 2), (1, 1)]
    return run(
        functools.partial(small_kernel, count),
        (rows,),
        [whole(rows.shape)],
        [whole(x) for x in shapes],
        [jax.ShapeDtypeStruct(x, F32) for x in shapes],
        (1,),
        "small_outputs",
        cost(0, 8 * rows.size),
    )


def lay_out(place, pieces, wi, wo, wb, b, stage_a, stage_b, sems):
    moves = []
    for far in range(2):
        own_a, rest_a = pieces[2 * far : 2 * far + 2]
        most_b, cross_b = pieces[4 + 2 * far : 6 + 2 * far]
        for m in range(4):
            k = 4 * far + m
            src_a = own_a if m == 0 else rest_a.at[pl.ds((m - 1) * 128, 128)]
            src_b = cross_b if m == 3 else most_b.at[pl.ds(m * 192, 192)]
            moves.append(pltpu.make_async_copy(src_a, stage_a.at[k], sems.at[k]))
            moves.append(pltpu.make_async_copy(src_b, stage_b.at[k], sems.at[8 + k]))
    for copy in moves:
        copy.start()
    for k in range(8):
        c = jnp.bitwise_xor(place[3], k)
        moves[2 * k].wait()
        wi[pl.ds(pl.multiple_of(c * 96, 16), 96), :] = stage_a[k, 0:96, :].astype(BF16)
        tail = stage_a[k, 96:120, :]
        wo[pl.ds(pl.multiple_of(c * 48, 16), 48), :] = jnp.concatenate(
            [tail[:, :D], tail[:, D:]], axis=0
        ).astype(BF16)
        moves[2 * k + 1].wait()
        wb[pl.ds(pl.multiple_of(c * 192, 16), 192), :] = stage_b[k].astype(BF16)
    b[...] = stage_a[0, 120:128, :]


def forward_kernel(first_block, count, has_prev, *refs):
    lens, place = refs[:2]
    if has_prev:
        ctx_own, ctx_oth, tok, teach, wo_own, wi_own, wb_own, b_own, bias_out, gain, shift = refs[2:13]
        wo_oth, wi_oth, wb_oth, b_oth = refs[13:17]
        out, act, gate, gffn, gsec, xlow, rstd, stats = refs[-8:]
        own, oth = ctx_own[...], ctx_oth[...]
    else:
        ctx_p, ctx_a, oth_p, oth_a, tok, teach, wo_own, wi_own, wb_own, b_own, bias_out, gain, shift = refs[2:15]
        pieces = refs[15:23]
        out, act, gate, gffn, gsec, xlow, rstd, stats, wo_oth, wi_oth, wb_oth, b_oth = refs[-15:-3]
        early = pl.program_id(0) < PROMPT // ROWS
        own = jnp.where(early, ctx_p[...], ctx_a[...])
        oth = jnp.where(early, oth_p[...], oth_a[...])

        @pl.when(pl.program_id(0) == 0)
        def _():
            lay_out(place, pieces, wi_oth, wo_oth, wb_oth, b_oth, *refs[-3:])

    i = pl.program_id(0)
    blk = i + first_block
    n_own = wi_own.shape[1] // UNITS

    @pl.when(i == 0)
    def _():
        stats[...] = jnp.zeros_like(stats)

    attn = nn(own.astype(BF16), wo_own[...]) + nn(oth.astype(BF16), wo_oth[...])
    fin = tok[...].astype(F32) + attn + bias_out[0:1]
    c1 = fin - jnp.mean(fin, axis=-1, keepdims=True)
    r1 = lax.rsqrt(jnp.mean(c1 * c1, axis=-1, keepdims=True) + EPS_NORM)
    rstd[...] = jnp.broadcast_to(r1, rstd.shape)
    first = c1 * r1 * gain[0:1] + shift[0:1]
    x = first.astype(BF16)
    xlow[...] = x
    ffn = None
    for side in range(2):
        wi, wb, bb = ((wi_own, wb_own, b_own), (wi_oth, wb_oth, b_oth))[side]
        for u in range(n_own):
            cols = slice(u * UNITS, (u + 1) * UNITS)
            h = nn(x, wi[:, cols]) + bb[0:1, cols]
            cdf = 0.5 + 0.5 * lax.erf(h * 0.7071067811865476)
            pdf = jnp.exp(-0.5 * h * h) * 0.3989422804014327
            a = (h * cdf).astype(BF16)
            at = (side * n_own + u) * UNITS
            gate[:, at : at + UNITS] = (cdf + h * pdf).astype(BF16)
            if side == 0:
                act[:, cols] = a
            part = nn(a, wb[cols, :])
            ffn = part if ffn is None else ffn + part
    sec = first + ffn + bias_out[1:2]
    c2 = sec - jnp.mean(sec, axis=-1, keepdims=True)
    r2 = lax.rsqrt(jnp.mean(c2 * c2, axis=-1, keepdims=True) + EPS_NORM)
    xh2 = c2 * r2
    result = xh2 * gain[1:2] + shift[1:2]
    left = place[0] == 0
    hd = D // 2
    out[...] = jnp.where(left, result[:, :hd], result[:, hd:]).astype(BF16)
    row = lax.broadcasted_iota(jnp.int32, (ROWS, 1), 0)
    per = ROWS // CONT_LEN
    cont0 = (blk - PROMPT // ROWS) * per
    valid = jnp.zeros((ROWS, 1), jnp.bool_)
    for m in range(per):
        length = jnp.where(cont0 < 0, CONT_LEN, lens[0, jnp.maximum(cont0 + m, 0)])
        valid = valid | ((row >= m * CONT_LEN) & (row < m * CONT_LEN + length))
    diff = jnp.where(valid, result - teach[...].astype(F32), 0.0)
    g = diff * (2.0 / count)
    gy = g * gain[1:2]
    g2 = r2 * (
        gy
        - jnp.mean(gy, axis=-1, keepdims=True)
        - xh2 * jnp.mean(gy * xh2, axis=-1, keepdims=True)
    )
    stats[0:1] += jnp.sum(diff * diff, axis=0, keepdims=True)
    stats[1:2] += jnp.sum(g2, axis=0, keepdims=True)
    stats[2:3] += jnp.sum(g * xh2, axis=0, keepdims=True)
    stats[3:4] += jnp.sum(g, axis=0, keepdims=True)
    gsec[...] = g2
    gffn[...] = g2.astype(BF16)


def rows_forward(first_block, blocks, count, lens, place, ctxs, tok, teach, fixed, more, prev=None, after=()):
    width = ctxs[0].shape[1]
    units = fixed[1].shape[1]
    row = lambda w: pl.BlockSpec((ROWS, w), lambda i, *_: (i + first_block, 0))
    split = PROMPT // ROWS
    if prev is None:
        low = pl.BlockSpec((ROWS, width), lambda i, *_: (jnp.minimum(i, split - 1), 0))
        high = pl.BlockSpec((ROWS, width), lambda i, *_: (jnp.maximum(i - split, 0), 0))
        ctx_specs = [low, high, low, high]
    else:
        ctx_specs = [pl.BlockSpec((ROWS, width), lambda i, *_: (i, 0))] * 2
    shapes = [(D // 2, BF16), (units, BF16), (2 * units, BF16), (D, BF16), (D, F32), (D, BF16), (128, F32)]
    operands = [lens, place, *ctxs, tok, teach, *fixed, *more]
    specs = ctx_specs + [row(D), row(D)] + [const(a) for a in fixed]
    specs += [IN_HBM if prev is None else const(a) for a in more]
    aliases, scratch = {}, []
    out_specs = [row(w) for w, _ in shapes] + [whole((16, D))]
    out_shape = [jax.ShapeDtypeStruct((SLOTS, w), t) for w, t in shapes] + [jax.ShapeDtypeStruct((16, D), F32)]
    if prev is None:
        weights = [
            jax.ShapeDtypeStruct((width, D), BF16),
            jax.ShapeDtypeStruct((D, units), BF16),
            jax.ShapeDtypeStruct((units, D), BF16),
            jax.ShapeDtypeStruct((8, units), F32),
        ]
        out_specs, out_shape = out_specs + [const(w) for w in weights], out_shape + weights
        scratch = [
            pltpu.VMEM((8, 128, units), F32),
            pltpu.VMEM((8, 192, D), F32),
            pltpu.SemaphoreType.DMA((16,)),
        ]
    else:
        aliases = {len(operands) + n: n for n in range(7)}
        operands, specs = operands + list(prev), specs + [ANY] * 7
    return run(
        functools.partial(forward_kernel, first_block, count, prev is not None),
        operands,
        specs,
        out_specs,
        out_shape,
        (blocks,),
        "rows_forward",
        cap=ROWS_CAP,
        scratch=scratch,
        estimate=cost(2 * blocks * ROWS * D * (4 * units + 2 * width), 8 * D * units + blocks * ROWS * 24000),
        scalars=2,
        aliases=aliases,
        after=after,
    )


def backward_kernel(place, gate, gffn, gsec, xlow, rstd, wo, wi_own, wi_oth, wb_own, wb_oth, gain, shift,
                    stats_f, *refs):
    ghid, gattn, gctx, gfin, stats, gbin = refs[-6:]
    i = pl.program_id(0)
    n_own = wi_own.shape[1] // UNITS

    @pl.when(i == 0)
    def _():
        stats[...] = stats_f[...]
        gbin[0:1, :D] = stats_f[7:8]
        gbin[0:1, D:] = stats_f[8:9]

    gf = gffn[...]
    gfirst = gsec[...]
    for side in range(2):
        wi, wb = ((wi_own, wb_own), (wi_oth, wb_oth))[side]
        for u in range(n_own):
            cols = slice(u * UNITS, (u + 1) * UNITS)
            at = (side * n_own + u) * UNITS
            gh = (nt(gf, wb[cols, :]) * gate[:, at : at + UNITS].astype(F32)).astype(BF16)
            if side == 0:
                ghid[:, cols] = gh
                gbin[0:1, cols] += jnp.sum(gh.astype(F32), axis=0, keepdims=True)
            gfirst = gfirst + nt(gh, wi[:, cols])
    xh1 = (xlow[...].astype(F32) - shift[0:1]) * (1.0 / gain[0:1])
    gy1 = gfirst * gain[0:1]
    g1 = rstd[:, 0:1] * (
        gy1
        - jnp.mean(gy1, axis=-1, keepdims=True)
        - xh1 * jnp.mean(gy1 * xh1, axis=-1, keepdims=True)
    )
    stats[4:5] += jnp.sum(g1, axis=0, keepdims=True)
    stats[5:6] += jnp.sum(gfirst * xh1, axis=0, keepdims=True)
    stats[6:7] += jnp.sum(gfirst, axis=0, keepdims=True)

    @pl.when(i == pl.num_programs(0) - 1)
    def _():
        stats[7:8] = gbin[0:1, :D]
        stats[8:9] = gbin[0:1, D:]

    hd = D // 2
    gfin[...] = jnp.where(place[0] == 0, g1[:, :hd], g1[:, hd:])
    ga1 = g1.astype(BF16)
    gattn[...] = ga1
    gctx[...] = nt(ga1, wo[...]).astype(BF16)


def rows_backward(first, blocks, place, gate, gffn, gsec, xlow, rstd, fixed, prev=None, after=()):
    wo, wi_own = fixed[:2]
    width, units = wo.shape[0], wi_own.shape[1]
    row = lambda w: pl.BlockSpec((BACK_ROWS, w), lambda i, *_: (i + first, 0))
    shapes = [(units, BF16), (D, BF16), (width, BF16), (D // 2, F32)]
    operands = [place, gate, gffn, gsec, xlow, rstd] + list(fixed)
    specs = [row(2 * units), row(D), row(D), row(D), row(128)] + [const(a) for a in fixed]
    aliases = {}
    if prev is not None:
        aliases = {len(operands) + n: n for n in range(4)}
        operands, specs = operands + list(prev), specs + [ANY] * 4
    return run(
        backward_kernel,
        operands,
        specs,
        [row(w) for w, _ in shapes] + [whole((16, D))],
        [jax.ShapeDtypeStruct((SLOTS, w), t) for w, t in shapes] + [jax.ShapeDtypeStruct((16, D), F32)],
        (blocks,),
        "rows_backward",
        cost(2 * SLOTS * D * (4 * units + width), 8 * D * units + SLOTS * 20000),
        scalars=1,
        scratch=[pltpu.VMEM((8, units), F32)],
        aliases=aliases,
        after=after,
    )


def attend_back(q, gctx, ctx, inv, load, vt, kall, gq, take, groups):
    heads = q.shape[1] // HEAD
    g2, inner, qt, gt = [], [], [], []
    for p in range(heads // 2):
        cols = pair(2 * p)
        g = (gctx[:, cols].astype(F32) * inv[:, cols]).astype(BF16)
        prod = g.astype(F32) * ctx[:, cols]
        g2.append(g)
        qt.append(q[:, cols].T)
        gt.append(g.T)
        inner += [jnp.sum(only(prod, h), axis=-1, keepdims=True) for h in range(2)]

    def weigh(h):
        gm = only(g2[h // 2], h % 2)
        return nn(gm, vt[pair(h), :PROMPT]), [
            nn(gm[r], vt[pair(h), c]) for r, c in zip(parts(groups), own_keys(groups))
        ]

    def finish(h, e, l):
        part = slice(h % 2 * HEAD, (h % 2 + 1) * HEAD)
        q_h, g_h = qt[h // 2][part], gt[h // 2][part]
        dq = nn(l[0], kall[:PROMPT, pair(h)])
        own = []
        if groups:
            dq = dq + jnp.concatenate(
                [nn(x, kall[c, pair(h)]) for x, c in zip(l[1], own_keys(groups))], axis=0
            )
            own = [
                (nn(q_h[:, r], x), nn(g_h[:, r], y))
                for r, x, y in zip(parts(groups), l[1], e[1])
            ]
        return dq, (nn(q_h, l[0]), nn(g_h, e[0])), own

    mine = half_mask(q.shape[0], 0)
    done = []

    def flush(h):
        done.append(finish(h, *held[h]))
        if h % 2:
            a, b = done[h - 1], done[h]
            gq[:, pair(h)] = (jnp.where(mine, a[0], b[0]) * 0.125).astype(BF16)
            both = lambda x, y: tuple(jnp.concatenate(z, axis=0) for z in zip(x, y))
            take(pair(h), both(a[1], b[1]), [both(x, y) for x, y in zip(a[2], b[2])])

    raw, held = [weigh(0)], []
    for h in range(heads):
        if h + 1 < heads:
            raw.append(weigh(h + 1))
        e = load(h)
        l = [(e[0].astype(F32) * (raw[h][0] - inner[h])).astype(BF16)]
        l.append(
            [
                (y.astype(F32) * (x - inner[h][r])).astype(BF16)
                for y, x, r in zip(e[1], raw[h][1], parts(groups))
            ]
        )
        held.append((e, l))
        if h:
            flush(h - 1)
    flush(heads - 1)


def cont_bwd_kernel(split, q, kp, vp, ko, vo, weights, gctx, ctx_a, inv_a, ctx_b, inv_b,
                    gq, gk, gv, gkp, gvp, vt, kall):
    early = pl.program_id(0) < split
    ctx = jnp.where(early, ctx_a[...], ctx_b[...])
    inv = jnp.where(early, inv_a[...], inv_b[...])

    @pl.when(pl.program_id(0) == 0)
    def _():
        gkp[...] = jnp.zeros_like(gkp)
        gvp[...] = jnp.zeros_like(gvp)
        vt[:, :PROMPT] = vp[...].T
        kall[:PROMPT] = kp[...]

    vt[:, PROMPT:] = vo[...].T
    kall[PROMPT:] = ko[...]

    def load(h):
        return (
            jnp.concatenate([weights[g, h, :, :PROMPT] for g in range(GROUP)], axis=0),
            [weights[g, h, :, PROMPT:] for g in range(GROUP)],
        )

    def take(cols, front, own):
        gkp[cols, :] += front[0]
        gvp[cols, :] += front[1]
        for r, (dk, dv) in zip(parts(GROUP), own):
            gk[r, cols] = dk.T.astype(BF16)
            gv[r, cols] = dv.T.astype(BF16)

    attend_back(q[...], gctx[...], ctx, inv, load, vt, kall, gq, take, GROUP)


def cont_backward(q, k, v, weights, gctx, ctx_a, inv_a, ctx_b, inv_b, after=()):
    heads = weights.shape[1]
    width = heads * HEAD
    rows = GROUP * CONT_LEN
    first = PROMPT // rows
    own = pl.BlockSpec((rows, width), lambda c: (c + first, 0))
    front = pl.BlockSpec((PROMPT, width), lambda c: (0, 0))
    big = pl.BlockSpec((GROUP, heads, CONT_LEN, KEYS), lambda c: (c, 0, 0, 0))
    shape = jax.ShapeDtypeStruct((SLOTS, width), BF16)
    sums = jax.ShapeDtypeStruct((width, PROMPT), F32)
    n = CONT * heads * CONT_LEN * KEYS
    split = ctx_a.shape[0] // rows
    head = pl.BlockSpec((rows, width), lambda c: (jnp.minimum(c, split - 1), 0))
    tail = pl.BlockSpec((rows, width), lambda c: (jnp.maximum(c - split, 0), 0))
    return run(
        functools.partial(cont_bwd_kernel, split),
        (q, k, v, k, v, weights, gctx, ctx_a, inv_a, ctx_b, inv_b),
        [own, front, front, own, own, big, own, head, head, tail, tail],
        [own, own, own, whole((width, PROMPT)), whole((width, PROMPT))],
        [shape, shape, shape, sums, sums],
        (CONT // GROUP,),
        "attn_cont_bwd",
        cost(8 * n * HEAD, 2 * n + 8 * SLOTS * heads * HEAD * 2),
        scratch=[pltpu.VMEM((width, PROMPT + rows), BF16), pltpu.VMEM((PROMPT + rows, width), BF16)],
        after=after,
    )


def prompt_bwd_kernel(q, k, v, weights, gctx, ctx, inv, gkp, gvp, a, b, c, gq, gk, gv, vt, ak, av):
    r = pl.program_id(0)

    @pl.when(r == 0)
    def _():
        vt[...] = v[...].T
        ak[...] = gkp[...]
        av[...] = gvp[...]

    def take(cols, front, own):
        ak[cols, :] += front[0]
        av[cols, :] += front[1]

    attend_back(q[...], gctx[...], ctx[...], inv[...], lambda h: (weights[h], []), vt, k, gq, take, 0)

    @pl.when(r == pl.num_programs(0) - 1)
    def _():
        gk[...] = ak[...].T.astype(BF16)
        gv[...] = av[...].T.astype(BF16)


def prompt_backward(q, k, v, weights, gctx, ctx, inv, gkp, gvp, gq, gk, gv, after=()):
    heads = weights.shape[0]
    width = heads * HEAD
    rows = 256
    row = pl.BlockSpec((rows, width), lambda r: (r, 0))
    front = pl.BlockSpec((PROMPT, width), lambda r: (0, 0))
    acc = whole((width, PROMPT))
    shape = jax.ShapeDtypeStruct((SLOTS, width), BF16)
    n = heads * PROMPT * PROMPT
    return run(
        prompt_bwd_kernel,
        (q, k, v, weights, gctx, ctx, inv, gkp, gvp, gq, gk, gv),
        [row, front, front, pl.BlockSpec((heads, rows, PROMPT), lambda r: (0, r, 0)), row, row, row, acc, acc]
        + [ANY] * 3,
        [row, front, front],
        [shape] * 3,
        (PROMPT // rows,),
        "attn_prompt_bwd",
        cost(8 * n * HEAD, 2 * n + 8 * PROMPT * heads * HEAD * 2),
        scratch=[
            pltpu.VMEM((width, PROMPT), BF16),
            pltpu.VMEM((width, PROMPT), F32),
            pltpu.VMEM((width, PROMPT), F32),
        ],
        aliases={9: 0, 10: 1, 11: 2},
        after=after,
    )


def input_grad_kernel(place, gq, gk, gv, w, base, *refs):
    sends, keep = refs[:-1], refs[-1]
    hd = D // 2
    mine = place[0] == 0
    part = nt(gq[...], w[0]) + nt(gk[...], w[1]) + nt(gv[...], w[2])
    keep[...] = base[...] + jnp.where(mine, part[:, :hd], part[:, hd:])
    away = jnp.where(mine, part[:, hd:], part[:, :hd])

    def put(send):
        send[...] = away

    per = SLOTS // part.shape[0] // len(sends)
    for n, send in enumerate(sends):
        pl.when(pl.program_id(0) // per == n)(functools.partial(put, send))


def input_grad(place, gq, gk, gv, w3, base, after=()):
    width = w3.shape[2]
    rows, cuts = 384, 4
    per = SLOTS // rows // cuts
    row = lambda w: pl.BlockSpec((rows, w), lambda i, *_: (i, 0))
    cut = lambda n: pl.BlockSpec((rows, D // 2), lambda i, *_: (jnp.clip(i - n * per, 0, per - 1), 0))
    return run(
        input_grad_kernel,
        (place, gq, gk, gv, w3, base),
        [row(width)] * 3 + [whole((3, D, width)), row(D // 2)],
        [cut(n) for n in range(cuts)] + [row(D // 2)],
        [jax.ShapeDtypeStruct((SLOTS // cuts, D // 2), F32)] * cuts + [jax.ShapeDtypeStruct((SLOTS, D // 2), F32)],
        (SLOTS // rows,),
        "input_grad",
        cost(2 * SLOTS * D * 3 * width, 2 * (SLOTS * 3 * width) + 6 * SLOTS * D),
        scalars=1,
        after=after,
    )


def swap(x):
    n = lax.axis_size("tensor")
    return lax.ppermute(x, "tensor", [(i, n - 1 - i) for i in range(n)])


def tie(*values):
    return lax.optimization_barrier(values)


def far_exchange(total):
    bit = 4
    while (1 << bit) < lax.axis_size("dp"):
        total = total + hop(total, bit)
        bit += 1
    return total


def local(
    tokens, teacher, lengths, prev_prompt, prev_cont, w_qkv, bias_qv, w_out, w_in, b_in, w_back,
    bias_out, norm_gain, norm_bias,
):
    width = w_qkv.shape[2]
    units = w_in.shape[1]
    w3 = jnp.transpose(w_qkv, (1, 0, 2))
    t = lax.axis_index("tensor").astype(jnp.int32)
    i = lax.axis_index("dp").astype(jnp.int32)
    core, x, z = i % 2, (i // 2) % 2, (i // 4) % 2
    x_first, z_first = 2 * x + z, 2 * z + x
    chunk = core * 4 + x_first
    place = jnp.stack(
        [
            t,
            core * 4 + jnp.where(core == 0, x_first, z_first),
            jnp.where(core == 0, z_first, x_first),
            chunk,
        ]
    )
    count = float(lax.axis_size("dp") * (PROMPT + TOTAL))

    part_o = lax.dynamic_slice_in_dim(w_out, chunk * 48, 48, 0)
    part_i = lax.dynamic_slice_in_dim(w_in, chunk * 96, 96, 0)
    piece_a = jnp.concatenate(
        [
            part_i.astype(F32),
            jnp.concatenate([part_o[:24], part_o[24:]], axis=1).astype(F32),
            jnp.broadcast_to(b_in[None], (8, units)),
        ],
        axis=0,
    )
    piece_b = lax.dynamic_slice_in_dim(w_back, chunk * 192, 192, 0).astype(F32)
    own_a = swap(piece_a)
    own_b = swap(piece_b)
    q, k, v = project(tokens, w3, bias_qv)
    logits_p, probs_p, ctx_p, inv_p = prompt_forward(q, k, v, prev_prompt[0], after=(piece_b,))
    own_a, ctx_p = tie(own_a, ctx_p)
    oth_p = swap(ctx_p)
    zs_a, xs_a, far_own_a = hop(own_a, 2), hop(own_a, 1), hop(own_a, 0)
    logits_c, probs_c, ctx_a, inv_a = cont_forward(0, EARLY, lengths, q, k, v, prev_cont[0], after=(own_a,))
    zs_a, xs_a, far_own_a, own_b, ctx_a = tie(zs_a, xs_a, far_own_a, own_b, ctx_a)
    oth_a = swap(ctx_a)
    logits_c, probs_c, ctx_b, inv_b = cont_forward(
        EARLY, CONT - EARLY, lengths, q, k, v, prev_cont[0], (logits_c, probs_c)
    )
    zs_b, xs_b = hop(own_b, 2), hop(own_b, 1)
    cross_a = turn(jnp.where(core == 0, zs_a, xs_a), 0)
    cross_a, oth_p, zs_b, xs_b, ctx_b = tie(cross_a, oth_p, zs_b, xs_b, ctx_b)
    cross_b = turn(jnp.where(core == 0, zs_b, xs_b), 0)
    rest_a = jnp.concatenate([zs_a, xs_a, cross_a], axis=0)
    most_b = jnp.concatenate([own_b, zs_b, xs_b], axis=0)
    far_rest_a, far_most_b = hop(rest_a, 0), hop(most_b, 0)
    oth_a, cross_b, far_rest_a, far_most_b, ctx_b = tie(oth_a, cross_b, far_rest_a, far_most_b, ctx_b)
    oth_b = swap(ctx_b)
    far_cross_b = hop(cross_b, 0)

    fixed = (w_out, w_in, w_back, b_in[None], bias_out, norm_gain, norm_bias)
    pieces = (
        own_a, rest_a, far_own_a, far_rest_a, most_b, cross_b, far_most_b, far_cross_b,
    )
    n_blocks = SLOTS // ROWS
    lead = (PROMPT + EARLY * CONT_LEN) // ROWS
    first = rows_forward(
        0, lead, count, lengths, place, (ctx_p, ctx_a, oth_p, oth_a), tokens, teacher, fixed, pieces
    )
    kept, stats_a, (wo_oth, wi_oth, wb_oth, b_oth) = list(first[:7]), first[7], first[8:]
    oth_b, kept[0] = tie(oth_b, kept[0])
    *kept, stats_f = rows_forward(
        lead, n_blocks - lead, count, lengths, place, (ctx_b, oth_b), tokens, teacher, fixed,
        (wo_oth, wi_oth, wb_oth, b_oth), kept,
    )
    output, act, gate, gffn, gsec, xlow, rstd = kept
    stats_f = stats_f + stats_a

    def split(keep, got, n):
        return keep[n:] + got[n:], keep[:n] + got[:n]

    w_fixed = (w_out, w_in, wi_oth, w_back, wb_oth, norm_gain, norm_bias, stats_f)
    b_send = grad_back(1, place, act, gffn)
    b_got = hop(b_send, 0)
    b_keep = grad_back(0, place, act, gffn, after=(b_send,))
    b_got, b_keep = tie(b_got, b_keep)
    b_out, b_keep = split(b_keep, b_got, 2)
    b_got = turn(b_out, 0)
    ghid, gattn, gctx, gfin_half, stats = rows_backward(
        0, SLOTS // BACK_ROWS, place, gate, gffn, gsec, xlow, rstd, w_fixed, after=(b_out, b_keep)
    )
    b_got, ghid = tie(b_got, ghid)
    b_out, b_keep = split(b_keep, b_got, 1)
    b_got = turn(b_out, 1)
    other_stats = swap(stats)
    i_send, i_keep = grad_in(place, xlow, ghid, after=(b_out, b_keep))
    b_got, other_stats, i_send = tie(b_got, other_stats, i_send)
    b_top, b_end = b_keep[:, :96] + b_got[:, :96], b_keep[:, 96:] + b_got[:, 96:]
    b_got = hop(b_top, 3)
    i_got = hop(i_send, 0)
    gq, gk, gv, gkp, gvp = cont_backward(
        q, k, v, probs_c, gctx, ctx_a, inv_a, ctx_b, inv_b, after=(b_top, b_end)
    )
    i_got, b_got, gq = tie(i_got, b_got, gq)
    i_out, i_keep = split(i_keep, i_got, 2)
    i_got = turn(i_out, 0)
    b_more = hop(b_end, 3)
    gq, gk, gv = prompt_backward(
        q, k, v, probs_p, gctx, ctx_p, inv_p, gkp, gvp, gq, gk, gv, after=(i_out, i_keep)
    )
    r_send, r_keep = grad_rest(place, tokens, gq, gk, gv, ctx_p, ctx_a, ctx_b, gattn, stats, other_stats)
    i_got, b_more, r_send = tie(i_got, b_more, r_send)
    r_got = hop(r_send, 0)
    i_out, i_keep = split(i_keep, i_got, 1)
    i_got = turn(i_out, 1)
    b_total = far_exchange(jnp.concatenate([b_top + b_got, b_end + b_more], axis=1))
    b_got = turn(b_total, 1)
    r_got, i_got, b_got = tie(r_got, i_got, b_got)
    r_out, r_keep = split(r_keep, r_got, 2)
    r_got = turn(r_out, 0)
    i_top, i_end = i_keep[:, :48] + i_got[:, :48], i_keep[:, 48:] + i_got[:, 48:]
    i_got = hop(i_top, 3)
    b_two = jnp.concatenate([b_total, b_got], axis=0)
    *sends, keep = input_grad(place, gq, gk, gv, w3, gfin_half, after=(r_out, r_keep, i_top, i_end, b_two))
    r_got, i_got, keep = tie(r_got, i_got, keep)
    swapped = [swap(sends[0])]
    r_out, r_keep = split(r_keep, r_got, 1)
    r_got = turn(r_out, 1)
    i_more = hop(i_end, 3)
    r_got, i_more, swapped[0] = tie(r_got, i_more, swapped[0])
    swapped.append(swap(sends[1]))
    r_total = r_keep + r_got
    r_got = hop(r_total, 3)
    b_got = turn(b_two, 0)
    i_total = far_exchange(jnp.concatenate([i_top + i_got, i_end + i_more], axis=1))
    i_got = turn(i_total, 1)
    r_got, b_got, i_got, swapped[1] = tie(r_got, b_got, i_got, swapped[1])
    swapped.append(swap(sends[2]))
    r_total = far_exchange(r_total + r_got)
    r_got = turn(r_total, 1)
    i_two = jnp.concatenate([i_total, i_got], axis=0)
    i_got = turn(i_two, 0)
    b_near = jnp.concatenate([b_two, b_got], axis=0)
    b_far = hop(b_near, 0)
    r_got, i_got, b_far, b_near, swapped[2] = tie(r_got, i_got, b_far, b_near, swapped[2])
    swapped.append(swap(sends[3]))
    grad_w_back = in_order(1, place, b_far, in_order(0, place, b_near))
    r_two = jnp.concatenate([r_total, r_got], axis=0)
    r_got = turn(r_two, 0)
    r_far = hop(r_two, 0)
    i_near = jnp.concatenate([i_two, i_got], axis=0)
    i_far = hop(i_near, 0)
    grad_w_in = in_order(1, place, i_far, in_order(0, place, i_near, after=(r_two,)))
    rest = order_rest(1, 0, place, r_far, width, order_rest(0, 0, place, r_two, width))
    grad_w_in, swapped[3] = tie(grad_w_in, swapped[3])
    grad_tokens = keep + jnp.concatenate(swapped, axis=0)
    r_got, grad_tokens, grad_w_back, *rest = tie(r_got, grad_tokens, grad_w_back, *rest)
    r_far = hop(r_got, 0)
    rest = order_rest(0, 2, place, r_got, width, rest)
    grad_w3, grad_w_out, rows = order_rest(1, 2, place, r_far, width, rest)
    grad_bias, grad_gain, grad_shift, grad_b_in, grad_qv, loss = small_outputs(count, rows)
    return (
        output,
        logits_p[None],
        logits_c[None],
        grad_tokens,
        jnp.transpose(grad_w3, (1, 0, 2)),
        grad_qv,
        grad_w_out,
        grad_w_in,
        grad_b_in.reshape(units),
        grad_w_back,
        grad_bias,
        grad_gain,
        grad_shift,
        loss.reshape(()),
    )


def solution(mesh):
    in_specs = (
        P("dp", None),
        P("dp", None),
        P("dp", None),
        P("dp", "tensor", None, None),
        P("dp", None, "tensor", None, None),
        P(None, None, "tensor"),
        P(None, "tensor"),
        P("tensor", None),
        P(None, "tensor"),
        P("tensor"),
        P("tensor", None),
        P(),
        P(),
        P(),
    )
    out_specs = (
        P("dp", "tensor"),
        P("dp", "tensor", None, None),
        P("dp", None, "tensor", None, None),
        P("dp", "tensor"),
        P(None, None, "tensor"),
        P(None, "tensor"),
        P("tensor", None),
        P(None, "tensor"),
        P("tensor"),
        P("tensor", None),
        P(),
        P(),
        P(),
        P(),
    )
    return jax.shard_map(local, mesh=mesh, in_specs=in_specs, out_specs=out_specs, check_vma=False)
```
